512 devices in a mesh: mem: 8 (over y, core), space: 64 (over z, x).
Axes of the slice: x: 4, y: 4, z: 16, core: 2. Of those that a mesh axis runs over, the one named last changes fastest.
Arguments:
- ensemble: bfloat16 [64, 160, 128, 128], P('mem', None, 'space'), may hold values from -6 to 6
- obs_value: float32 [64, 256], P('space'), may hold values from -6 to 6
- obs_error: float32 [64, 256], P('space'), may hold values from 0.3 to 3
- obs_cell: int32 [64, 256], P('space'), may hold values from 0 to 255
- obs_species: int32 [64, 256], P('space'), may hold values from 0 to 39
- patch_index: int32 [64, 256, 32], P('space', 'mem'), may hold values from 0 to 767, as said below
- patch_count: int32 [64, 256], P('space', 'mem'), may hold values from 1 to 32, as said below
- courant_x: float32 [4, 128, 128], P(None, 'space'), may hold values from -0.7 to 0.7
- courant_y: float32 [4, 128, 128], P(None, 'space'), may hold values from -0.7 to 0.7
- dep_velocity: float32 [40], replicated, may hold values from 0.05 to 0.5
- surface_factor: float32 [128, 128], P('space'), may hold values from 0.5 to 2
Outputs:
- forecast: bfloat16 [64, 160, 128, 128], P('mem', None, 'space')
The draws below stay inside these ranges and needn't reach their ends.
Inputs may be any that keep to these rules, and one draw needn't show every extreme that they name: `patch_index`: each cell's list names distinct pool observations of existing tiles, nearest to the cell first; those within 3 cells of the cell come first. `patch_count`: the number of listed observations used for the cell, at least 1 and at most 32; the most is reached in every draw.
All inputs are finite; a program needn't handle non-finite values.
Results may differ from the reference program's by a relative error of at most 0.0049.
Values may be sent and summed in bfloat16 or wider, within the bound.
No kernel may reach another device: no remote copies, remote signals or barrier semaphores. Data moves between devices by JAX's collectives and lax.ppermute only.
A program may use at most 64 MiB of HBM per device.

```python
import math
import jax
import jax.numpy as jnp
from jax import lax

MEMBERS = 64
SPECIES = 40
LEVELS = 4
NX = 128
ROWS = 2
OBS_TILE = 256
MAXOBS = 32
NEWTON = 8
SUBSTEPS = 2
TILES = 64
NY = 128
FIELDS = 160
LOC = 1


def shared_cells(key):
    return jax.random.randint(jax.random.fold_in(key, 7177), (TILES, OBS_TILE), 0, ROWS * NX, dtype=jnp.int32)


def nearest_lists(key):
    cells = shared_cells(key)
    padded = jnp.pad(cells, ((1, 1), (0, 0)))
    tile_ids = jnp.arange(TILES, dtype=jnp.int32)
    reach = 3 * LOC

    def one_tile(tile_num):
        pool_cells = lax.dynamic_slice_in_dim(padded, tile_num, 3, 0)
        offsets = (jnp.arange(3, dtype=jnp.int32) - 1) * ROWS
        pool_row = (pool_cells // NX + offsets[:, None]).reshape(-1)
        pool_col = (pool_cells % NX).reshape(-1)
        source_tile = tile_num - 1 + jnp.arange(3, dtype=jnp.int32)
        exists = (source_tile >= 0) & (source_tile < TILES)
        exists = jnp.broadcast_to(exists[:, None], (3, OBS_TILE)).reshape(-1)
        cell_ids = jnp.arange(ROWS * NX, dtype=jnp.int32)
        cell_row = cell_ids // NX
        cell_col = cell_ids % NX
        dist_sq = (pool_row[None, :] - cell_row[:, None]) ** 2 + (pool_col[None, :] - cell_col[:, None]) ** 2
        dist_sq = jnp.where(exists[None, :], dist_sq, 40000)
        score = dist_sq * 2048 + jnp.arange(3 * OBS_TILE, dtype=jnp.int32)[None, :]
        neg_top, chosen = lax.top_k(-score, MAXOBS)
        near = jnp.sum(((dist_sq <= reach * reach) & exists[None, :]).astype(jnp.int32), axis=1)
        return (chosen.astype(jnp.int32), jnp.clip(near, 1, MAXOBS).astype(jnp.int32))
    chosen, counts = lax.map(one_tile, tile_ids)
    counts = counts.at[0, 0].set(MAXOBS)
    return (chosen, counts)


def draw_obs_cell(key, part):
    return shared_cells(key)


def draw_patch_index(key, part):
    return nearest_lists(key)[0]


def draw_patch_count(key, part):
    return nearest_lists(key)[1]


def touch_ends(array, stream_key, smallest, largest):
    longest = array.shape.index(max(array.shape))
    spots = []
    for shift in (0, 1):
        where = [jax.random.randint(jax.random.fold_in(stream_key, axis), (), 0, length) for axis, length in enumerate(array.shape)]
        where[longest] = (where[longest] + shift) % array.shape[longest]
        spots.append(tuple(where))
    return array.at[spots[0]].set(smallest).at[spots[1]].set(largest)


def block_levels(stream_key, dims, split, least, largest):
    def one(axis_at, parts):
        draws = jax.random.uniform(jax.random.fold_in(jax.random.fold_in(stream_key, 6), axis_at), (parts,), jnp.float32, least / len(split), largest / len(split))
        return jnp.repeat(jnp.exp(draws), dims[axis_at] // parts).reshape((-1,) + (1,) * (len(dims) - axis_at - 1))

    level = one(*split[0])
    for cut in split[1:]:
        level = level * one(*cut)
    return level


def noise(stream_key, extent, spread, most, pieces=(), kind=jnp.bfloat16):
    array = jax.random.normal(stream_key, extent, jnp.float32) * spread
    if len(pieces) > 0:
        array = block_levels(stream_key, extent, pieces, -0.22, 0.18) * array
    return jnp.clip(array, min=-most, max=most).astype(kind)


def setup_inputs(seed: int = 0) -> dict:
    splits = jax.random.split(jax.random.key(seed), 12)
    return {
        "ensemble": noise(splits[0], (MEMBERS, FIELDS, NY, NX), 1.0, 6.0, ((0, 8), (2, 64))),
        "obs_value": noise(splits[1], (TILES, OBS_TILE), 1.0, 6.0, ((0, 64),), jnp.float32),
        "obs_error": jnp.clip(jnp.exp(math.log(3.0) - 2.3025851 * jax.random.uniform(splits[2], (TILES, OBS_TILE), jnp.float32) ** block_levels(splits[2], (TILES, OBS_TILE), ((0, 64),), -0.2, 0.2)), 0.3, 3.0),
        "obs_cell": draw_obs_cell(jax.random.fold_in(splits[11], 71), 0),
        "obs_species": touch_ends(jax.random.randint(splits[4], (TILES, OBS_TILE), 0, SPECIES), jax.random.fold_in(splits[4], 1), 0, SPECIES - 1).astype(jnp.int32),
        "patch_index": draw_patch_index(jax.random.fold_in(splits[11], 71), 0),
        "patch_count": draw_patch_count(jax.random.fold_in(splits[11], 71), 0),
        "courant_x": jnp.clip(jax.random.uniform(splits[7], (LEVELS, NY, NX), jnp.float32, -0.7, 0.7) * block_levels(splits[7], (LEVELS, NY, NX), ((1, 64),), -0.4, 0.0), -0.7, 0.7),
        "courant_y": jnp.clip(jax.random.uniform(splits[8], (LEVELS, NY, NX), jnp.float32, -0.7, 0.7) * block_levels(splits[8], (LEVELS, NY, NX), ((1, 64),), -0.4, 0.0), -0.7, 0.7),
        "dep_velocity": jnp.clip(jnp.exp(jax.random.uniform(splits[9], (SPECIES,), jnp.float32, math.log(0.05), math.log(0.5))), 0.05, 0.5),
        "surface_factor": jnp.clip(0.5 + 1.5 * jax.random.uniform(splits[10], (NY, NX), jnp.float32) ** block_levels(splits[10], (NY, NX), ((0, 64),), -0.2, 0.2), 0.5, 2.0),
    }


def inverse_root(matrix, trace_val, repeats):
    matrix_order = matrix.shape[-1]
    identity = jnp.eye(matrix_order, dtype=jnp.float32)
    iterate = matrix / trace_val[:, None, None]
    inv_root = jnp.broadcast_to(identity, matrix.shape)
    for repeat in range(repeats):
        middle = 1.5 * identity - 0.5 * jnp.einsum('cij,cjk->cik', inv_root, iterate, precision=lax.Precision.HIGHEST)
        iterate = jnp.einsum('cij,cjk->cik', iterate, middle, precision=lax.Precision.HIGHEST)
        inv_root = jnp.einsum('cij,cjk->cik', middle, inv_root, precision=lax.Precision.HIGHEST)
    return inv_root

def prepare_pool(obs_pool, members, row_offsets):
    pooled = jnp.transpose(obs_pool[:, :members], (1, 0, 2)).reshape(members, -1)
    extra = obs_pool[:, members:]
    obs_mean = lax.optimization_barrier(jnp.mean(pooled, axis=0))
    obs_dev = jnp.transpose(pooled - obs_mean[None, :])
    values = extra[:, 0].reshape(-1)
    errors = extra[:, 1].reshape(-1)
    obs_row = (extra[:, 2] + row_offsets[:, None]).reshape(-1)
    obs_col = extra[:, 3].reshape(-1)
    return (obs_dev, obs_mean, values, errors, obs_row, obs_col)

def analyse(block_state, prepared, indices, counts, cell_ids, columns, radius, repeats):
    obs_dev, obs_mean, values, errors, obs_row, obs_col = prepared
    members = obs_dev.shape[1]
    picked = obs_dev[indices]
    cell_row = (cell_ids // columns).astype(jnp.float32)
    cell_col = (cell_ids % columns).astype(jnp.float32)
    distance_sq = (obs_row[indices] - cell_row[:, None]) ** 2 + (obs_col[indices] - cell_col[:, None]) ** 2
    active = jnp.arange(indices.shape[1], dtype=jnp.int32)[None, :] < counts[:, None]
    obs_weight = jnp.where(active, jnp.exp(-distance_sq / (2.0 * radius * radius)) / errors[indices], 0.0)
    innovation = values[indices] - obs_mean[indices]
    identity = jnp.eye(members, dtype=jnp.float32)
    gram_mat = jnp.einsum('cok,col->ckl', picked * obs_weight[:, :, None], picked, precision=lax.Precision.HIGHEST) + (members - 1.0) * identity
    trace_val = jnp.einsum('ckk->c', gram_mat)
    inv_root = inverse_root(gram_mat, trace_val, repeats)
    gain_vec = jnp.einsum('cok,co->ck', picked, obs_weight * innovation, precision=lax.Precision.HIGHEST)
    analysis_cov = jnp.einsum('ckl,clm->ckm', inv_root, inv_root, precision=lax.Precision.HIGHEST) / trace_val[:, None, None]
    mean_w = jnp.einsum('ckl,cl->ck', analysis_cov, gain_vec, precision=lax.Precision.HIGHEST)
    weights = math.sqrt(members - 1.0) * inv_root / jnp.sqrt(trace_val)[:, None, None] + mean_w[:, :, None]
    state_mean = lax.optimization_barrier(jnp.mean(block_state, axis=0))
    state_dev = block_state - state_mean[None]
    result = state_mean[None] + jnp.einsum('ifc,cij->jfc', state_dev, weights, precision=lax.Precision.HIGHEST)
    return result.astype(jnp.bfloat16)

def rows_step(extended, courant):
    middle = extended[..., 1:-1, :]
    north_row = extended[..., 2:, :]
    south_row = extended[..., :-2, :]
    return middle - 0.5 * courant * (north_row - south_row) + 0.5 * courant * courant * (north_row - 2.0 * middle + south_row)

def cols_step(field_now, courant):
    padded = jnp.pad(field_now, [(0, 0)] * (field_now.ndim - 1) + [(1, 1)])
    middle = padded[..., 1:-1]
    east_col = padded[..., 2:]
    west_col = padded[..., :-2]
    return middle - 0.5 * courant * (east_col - west_col) + 0.5 * courant * courant * (east_col - 2.0 * middle + west_col)

def deposit(field_now, dep_velocity, surface_factor):
    loss = jnp.exp(-dep_velocity[:, None, None] * surface_factor[None])
    lowest = (jnp.arange(field_now.shape[2], dtype=jnp.int32) == 0)[:, None, None]
    factor = jnp.where(lowest[None], loss[:, None], 1.0)
    return field_now * factor[None]

def reference(ensemble, obs_value, obs_error, obs_cell, obs_species, patch_index, patch_count, courant_x, courant_y, dep_velocity, surface_factor):
    tile_cells = ROWS * NX
    by_tile = jnp.transpose(ensemble.reshape(MEMBERS, FIELDS, TILES, tile_cells), (2, 0, 1, 3))
    flat_state = by_tile.reshape(TILES, MEMBERS, FIELDS * tile_cells)
    position = obs_species * (LEVELS * tile_cells) + obs_cell
    position = jnp.broadcast_to(position[:, None, :], (TILES, MEMBERS, OBS_TILE))
    equivalents = jnp.take_along_axis(flat_state, position, axis=2).astype(jnp.float32)
    obs_info = jnp.stack([obs_value, obs_error, (obs_cell // NX).astype(jnp.float32), (obs_cell % NX).astype(jnp.float32)], axis=1)
    packed = jnp.concatenate([equivalents, obs_info], axis=1)
    padded = jnp.pad(packed, ((1, 1), (0, 0), (0, 0)))
    row_offsets = (jnp.arange(3, dtype=jnp.float32) - 1.0) * ROWS

    def one_tile(tile_num):
        obs_pool = lax.dynamic_slice_in_dim(padded, tile_num, 3, 0)
        prepared = prepare_pool(obs_pool, MEMBERS, row_offsets)
        block_state = by_tile[tile_num].astype(jnp.float32)
        cell_ids = jnp.arange(tile_cells, dtype=jnp.int32)
        return analyse(block_state, prepared, patch_index[tile_num], patch_count[tile_num], cell_ids, NX, LOC, NEWTON)
    analysed = lax.map(one_tile, jnp.arange(TILES, dtype=jnp.int32))
    analysed = jnp.transpose(analysed, (1, 2, 0, 3)).reshape(MEMBERS, SPECIES, LEVELS, NY, NX)
    field_now = analysed.astype(jnp.float32)
    for repeat in range(SUBSTEPS):
        padded_rows = jnp.pad(field_now, ((0, 0), (0, 0), (0, 0), (1, 1), (0, 0)))
        field_now = rows_step(padded_rows, courant_y)
        field_now = cols_step(field_now, courant_x)
    field_now = deposit(field_now, dep_velocity, surface_factor)
    return field_now.reshape(MEMBERS, FIELDS, NY, NX).astype(jnp.bfloat16)
```

```python
import functools
import math

import jax
import jax.numpy as jnp
from jax import lax
from jax.experimental import pallas as pl
from jax.experimental.pallas import tpu as pltpu
from jax.sharding import PartitionSpec as P

NEWTON = 8
SUBSTEPS = 2
LOC = 1
F32 = jnp.float32
BF16 = jnp.bfloat16
VMEM = pl.BlockSpec(memory_space=pltpu.VMEM)


def iota(shape, dim):
    return lax.broadcasted_iota(jnp.int32, shape, dim)


def split2(x):
    hi = x.astype(BF16)
    return hi, (x - hi.astype(F32)).astype(BF16)


def split3(x):
    hi = x.astype(BF16).astype(F32)
    mid = (x - hi).astype(BF16).astype(F32)
    return hi, mid, x - hi - mid


def mm(a, b):
    return jnp.dot(a, b, preferred_element_type=F32)


def mm_nt(a, b):
    return lax.dot_general(a, b, (((1,), (1,)), ((), ())), preferred_element_type=F32)


def block_rows(x, width):
    lane = iota(x.shape, 1) // width
    zero = jnp.zeros_like(x)
    return jnp.concatenate([jnp.where(lane == b, x, zero) for b in range(4)], axis=0)


def product(a2, b2, dot=mm):
    rows = a2[0].shape[0]
    first = dot(jnp.concatenate(a2, axis=0), b2[0])
    return first[:rows] + first[rows:] + dot(a2[0], b2[1])


def blocks2(x, width=64):
    hi, lo = split2(x)
    return block_rows(hi, width), block_rows(lo, width)


def weights_kernel(left, own, right, idx_ref, pos_ref, hi_ref, lo_ref, p_ref, z_ref, q_ref, tr_ref):
    members, maxobs, cells_g = 64, 32, 4
    groups = hi_ref.shape[0]
    parts = [left[...], own[...], right[...]]
    equiv = jnp.concatenate([p[:members] for p in parts], axis=1)
    info = jnp.concatenate([p[members : members + 8] for p in parts], axis=1)
    n_obs = info.shape[1]
    tile = n_obs // 3
    row_obs = info[2:3] + ((iota((1, n_obs), 1) // tile).astype(F32) - 1.0) * 2.0
    sub = iota((8, n_obs), 0)
    rows = [*split3(info[0:1]), *split3(info[1:2]), row_obs, info[3:4]]
    table = jnp.zeros((8, n_obs), F32)
    for r, line in enumerate(rows):
        table = jnp.where(sub == r, line, table)
    lhs = jnp.concatenate([equiv, table, jnp.zeros((8, n_obs), F32)], axis=0).astype(BF16)

    eye = (iota((members, 256), 0) == iota((members, 256), 1) % 64).astype(F32)
    spread = (iota((128, 256), 0) // maxobs == iota((128, 256), 1) // 64).astype(BF16)
    for half in range(groups // 2):
        sl = slice(half * 256, half * 256 + 256)
        idx = idx_ref[:, sl]
        onehot = (iota((n_obs, 256), 0) == idx).astype(F32).astype(BF16)
        got = mm(lhs, onehot)
        raw = got[:members]
        mean = jnp.sum(raw, axis=0, keepdims=True) * (1.0 / members)
        dev = raw - mean
        value = got[64:65] + got[65:66] + got[66:67]
        error = got[67:68] + got[68:69] + got[69:70]
        active = idx >= 0
        d2 = (got[70:71] - pos_ref[0:1, sl]) ** 2 + (got[71:72] - pos_ref[1:2, sl]) ** 2
        rho = jnp.where(
            active, jnp.exp(-d2 / (2.0 * LOC * LOC)) / jnp.where(active, error, 1.0), 0.0
        )
        scaled = dev * rho
        pull = rho * (value - mean)
        power = jnp.sum(dev * scaled, axis=0, keepdims=True)
        for part in range(2):
            g = half * 2 + part
            gs = slice(part * 128, part * 128 + 128)
            dev_g = dev[:, gs]
            lhs_g = jnp.concatenate(
                [scaled[:, gs], jnp.broadcast_to(pull[:, gs], (16, 128))], axis=0
            )
            both = product(split2(lhs_g), blocks2(dev_g, maxobs), mm_nt)
            sub16 = iota((16, 128), 0)
            p_hi, p_mid, p_lo = split3(power[:, gs])
            power3 = jnp.where(
                sub16 == 0, p_hi, jnp.where(sub16 == 1, p_mid, jnp.where(sub16 == 2, p_lo, 0.0))
            )
            trace = (members - 1.0) * members + jnp.sum(
                mm(power3.astype(BF16), spread), axis=0, keepdims=True
            )
            pmat = (both[:members] + (members - 1.0) * eye) / trace
            middle = 1.5 * eye - 0.5 * pmat
            p_ref[g] = product(split2(pmat), blocks2(middle))
            z_ref[g] = middle
            q_ref[g] = both[members : members + 8]
            tr_ref[g] = jnp.broadcast_to(trace, (8, 256))

    def step(_, carry):
        for g in range(groups):
            pmat, zmat = p_ref[g], z_ref[g]
            zs = split2(zmat)
            ps = split2(pmat)
            middle = 1.5 * eye - 0.5 * product(zs, tuple(block_rows(x, 64) for x in ps))
            ms = split2(middle)
            p_ref[g] = product(ps, tuple(block_rows(x, 64) for x in ms))
            z_ref[g] = product(ms, tuple(block_rows(x, 64) for x in zs))
        return carry

    lax.fori_loop(0, NEWTON - 2, step, 0)
    for g in range(groups):
        pmat, zmat = p_ref[g], z_ref[g]
        middle = 1.5 * eye - 0.5 * product(split2(zmat), blocks2(pmat))
        root = product(split2(middle), blocks2(zmat))
        trace = tr_ref[g][:1]
        blocks = blocks2(root)
        q16 = jnp.concatenate([q_ref[g], q_ref[g]], axis=0)
        pulled = product(split2(product(split2(q16), blocks)), blocks)[:1] / trace
        scale = math.sqrt(members - 1.0) / jnp.sqrt(trace)
        p0 = (members - 1.0) / trace
        z0 = jnp.ones_like(p0)
        for _ in range(NEWTON):
            m0 = 1.5 - 0.5 * z0 * p0
            p0 = p0 * m0
            z0 = m0 * z0
        full = scale * root + (pulled + (1.0 - scale * z0) * (1.0 / members))
        hi, lo = split2(full)
        hi_ref[g] = hi
        lo_ref[g] = lo


def transform_kernel(hi_ref, lo_ref, x_ref, *refs):
    outs, scr = refs[:-1], refs[-1]
    groups = hi_ref.shape[0]
    per = 32
    for g in range(groups):
        lhs = jnp.concatenate([block_rows(hi_ref[g], 64), block_rows(lo_ref[g], 64)], axis=0)
        x = jnp.concatenate(
            [x_ref[:, g * 4 + c].astype(F32).reshape(64, 256) for c in range(4)], axis=0
        ).astype(BF16)
        out = mm(lhs, x)
        for c in range(4):
            scr_val = out[c * 64 : c * 64 + 64] + out[256 + c * 64 : 256 + c * 64 + 64]
            scr[0, pl.ds(g * 4 + c, 64, stride=per), :] = scr_val[:, :128]
            scr[1, pl.ds(g * 4 + c, 64, stride=per), :] = scr_val[:, 128:]
    lane = iota((8, 128), 1) // 32
    chunk = 8 // len(outs)
    for dest in range(8):
        for ml in range(8):
            base = (dest * 8 + ml) * per
            main = scr[0, base : base + per, :]
            rest = jnp.zeros((8, 128), F32)
            for cc in range(4):
                piece = scr[1, base + cc * 8 : base + cc * 8 + 8, :]
                piece = pltpu.roll(piece, 32 * cc, 1) if cc else piece
                rest = jnp.where(lane == cc, piece, rest)
            outs[ml // chunk][dest, ml % chunk] = jnp.concatenate([main, rest, jnp.zeros_like(rest)], axis=0)[:48].astype(BF16)[:40]


def relayout_kernel(x_ref, o_ref):
    fields = o_ref.shape[2]
    ident = (iota((fields, 256), 0) == iota((fields, 256), 1)).astype(F32).astype(BF16)
    for row in range(2):
        for ml in range(x_ref.shape[1]):
            mains, rests = [], []
            for q in range(4):
                block = x_ref[row * 4 + q, ml].astype(F32)
                mains.append(block[:32])
                tail = block[32:40]
                for cc in range(4):
                    rests.append(pltpu.roll(tail, 128 - 32 * cc, 1) if cc else tail)
            full = jnp.concatenate(
                [jnp.concatenate(mains, axis=0), jnp.concatenate(rests, axis=0)], axis=1
            ).astype(BF16)
            o_ref[row, ml] = mm_nt(ident, full).astype(BF16)


def advect_kernel(low_ref, own_ref, high_ref, cl_ref, co_ref, ch_ref, dep_ref, surf_ref, o_ref, fac):
    members, fields = own_ref.shape[1], own_ref.shape[2]
    lane = iota((8, 128), 1)

    def coeffs(c):
        half, sq = 0.5 * c, 0.5 * c * c
        return half + sq, 1.0 - c * c, sq - half

    courant = [(cl_ref, 1), (co_ref, 0), (co_ref, 1), (ch_ref, 0)]
    cy = [coeffs(r[1, k]) for r, k in courant]
    cx = []
    for r, k in courant:
        a, b, c = coeffs(r[0, k])
        cx.append((jnp.where(lane == 0, 0.0, a), b, jnp.where(lane == 127, 0.0, c)))
    for row in range(2):
        fac[row] = jnp.exp(-dep_ref[...] * surf_ref[row : row + 1, :])

    def rows(south, mid, north, k):
        a, b, c = cy[k]
        return a * south + b * mid + c * north

    def cols(q, k):
        a, b, c = cx[k]
        return a * pltpu.roll(q, 1, 1) + b * q + c * pltpu.roll(q, 127, 1)

    def member(m, carry):
        for f in range(0, fields, 16):
            pieces = [[], []]
            loads = [
                r[k, m, f : f + 16].astype(F32)
                for r, k in [
                    (low_ref, 0), (low_ref, 1), (own_ref, 0),
                    (own_ref, 1), (high_ref, 0), (high_ref, 1),
                ]
            ]
            for h in (0, 8):
                q = [x[h : h + 8] for x in loads]
                q1 = [cols(rows(q[i], q[i + 1], q[i + 2], i), i) for i in range(4)]
                for r in range(2):
                    q2 = cols(rows(q1[r], q1[r + 1], q1[r + 2], r + 1), r + 1)
                    pieces[r].append(q2 * fac[r, f + h : f + h + 8])
            for r in range(2):
                o_ref[r, m, f : f + 16] = jnp.concatenate(pieces[r], axis=0).astype(BF16)
        return carry

    lax.fori_loop(0, members, member, 0)


def call(kernel, outs, scratch=(), flops=10**8, nbytes=10**6):
    return pl.pallas_call(
        kernel,
        out_shape=outs,
        scratch_shapes=list(scratch),
        compiler_params=pltpu.CompilerParams(vmem_limit_bytes=40 << 20),
        cost_estimate=pl.CostEstimate(flops=flops, bytes_accessed=nbytes, transcendentals=0),
    )


def from_low(x):
    count = lax.axis_size("space")
    return lax.ppermute(x, "space", [(i, i + 1) for i in range(count - 1)])


def from_high(x):
    count = lax.axis_size("space")
    return lax.ppermute(x, "space", [(i + 1, i) for i in range(count - 1)])


def shards(
    ensemble,
    obs_value,
    obs_error,
    obs_cell,
    obs_species,
    patch_index,
    patch_count,
    courant_x,
    courant_y,
    dep_velocity,
    surface_factor,
):
    local, fields, tile_rows, columns = ensemble.shape
    species = dep_velocity.shape[0]
    levels = fields // species
    n_obs = obs_cell.shape[1]
    per = patch_index.shape[1]
    maxobs = patch_index.shape[2]
    groups_mem = 8

    surface = ensemble.reshape(local, species, levels, tile_rows, columns)[:, :, 0]
    cell = obs_cell[0]
    pick = (
        jnp.arange(tile_rows * columns, dtype=jnp.int32)[:, None] == cell[None, :]
    ).astype(BF16)
    at_cell = jnp.dot(
        surface.reshape(local * species, tile_rows * columns), pick, preferred_element_type=F32
    ).reshape(local, species, n_obs)
    chosen = jnp.arange(species, dtype=jnp.int32)[:, None] == obs_species
    equiv = jnp.sum(jnp.where(chosen[None], at_cell, 0.0), axis=1)
    everywhere = lax.all_to_all(
        jnp.broadcast_to(equiv[None], (groups_mem, local, n_obs)), "mem", 0, 0, tiled=True
    ).reshape(groups_mem * local, n_obs)

    wind = jnp.stack([courant_x, courant_y])
    packed = jnp.concatenate(
        [
            everywhere,
            obs_value,
            obs_error,
            (obs_cell // columns).astype(F32),
            (obs_cell % columns).astype(F32),
            jnp.zeros((4, n_obs), F32),
            wind.reshape(8, 256),
        ],
        axis=0,
    )
    low, high = from_low(packed), from_high(packed)

    payload = ensemble.reshape(local, fields, tile_rows, 4, per)
    payload = jnp.pad(payload, ((0, 0), (0, 256 - fields), (0, 0), (0, 0), (0, 0)))
    payload = jnp.transpose(payload, (2, 3, 4, 0, 1)).reshape(groups_mem, per, local, 256)
    state = lax.all_to_all(payload, "mem", 0, 0, tiled=True)

    used = jnp.arange(maxobs, dtype=jnp.int32)[None, :] < patch_count[0][:, None]
    idx = jnp.where(used, patch_index[0], -1).reshape(1, per * maxobs)
    cell_id = lax.axis_index("mem") * per + jnp.arange(per, dtype=jnp.int32)
    cell_id = jnp.broadcast_to(cell_id[:, None], (per, maxobs)).reshape(1, per * maxobs)
    pos = jnp.concatenate([cell_id // columns, cell_id % columns], axis=0).astype(F32)

    groups = per // 4
    hi, lo = call(
        weights_kernel,
        [jax.ShapeDtypeStruct((groups, 64, 256), BF16)] * 2,
        [
            pltpu.VMEM((groups, 64, 256), F32),
            pltpu.VMEM((groups, 64, 256), F32),
            pltpu.VMEM((groups, 8, 256), F32),
            pltpu.VMEM((groups, 8, 256), F32),
        ],
        flops=10**10,
    )(low[:72], packed[:72], high[:72], idx, pos)
    back = call(
        transform_kernel,
        [jax.ShapeDtypeStruct((groups_mem, local, 40, 128), BF16)],
        [pltpu.VMEM((2, 64 * per, 128), F32)],
        flops=10**9,
    )(hi, lo, state)[0]
    returned = lax.all_to_all(back, "mem", 0, 0, tiled=True)
    planes = call(
        relayout_kernel,
        jax.ShapeDtypeStruct((tile_rows, local, fields, columns), BF16),
        flops=10**9,
    )(returned)
    below, above = from_low(planes), from_high(planes)

    def rims(array):
        wind_now = array[72:80].reshape(2, levels, tile_rows, columns)
        wind_now = jnp.transpose(wind_now, (0, 2, 1, 3))
        return jnp.concatenate([wind_now, wind_now], axis=2)

    rate = jnp.where(
        (jnp.arange(fields, dtype=jnp.int32) % levels == 0)[:, None],
        jnp.repeat(dep_velocity, levels)[:, None],
        0.0,
    )
    done = call(
        advect_kernel,
        jax.ShapeDtypeStruct((tile_rows, local, fields, columns), BF16),
        [pltpu.VMEM((tile_rows, fields, columns), F32)],
        flops=10**8,
    )(below, planes, above, rims(low), rims(packed), rims(high), rate, surface_factor)
    return jnp.transpose(done, (1, 2, 0, 3))


def solution(mesh):
    in_specs = (
        P("mem", None, "space", None),
        P("space", None),
        P("space", None),
        P("space", None),
        P("space", None),
        P("space", "mem", None),
        P("space", "mem"),
        P(None, "space", None),
        P(None, "space", None),
        P(),
        P("space", None),
    )
    out_specs = P("mem", None, "space", None)
    return jax.shard_map(shards, mesh=mesh, in_specs=in_specs, out_specs=out_specs, check_vma=False)
```

```python
import functools
import math

import jax
import jax.numpy as jnp
from jax import lax
from jax.experimental import pallas as pl
from jax.experimental.pallas import tpu as pltpu
from jax.sharding import PartitionSpec as P

NEWTON = 8
SUBSTEPS = 2
LOC = 1
F32 = jnp.float32
BF16 = jnp.bfloat16
VMEM = pl.BlockSpec(memory_space=pltpu.VMEM)


def iota(shape, dim):
    return lax.broadcasted_iota(jnp.int32, shape, dim)


def split2(x):
    hi = x.astype(BF16)
    return hi, (x - hi.astype(F32)).astype(BF16)


def split3(x):
    hi = x.astype(BF16).astype(F32)
    mid = (x - hi).astype(BF16).astype(F32)
    return hi, mid, x - hi - mid


def mm(a, b):
    return jnp.dot(a, b, preferred_element_type=F32)


def mm_nt(a, b):
    return lax.dot_general(a, b, (((1,), (1,)), ((), ())), preferred_element_type=F32)


def block_rows(x, width):
    lane = iota(x.shape, 1) // width
    zero = jnp.zeros_like(x)
    return jnp.concatenate(
        [jnp.where(lane == b, x, zero) for b in range(x.shape[1] // width)], axis=0
    )


def product(a2, b2, dot=mm):
    rows = a2[0].shape[0]
    first = dot(jnp.concatenate(a2, axis=0), b2[0])
    return first[:rows] + first[rows:] + dot(a2[0], b2[1])


def blocks2(x, width):
    hi, lo = split2(x)
    return block_rows(hi, width), block_rows(lo, width)


def side_by_side(x):
    return jnp.concatenate(split2(x), axis=1)


def paired(x, masks):
    cols = [jnp.concatenate([part * masks[0], part * masks[1]], axis=0) for part in split2(x)]
    once = jnp.concatenate(cols, axis=1)
    return jnp.concatenate([once, once], axis=0)


def pair_product(a, b):
    out = mm(a, b)
    return out[:, :128] + out[:, 128:]


def weights_kernel(left, own, right, idx_ref, pos_ref, hi_ref, lo_ref, t_ref, z_ref, m_ref, q_ref, tr_ref):
    members, maxobs = 64, 32
    pairs = t_ref.shape[0]
    parts = [left[...], own[...], right[...]]
    equiv = jnp.concatenate([p[:members] for p in parts], axis=1)
    info = jnp.concatenate([p[members : members + 8] for p in parts], axis=1)
    n_obs = info.shape[1]
    tile = n_obs // 3
    row_obs = info[2:3] + ((iota((1, n_obs), 1) // tile).astype(F32) - 1.0) * 2.0
    sub = iota((8, n_obs), 0)
    rows = [*split3(info[0:1]), *split3(info[1:2]), row_obs, info[3:4]]
    table = jnp.zeros((8, n_obs), F32)
    for r, line in enumerate(rows):
        table = jnp.where(sub == r, line, table)
    lhs = jnp.concatenate([equiv, table, jnp.zeros((8, n_obs), F32)], axis=0).astype(BF16)

    eye = (iota((members, 128), 0) == iota((members, 128), 1) % 64).astype(F32)
    eye2 = jnp.concatenate([eye, eye], axis=1)
    spread = (iota((128, 256), 0) // maxobs == iota((128, 256), 1) // 64).astype(BF16)
    lane = iota((members, 128), 1)
    masks = [(lane < 64).astype(F32).astype(BF16), (lane >= 64).astype(F32).astype(BF16)]
    quarters = range(pairs // 4)
    sls = [slice(n * 256, n * 256 + 256) for n in quarters]
    gots = []
    for sl in sls:
        onehot = (iota((n_obs, 256), 0) == idx_ref[:, sl]).astype(F32).astype(BF16)
        gots.append(mm(lhs, onehot))
    grams = []
    for sl, got in zip(sls, gots):
        raw = got[:members]
        mean = jnp.sum(raw, axis=0, keepdims=True) * (1.0 / members)
        dev = raw - mean
        value = got[64:65] + got[65:66] + got[66:67]
        error = got[67:68] + got[68:69] + got[69:70]
        active = idx_ref[:, sl] >= 0
        d2 = (got[70:71] - pos_ref[0:1, sl]) ** 2 + (got[71:72] - pos_ref[1:2, sl]) ** 2
        rho = jnp.where(
            active, jnp.exp(-d2 / (2.0 * LOC * LOC)) / jnp.where(active, error, 1.0), 0.0
        )
        scaled = dev * rho
        pull = rho * (value - mean)
        power = jnp.sum(dev * scaled, axis=0, keepdims=True)
        for part in range(2):
            gs = slice(part * 128, part * 128 + 128)
            lhs_g = jnp.concatenate(
                [scaled[:, gs], jnp.broadcast_to(pull[:, gs], (16, 128))], axis=0
            )
            both = product(split2(lhs_g), blocks2(dev[:, gs], maxobs), mm_nt)
            sub16 = iota((16, 128), 0)
            p_hi, p_mid, p_lo = split3(power[:, gs])
            power3 = jnp.where(
                sub16 == 0, p_hi, jnp.where(sub16 == 1, p_mid, jnp.where(sub16 == 2, p_lo, 0.0))
            )
            grams.append((both, mm(power3.astype(BF16), spread)))
    for g, (both, powers) in enumerate(grams):
        trace = (members - 1.0) * members + jnp.sum(powers, axis=0, keepdims=True)
        pmat = (both[:members] + (members - 1.0) * eye2) * (1.0 / trace)
        for k in range(2):
            ks = slice(k * 128, k * 128 + 128)
            p = g * 2 + k
            t_ref[p] = pmat[:, ks]
            q_ref[p] = both[members : members + 16, ks]
            tr_ref[p] = jnp.broadcast_to(trace[:, ks], (8, 128))
    for p in range(pairs):
        middle = 1.5 * eye - 0.5 * t_ref[p]
        rows_m = jnp.concatenate([middle, q_ref[p]], axis=0)
        out = pair_product(side_by_side(rows_m), paired(middle, masks))
        z_ref[p] = middle
        q_ref[p] = out[members:]
        m_ref[p] = out[:members]
    for p in range(pairs):
        t_ref[p] = pair_product(side_by_side(t_ref[p]), paired(m_ref[p], masks))

    def step(_, carry):
        for p in range(pairs):
            middle = 1.5 * eye - 0.5 * t_ref[p]
            rows_m = jnp.concatenate([middle, z_ref[p], q_ref[p]], axis=0)
            out = pair_product(side_by_side(rows_m), paired(middle, masks))
            m_ref[p] = out[:members]
            z_ref[p] = out[members : 2 * members]
            q_ref[p] = out[2 * members :]
        for p in range(pairs):
            t_ref[p] = pair_product(side_by_side(t_ref[p]), paired(m_ref[p], masks))
        return carry

    lax.fori_loop(0, NEWTON - 2, step, 0)
    for p in range(pairs):
        middle = 1.5 * eye - 0.5 * t_ref[p]
        rows_z = jnp.concatenate([z_ref[p], q_ref[p]], axis=0)
        out = pair_product(side_by_side(rows_z), paired(middle, masks))
        z_ref[p] = out[:members]
        q_ref[p] = out[members:]
    for p in range(pairs):
        root = z_ref[p]
        trace = tr_ref[p][:1]
        pulled = pair_product(side_by_side(q_ref[p]), paired(root, masks))[:1] / trace
        scale = math.sqrt(members - 1.0) / jnp.sqrt(trace)
        p0 = (members - 1.0) / trace
        z0 = jnp.ones_like(p0)
        for _ in range(NEWTON):
            m0 = 1.5 - 0.5 * z0 * p0
            p0 = p0 * m0
            z0 = m0 * z0
        full = scale * root + (pulled + (1.0 - scale * z0) * (1.0 / members))
        hi, lo = split2(full)
        ks = slice((p % 2) * 128, (p % 2) * 128 + 128)
        hi_ref[p // 2, :, ks] = hi
        lo_ref[p // 2, :, ks] = lo


def equivalents_kernel(planes, cell, kind, value, error, wind_x, wind_y, o_ref, info, *scratch):
    local, fields = planes.shape[1], planes.shape[2]
    n_obs = o_ref.shape[2]
    sems, buf_i, buf_f, buf_w = scratch
    jobs = [(cell, buf_i.at[0]), (kind, buf_i.at[1]), (value, buf_f.at[0]), (error, buf_f.at[1])]
    jobs += [(wind_x, buf_w.at[0]), (wind_y, buf_w.at[1])]
    copies = [pltpu.make_async_copy(src, dst, sems.at[n]) for n, (src, dst) in enumerate(jobs)]
    for copy in copies:
        copy.start()
    for copy in copies:
        copy.wait()
    cells = buf_i[0]
    pick = (iota((256, n_obs), 0) == cells).astype(F32).astype(BF16)
    wanted = iota((fields, n_obs), 0) == buf_i[1] * 4
    found = [
        mm(jnp.concatenate([planes[0, m], planes[1, m]], axis=1), pick) for m in range(local)
    ]
    rows = [jnp.sum(jnp.where(wanted, x, 0.0), axis=0, keepdims=True) for x in found]
    full = jnp.concatenate(rows, axis=0)
    for d in range(o_ref.shape[0]):
        o_ref[d] = full
    row = (cells >= 128).astype(jnp.int32)
    sub = iota((8, n_obs), 0)
    lines = [buf_f[0], buf_f[1], row.astype(F32), (cells - 128 * row).astype(F32)]
    top = jnp.zeros((8, n_obs), F32)
    for r, line in enumerate(lines):
        top = jnp.where(sub == r, line, top)
    info[:8] = top
    for axis in range(2):
        for level in range(4):
            for half in range(2):
                info[8 + axis * 4 + level : 9 + axis * 4 + level, half * 128 : half * 128 + 128] = (
                    buf_w[axis, level, half : half + 1]
                )


def payload_kernel(planes, o_ref, main, rest):
    local = planes.shape[1]
    ident = (iota((128, 128), 0) == iota((128, 128), 1)).astype(F32).astype(BF16)
    lane = iota((8, 128), 1) // 32
    turned = []
    for row in range(2):
        for m in range(local):
            x = planes[row, m]
            turned.append(mm_nt(ident, jnp.concatenate([x[:128]] + [x[128:]] * 4, axis=0)))
    for row in range(2):
        for m in range(local):
            out = turned[row * local + m]
            main[pl.ds(row * 1024 + m, 128, stride=local), :] = out[:, :128]
            for q in range(4):
                tail = jnp.zeros((8, 128), F32)
                for cc in range(4):
                    at = q * 32 + cc * 8
                    tail = jnp.where(lane == cc, out[at : at + 8, 128:], tail)
                rest[pl.ds((row * 4 + q) * 64 + m, 8, stride=local), :] = tail
    for dest in range(8):
        o_ref[dest, :256] = main[dest * 256 : dest * 256 + 256, :].astype(BF16)
        o_ref[dest, 256:] = rest[dest * 64 : dest * 64 + 64, :].astype(BF16)


def transform_kernel(hi_ref, lo_ref, x_ref, *refs):
    outs, scr = refs[:-1], refs[-1]
    groups = hi_ref.shape[0]
    per = 32

    def members_of(base):
        x = x_ref[:, base : base + 16].astype(F32)
        return [x[:, k * 8 : k * 8 + 8].reshape(64, 128) for k in range(2)]

    lane64 = iota((64, 128), 1)
    masks = [(lane64 < 64).astype(F32).astype(BF16), (lane64 >= 64).astype(F32).astype(BF16)]

    def solved(p):
        ks = slice((p % 2) * 128, (p % 2) * 128 + 128)
        hi, lo = hi_ref[p // 2, :, ks], lo_ref[p // 2, :, ks]
        lhs = jnp.concatenate(
            [jnp.concatenate([hi * k, lo * k], axis=1) for k in masks], axis=0
        )
        x = jnp.concatenate(
            [
                jnp.concatenate(members_of(p * 16), axis=0),
                jnp.concatenate(members_of(256 + (p % 4) * 16), axis=0),
            ],
            axis=1,
        ).astype(BF16)
        return mm(lhs, jnp.concatenate([x, x], axis=0))

    ahead = 3
    count = 2 * groups
    results = {p: solved(p) for p in range(ahead)}
    for p in range(count):
        if p + ahead < count:
            results[p + ahead] = solved(p + ahead)
        out = results.pop(p)
        for c in range(2):
            val = out[c * 64 : c * 64 + 64]
            scr[0, pl.ds(p * 2 + c, 64, stride=per), :] = val[:, :128]
            scr[1, pl.ds(p * 2 + c, 64, stride=per), :] = val[:, 128:]
    lane = iota((8, 128), 1) // 32
    chunk = 8 // len(outs)
    for ml in range(8):
        for dest in range(8):
            base = (dest * 8 + ml) * per
            main = scr[0, base : base + per, :]
            rest = jnp.zeros((8, 128), F32)
            for cc in range(4):
                rest = jnp.where(lane == cc, scr[1, base + cc * 8 : base + cc * 8 + 8, :], rest)
            outs[ml // chunk][dest, ml % chunk] = jnp.concatenate(
                [main, rest, jnp.zeros_like(rest)], axis=0
            ).astype(BF16)[:40]


def relayout_kernel(x_ref, *outs):
    fields, chunk = outs[0].shape[2], outs[0].shape[1]
    f, at = iota((fields, 256), 0), iota((fields, 256), 1)
    ident = (((at < 128) & (f == at)) | ((at >= 128) & (f - 128 == at % 32))).astype(F32)
    ident = ident.astype(BF16)
    lane = iota((8, 128), 1) // 32
    for row in range(2):
        for ml in range(x_ref.shape[1]):
            mains, rests = [], []
            for q in range(4):
                block = x_ref[row * 4 + q, ml].astype(F32)
                mains.append(block[:32])
                rests += [jnp.where(lane == cc, block[32:40], 0.0) for cc in range(4)]
            full = jnp.concatenate(
                [jnp.concatenate(mains, axis=0), jnp.concatenate(rests, axis=0)], axis=1
            ).astype(BF16)
            outs[ml // chunk][row, ml % chunk] = mm_nt(ident, full).astype(BF16)


def advect_kernel(low_ref, own_ref, high_ref, cl_ref, co_ref, ch_ref, fac, o_ref):
    members, fields = own_ref.shape[1], own_ref.shape[2]
    lane = iota((8, 128), 1)

    def coeffs(ref, axis, row):
        c = ref[72:80, row * 128 : row * 128 + 128][axis * 4 : axis * 4 + 4]
        c = jnp.concatenate([c, c], axis=0)
        half, sq = 0.5 * c, 0.5 * c * c
        return half + sq, 1.0 - c * c, sq - half

    courant = [(cl_ref, 1), (co_ref, 0), (co_ref, 1), (ch_ref, 0)]
    cy = [coeffs(r, 1, k) for r, k in courant]
    cx = []
    for r, k in courant:
        a, b, c = coeffs(r, 0, k)
        cx.append((jnp.where(lane == 0, 0.0, a), b, jnp.where(lane == 127, 0.0, c)))
    shift_in, shift_out = iota((256, 256), 0) % 128, iota((256, 256), 1)
    shift = (
        ((shift_out < 128) & (shift_in == shift_out - 1))
        | ((shift_out >= 128) & (shift_in == shift_out - 127))
    ).astype(F32).astype(BF16)
    part = 80

    def scale(c, q):
        return (q.reshape(part // 8, 8, 128) * c[None]).reshape(part, 128)

    def rows(south, mid, north, k):
        a, b, c = cy[k]
        return scale(a, south) + scale(b, mid) + scale(c, north)

    def cols(planes, first):
        both = mm(
            jnp.concatenate([jnp.concatenate(split2(q), axis=1) for q in planes], axis=0), shift
        )
        outs = []
        for n, q in enumerate(planes):
            a, b, c = cx[first + n]
            near = both[n * part : n * part + part]
            outs.append(scale(a, near[:, :128]) + scale(b, q) + scale(c, near[:, 128:]))
        return outs

    units = [(m, f) for m in range(members) for f in range(0, fields, part)]

    def first(m, f):
        q = [
            r[k, m, f : f + part].astype(F32)
            for r, k in [
                (low_ref, 0), (low_ref, 1), (own_ref, 0),
                (own_ref, 1), (high_ref, 0), (high_ref, 1),
            ]
        ]
        return cols([rows(q[i], q[i + 1], q[i + 2], i) for i in range(4)], 0)

    ahead = 2
    mids = {u: first(*units[u]) for u in range(ahead)}
    for u, (m, f) in enumerate(units):
        if u + ahead < len(units):
            mids[u + ahead] = first(*units[u + ahead])
        q1 = mids.pop(u)
        q2 = cols([rows(q1[i], q1[i + 1], q1[i + 2], i + 1) for i in range(2)], 1)
        for r in range(2):
            o_ref[r, m, f : f + part] = (q2[r] * fac[r, f : f + part]).astype(BF16)


def call(kernel, outs, scratch=(), flops=10**8, nbytes=10**6):
    return pl.pallas_call(
        kernel,
        out_shape=outs,
        scratch_shapes=list(scratch),
        compiler_params=pltpu.CompilerParams(vmem_limit_bytes=40 << 20),
        cost_estimate=pl.CostEstimate(flops=flops, bytes_accessed=nbytes, transcendentals=0),
    )


def from_low(x):
    count = lax.axis_size("space")
    return lax.ppermute(x, "space", [(i, i + 1) for i in range(count - 1)])


def from_high(x):
    count = lax.axis_size("space")
    return lax.ppermute(x, "space", [(i + 1, i) for i in range(count - 1)])


def shards(
    ensemble,
    obs_value,
    obs_error,
    obs_cell,
    obs_species,
    patch_index,
    patch_count,
    courant_x,
    courant_y,
    dep_velocity,
    surface_factor,
):
    local, fields, tile_rows, columns = ensemble.shape
    levels = fields // dep_velocity.shape[0]
    n_obs = obs_cell.shape[1]
    per = patch_index.shape[1]
    maxobs = patch_index.shape[2]
    groups_mem = 8

    chunks = 2
    planes_in = jnp.transpose(ensemble, (2, 0, 1, 3))
    hbm = pl.BlockSpec(memory_space=pltpu.HBM)
    equiv, info = pl.pallas_call(
        equivalents_kernel,
        out_shape=[
            jax.ShapeDtypeStruct((groups_mem, local, n_obs), F32),
            jax.ShapeDtypeStruct((16, n_obs), F32),
        ],
        in_specs=[VMEM] + [hbm] * 6,
        scratch_shapes=[
            pltpu.SemaphoreType.DMA((6,)),
            pltpu.VMEM((2, 1, n_obs), jnp.int32),
            pltpu.VMEM((2, 1, n_obs), F32),
            pltpu.VMEM((2, levels, tile_rows, columns), F32),
        ],
        compiler_params=pltpu.CompilerParams(vmem_limit_bytes=40 << 20),
        cost_estimate=pl.CostEstimate(flops=10**8, bytes_accessed=10**6, transcendentals=0),
    )(planes_in, obs_cell, obs_species, obs_value, obs_error, courant_x, courant_y)
    everywhere = lax.all_to_all(equiv, "mem", 0, 0, tiled=True)
    payload = call(
        payload_kernel,
        jax.ShapeDtypeStruct((groups_mem, 320, 128), BF16),
        [pltpu.VMEM((2048, 128), F32), pltpu.VMEM((512, 128), F32)],
        flops=10**8,
    )(planes_in)

    packed = jnp.concatenate([everywhere.reshape(groups_mem * local, n_obs), info], axis=0)
    payload, packed = lax.optimization_barrier((payload, packed))
    low, high = from_low(packed), from_high(packed)
    state = lax.all_to_all(payload, "mem", 0, 0, tiled=True)

    used = jnp.arange(maxobs, dtype=jnp.int32)[None, :] < patch_count[0][:, None]
    idx = jnp.where(used, patch_index[0], -1).reshape(1, per * maxobs)
    cell_id = lax.axis_index("mem") * per + jnp.arange(per, dtype=jnp.int32)
    cell_id = jnp.broadcast_to(cell_id[:, None], (per, maxobs)).reshape(1, per * maxobs)
    pos = jnp.concatenate([cell_id // columns, cell_id % columns], axis=0).astype(F32)
    rate = jnp.where(
        (jnp.arange(fields, dtype=jnp.int32) % levels == 0)[:, None],
        jnp.repeat(dep_velocity, levels)[:, None],
        0.0,
    )
    factor = jnp.exp(-rate[None] * surface_factor[:, None, :])

    groups = per // 4
    hi, lo = call(
        weights_kernel,
        [jax.ShapeDtypeStruct((groups, 64, 256), BF16)] * 2,
        [
            pltpu.VMEM((2 * groups, 64, 128), F32),
            pltpu.VMEM((2 * groups, 64, 128), F32),
            pltpu.VMEM((2 * groups, 64, 128), F32),
            pltpu.VMEM((2 * groups, 16, 128), F32),
            pltpu.VMEM((2 * groups, 8, 128), F32),
        ],
        flops=10**10,
    )(low, packed, high, idx, pos)
    back = call(
        transform_kernel,
        [jax.ShapeDtypeStruct((groups_mem, local, 40, 128), BF16)],
        [pltpu.VMEM((2, 64 * per, 128), F32)],
        flops=10**9,
    )(hi, lo, state)[0]
    returned = lax.all_to_all(back, "mem", 0, 0, tiled=True)
    part_shape = jax.ShapeDtypeStruct((tile_rows, local // chunks, fields, columns), BF16)
    parts = call(relayout_kernel, [part_shape] * chunks, flops=10**8)(returned)
    halos = [(from_low(x), from_high(x)) for x in parts]
    outs = [
        call(advect_kernel, part_shape, flops=10**9)(below, x, above, low, packed, high, factor)
        for x, (below, above) in zip(parts, halos)
    ]
    done = jnp.concatenate(outs, axis=1)
    return jnp.transpose(done, (1, 2, 0, 3))


def solution(mesh):
    in_specs = (
        P("mem", None, "space", None),
        P("space", None),
        P("space", None),
        P("space", None),
        P("space", None),
        P("space", "mem", None),
        P("space", "mem"),
        P(None, "space", None),
        P(None, "space", None),
        P(),
        P("space", None),
    )
    out_specs = P("mem", None, "space", None)
    return jax.shard_map(shards, mesh=mesh, in_specs=in_specs, out_specs=out_specs, check_vma=False)
```

```python
import functools
import math

import jax
import jax.numpy as jnp
from jax import lax
from jax.experimental import pallas as pl
from jax.experimental.pallas import tpu as pltpu
from jax.sharding import PartitionSpec as P

NEWTON = 8
SUBSTEPS = 2
LOC = 1
F32 = jnp.float32
BF16 = jnp.bfloat16
VMEM = pl.BlockSpec(memory_space=pltpu.VMEM)


def iota(shape, dim):
    return lax.broadcasted_iota(jnp.int32, shape, dim)


def split2(x):
    hi = x.astype(BF16)
    return hi, (x - hi.astype(F32)).astype(BF16)


def split3(x):
    hi = x.astype(BF16).astype(F32)
    mid = (x - hi).astype(BF16).astype(F32)
    return hi, mid, x - hi - mid


def mm(a, b):
    return jnp.dot(a, b, preferred_element_type=F32)


def mm_nt(a, b):
    return lax.dot_general(a, b, (((1,), (1,)), ((), ())), preferred_element_type=F32)


def block_rows(x, width):
    lane = iota(x.shape, 1) // width
    zero = jnp.zeros_like(x)
    return jnp.concatenate(
        [jnp.where(lane == b, x, zero) for b in range(x.shape[1] // width)], axis=0
    )


def product(a2, b2, dot=mm):
    rows = a2[0].shape[0]
    first = dot(jnp.concatenate(a2, axis=0), b2[0])
    return first[:rows] + first[rows:] + dot(a2[0], b2[1])


def blocks2(x, width):
    hi, lo = split2(x)
    return block_rows(hi, width), block_rows(lo, width)


def side_by_side(x):
    return jnp.concatenate(split2(x), axis=1)


def paired(x, masks):
    cols = [jnp.concatenate([part * masks[0], part * masks[1]], axis=0) for part in split2(x)]
    once = jnp.concatenate(cols, axis=1)
    return jnp.concatenate([once, once], axis=0)


def pair_product(a, b):
    out = mm(a, b)
    return out[:, :128] + out[:, 128:]


def by_parity(is_odd, a, b):
    return jnp.where(is_odd, a, b), jnp.where(is_odd, b, a)


def weights_kernel(odd, near_a, own, near_b, idx_ref, pos_ref, hi_ref, lo_ref, t_ref, z_ref, m_ref, q_ref, tr_ref):
    members, maxobs = 64, 32
    pairs = t_ref.shape[0]
    is_odd = odd[0, 0] == 1
    low, high = by_parity(is_odd, near_a[...], near_b[...])
    parts = [low, own[...], high]
    equiv = jnp.concatenate([p[:members] for p in parts], axis=1)
    info = jnp.concatenate([p[members : members + 8] for p in parts], axis=1)
    n_obs = info.shape[1]
    tile = n_obs // 3
    row_obs = info[2:3] + ((iota((1, n_obs), 1) // tile).astype(F32) - 1.0) * 2.0
    sub = iota((8, n_obs), 0)
    rows = [*split3(info[0:1]), *split3(info[1:2]), row_obs, info[3:4]]
    table = jnp.zeros((8, n_obs), F32)
    for r, line in enumerate(rows):
        table = jnp.where(sub == r, line, table)
    lhs = jnp.concatenate([equiv, table, jnp.zeros((8, n_obs), F32)], axis=0).astype(BF16)

    eye = (iota((members, 128), 0) == iota((members, 128), 1) % 64).astype(F32)
    eye2 = jnp.concatenate([eye, eye], axis=1)
    spread = (iota((128, 256), 0) // maxobs == iota((128, 256), 1) // 64).astype(BF16)
    lane = iota((members, 128), 1)
    masks = [(lane < 64).astype(F32).astype(BF16), (lane >= 64).astype(F32).astype(BF16)]
    quarters = range(pairs // 4)
    sls = [slice(n * 256, n * 256 + 256) for n in quarters]
    gots = []
    for sl in sls:
        onehot = (iota((n_obs, 256), 0) == idx_ref[:, sl]).astype(F32).astype(BF16)
        gots.append(mm(lhs, onehot))
    grams = []
    for sl, got in zip(sls, gots):
        raw = got[:members]
        mean = jnp.sum(raw, axis=0, keepdims=True) * (1.0 / members)
        dev = raw - mean
        value = got[64:65] + got[65:66] + got[66:67]
        error = got[67:68] + got[68:69] + got[69:70]
        active = idx_ref[:, sl] >= 0
        d2 = (got[70:71] - pos_ref[0:1, sl]) ** 2 + (got[71:72] - pos_ref[1:2, sl]) ** 2
        rho = jnp.where(
            active, jnp.exp(-d2 / (2.0 * LOC * LOC)) / jnp.where(active, error, 1.0), 0.0
        )
        scaled = dev * rho
        pull = rho * (value - mean)
        power = jnp.sum(dev * scaled, axis=0, keepdims=True)
        for part in range(2):
            gs = slice(part * 128, part * 128 + 128)
            lhs_g = jnp.concatenate(
                [scaled[:, gs], jnp.broadcast_to(pull[:, gs], (16, 128))], axis=0
            )
            both = product(split2(lhs_g), blocks2(dev[:, gs], maxobs), mm_nt)
            sub16 = iota((16, 128), 0)
            p_hi, p_mid, p_lo = split3(power[:, gs])
            power3 = jnp.where(
                sub16 == 0, p_hi, jnp.where(sub16 == 1, p_mid, jnp.where(sub16 == 2, p_lo, 0.0))
            )
            grams.append((both, mm(power3.astype(BF16), spread)))
    for g, (both, powers) in enumerate(grams):
        trace = (members - 1.0) * members + jnp.sum(powers, axis=0, keepdims=True)
        pmat = (both[:members] + (members - 1.0) * eye2) * (1.0 / trace)
        for k in range(2):
            ks = slice(k * 128, k * 128 + 128)
            p = g * 2 + k
            t_ref[p] = pmat[:, ks]
            q_ref[p] = both[members : members + 16, ks]
            tr_ref[p] = jnp.broadcast_to(trace[:, ks], (8, 128))
    for p in range(pairs):
        middle = 1.5 * eye - 0.5 * t_ref[p]
        rows_m = jnp.concatenate([middle, q_ref[p]], axis=0)
        out = pair_product(side_by_side(rows_m), paired(middle, masks))
        z_ref[p] = middle
        q_ref[p] = out[members:]
        m_ref[p] = out[:members]
    for p in range(pairs):
        t_ref[p] = pair_product(side_by_side(t_ref[p]), paired(m_ref[p], masks))

    def step(_, carry):
        for p in range(pairs):
            middle = 1.5 * eye - 0.5 * t_ref[p]
            rows_m = jnp.concatenate([middle, z_ref[p], q_ref[p]], axis=0)
            out = pair_product(side_by_side(rows_m), paired(middle, masks))
            m_ref[p] = out[:members]
            z_ref[p] = out[members : 2 * members]
            q_ref[p] = out[2 * members :]
        for p in range(pairs):
            t_ref[p] = pair_product(side_by_side(t_ref[p]), paired(m_ref[p], masks))
        return carry

    lax.fori_loop(0, NEWTON - 2, step, 0)
    for p in range(pairs):
        middle = 1.5 * eye - 0.5 * t_ref[p]
        rows_z = jnp.concatenate([z_ref[p], q_ref[p]], axis=0)
        out = pair_product(side_by_side(rows_z), paired(middle, masks))
        z_ref[p] = out[:members]
        q_ref[p] = out[members:]
    for p in range(pairs):
        root = z_ref[p]
        trace = tr_ref[p][:1]
        pulled = pair_product(side_by_side(q_ref[p]), paired(root, masks))[:1] / trace
        scale = math.sqrt(members - 1.0) / jnp.sqrt(trace)
        p0 = (members - 1.0) / trace
        z0 = jnp.ones_like(p0)
        for _ in range(NEWTON):
            m0 = 1.5 - 0.5 * z0 * p0
            p0 = p0 * m0
            z0 = m0 * z0
        full = scale * root + (pulled + (1.0 - scale * z0) * (1.0 / members))
        hi, lo = split2(full)
        ks = slice((p % 2) * 128, (p % 2) * 128 + 128)
        hi_ref[p // 2, :, ks] = hi
        lo_ref[p // 2, :, ks] = lo


def equivalents_kernel(ens, cell, kind, o_ref, held, picks, sems):
    span = ens.shape[0] // 8
    n_obs = cell.shape[1]
    jobs = [(cell, picks.at[0]), (kind, picks.at[1])]
    jobs += [(ens.at[pl.ds(m * span, span)], held.at[m]) for m in range(8)]
    copies = [pltpu.make_async_copy(src, dst, sems.at[n]) for n, (src, dst) in enumerate(jobs)]
    for copy in copies:
        copy.start()
    copies[0].wait()
    copies[1].wait()
    cells = picks[0]
    row = (cells >= 128).astype(jnp.int32)
    pick = (iota((128, n_obs), 0) == cells - 128 * row).astype(F32).astype(BF16)
    wanted = iota((span, n_obs), 0) == picks[1] * 8 + row
    rows = []
    for m in range(0, 8, 2):
        copies[2 + m].wait()
        copies[3 + m].wait()
        found = [mm(held[m + k], pick) for k in range(2)]
        rows += [jnp.sum(jnp.where(wanted, x, 0.0), axis=0, keepdims=True) for x in found]
    full = jnp.concatenate(rows, axis=0)
    for d in range(o_ref.shape[0]):
        o_ref[d] = full


def payload_kernel(ens, cell, value, error, wind_x, wind_y, o_ref, info, flat, main, rest):
    local = 8
    fields = ens.shape[0] // (2 * local)
    ident = (iota((128, 128), 0) == iota((128, 128), 1)).astype(F32).astype(BF16)
    lane = iota((8, 128), 1) // 32
    flat[...] = ens[...].astype(F32)

    def turned(n):
        row, m = n // local, n % local
        x = flat[pl.ds(m * 2 * fields + row, fields, stride=2), :].astype(BF16)
        return mm_nt(ident, jnp.concatenate([x[:128]] + [x[128:]] * 4, axis=0))

    ahead = 3
    queue = [turned(n) for n in range(ahead)]
    for n in range(2 * local):
        row, m = n // local, n % local
        if n + ahead < 2 * local:
            queue.append(turned(n + ahead))
        out = queue.pop(0)
        main[pl.ds(row * 1024 + m, 128, stride=local), :] = out[:, :128]
        for q in range(4):
            tail = jnp.zeros((8, 128), F32)
            for cc in range(4):
                at = q * 32 + cc * 8
                tail = jnp.where(lane == cc, out[at : at + 8, 128:], tail)
            rest[pl.ds((row * 4 + q) * 64 + m, 8, stride=local), :] = tail
    for dest in range(8):
        o_ref[dest, :256] = main[dest * 256 : dest * 256 + 256, :].astype(BF16)
        o_ref[dest, 256:] = rest[dest * 64 : dest * 64 + 64, :].astype(BF16)
    cells = cell[...]
    n_obs = cells.shape[1]
    row = (cells >= 128).astype(jnp.int32)
    sub = iota((8, n_obs), 0)
    lines = [value[...], error[...], row.astype(F32), (cells - 128 * row).astype(F32)]
    top = jnp.zeros((8, n_obs), F32)
    for r, line in enumerate(lines):
        top = jnp.where(sub == r, line, top)
    info[:8] = top
    for axis, wind in enumerate((wind_x, wind_y)):
        for level in range(4):
            for half in range(2):
                info[8 + axis * 4 + level : 9 + axis * 4 + level, half * 128 : half * 128 + 128] = (
                    wind[level, half : half + 1]
                )


def transform_kernel(hi_ref, lo_ref, x_ref, *refs):
    outs, scr = refs[:-1], refs[-1]
    groups = hi_ref.shape[0]
    per = 32

    def members_of(base):
        x = x_ref[:, base : base + 16].astype(F32)
        return [x[:, k * 8 : k * 8 + 8].reshape(64, 128) for k in range(2)]

    lane64 = iota((64, 128), 1)
    masks = [(lane64 < 64).astype(F32).astype(BF16), (lane64 >= 64).astype(F32).astype(BF16)]

    def solved(p):
        ks = slice((p % 2) * 128, (p % 2) * 128 + 128)
        hi, lo = hi_ref[p // 2, :, ks], lo_ref[p // 2, :, ks]
        lhs = jnp.concatenate(
            [jnp.concatenate([hi * k, lo * k], axis=1) for k in masks], axis=0
        )
        x = jnp.concatenate(
            [
                jnp.concatenate(members_of(p * 16), axis=0),
                jnp.concatenate(members_of(256 + (p % 4) * 16), axis=0),
            ],
            axis=1,
        ).astype(BF16)
        return mm(lhs, jnp.concatenate([x, x], axis=0))

    ahead = 3
    count = 2 * groups
    results = {p: solved(p) for p in range(ahead)}
    for p in range(count):
        if p + ahead < count:
            results[p + ahead] = solved(p + ahead)
        out = results.pop(p)
        for c in range(2):
            val = out[c * 64 : c * 64 + 64]
            scr[0, pl.ds(p * 2 + c, 64, stride=per), :] = val[:, :128]
            scr[1, pl.ds(p * 2 + c, 64, stride=per), :] = val[:, 128:]
    lane = iota((8, 128), 1) // 32
    chunk = 8 // len(outs)
    for ml in range(8):
        for dest in range(8):
            base = (dest * 8 + ml) * per
            main = scr[0, base : base + per, :]
            rest = jnp.zeros((8, 128), F32)
            for cc in range(4):
                rest = jnp.where(lane == cc, scr[1, base + cc * 8 : base + cc * 8 + 8, :], rest)
            outs[ml // chunk][dest, ml % chunk] = jnp.concatenate(
                [main, rest, jnp.zeros_like(rest)], axis=0
            ).astype(BF16)[:40]


def relayout_kernel(x_ref, *outs):
    fields = outs[0].shape[2]
    places = [(o, k) for o in outs for k in range(o.shape[1])]
    f, at = iota((fields, 256), 0), iota((fields, 256), 1)
    ident = (((at < 128) & (f == at)) | ((at >= 128) & (f - 128 == at % 32))).astype(F32)
    ident = ident.astype(BF16)
    lane = iota((8, 128), 1) // 32
    for row in range(2):
        for ml in range(x_ref.shape[1]):
            mains, rests = [], []
            for q in range(4):
                block = x_ref[row * 4 + q, ml].astype(F32)
                mains.append(block[:32])
                rests += [jnp.where(lane == cc, block[32:40], 0.0) for cc in range(4)]
            full = jnp.concatenate(
                [jnp.concatenate(mains, axis=0), jnp.concatenate(rests, axis=0)], axis=1
            ).astype(BF16)
            out, k = places[ml]
            out[row, k] = mm_nt(ident, full).astype(BF16)


def advect_kernel(odd, a_ref, own_ref, b_ref, ca_ref, co_ref, cb_ref, dep_ref, surf_ref, *refs):
    o_ref, fac, flat = refs[-3:]
    fields = own_ref.shape[2]
    is_odd = odd[0, 0] == 1
    lane = iota((8, 128), 1)
    wind_low, wind_high = by_parity(is_odd, ca_ref[72:80], cb_ref[72:80])
    wind_own = co_ref[72:80]

    def coeffs(wind, axis, row):
        c = wind[axis * 4 : axis * 4 + 4, row * 128 : row * 128 + 128]
        c = jnp.concatenate([c, c], axis=0)
        half, sq = 0.5 * c, 0.5 * c * c
        return half + sq, 1.0 - c * c, sq - half

    courant = [(wind_low, 1), (wind_own, 0), (wind_own, 1), (wind_high, 0)]
    cy = [coeffs(w, 1, k) for w, k in courant]
    cx = []
    for w, k in courant:
        a, b, c = coeffs(w, 0, k)
        cx.append((jnp.where(lane == 0, 0.0, a), b, jnp.where(lane == 127, 0.0, c)))

    @pl.when(pl.program_id(0) == 0)
    def _():
        own_level = iota((fields, dep_ref.shape[1]), 0) == 4 * iota((fields, dep_ref.shape[1]), 1)
        rate = jnp.sum(jnp.where(own_level, dep_ref[...], 0.0), axis=1, keepdims=True)
        for row in range(2):
            fac[row] = jnp.exp(-rate * surf_ref[row : row + 1, :])

    shift_in, shift_out = iota((256, 256), 0) % 128, iota((256, 256), 1)
    shift = (
        ((shift_out < 128) & (shift_in == shift_out - 1))
        | ((shift_out >= 128) & (shift_in == shift_out - 127))
    ).astype(F32).astype(BF16)
    part = 80

    def scale(c, q):
        return (q.reshape(part // 8, 8, 128) * c[None]).reshape(part, 128)

    def rows(south, mid, north, k):
        a, b, c = cy[k]
        return scale(a, south) + scale(b, mid) + scale(c, north)

    def cols(planes, first):
        both = mm(
            jnp.concatenate([jnp.concatenate(split2(q), axis=1) for q in planes], axis=0), shift
        )
        outs = []
        for n, q in enumerate(planes):
            a, b, c = cx[first + n]
            near = both[n * part : n * part + part]
            outs.append(scale(a, near[:, :128]) + scale(b, q) + scale(c, near[:, 128:]))
        return outs

    members = o_ref.shape[0] // (2 * fields)
    units = [(m, f) for m in range(members) for f in range(0, fields, part)]

    def first(j, f):
        m = pl.program_id(0) * members + j
        near = [
            by_parity(is_odd, a_ref[k, m, f : f + part], b_ref[k, m, f : f + part])
            for k in range(2)
        ]
        q = [near[0][0], near[1][0], own_ref[0, m, f : f + part]]
        q += [own_ref[1, m, f : f + part], near[0][1], near[1][1]]
        q = [x.astype(F32) for x in q]
        return cols([rows(q[i], q[i + 1], q[i + 2], i) for i in range(4)], 0)

    ahead = 2
    mids = {u: first(*units[u]) for u in range(ahead)}
    for u, (j, f) in enumerate(units):
        if u + ahead < len(units):
            mids[u + ahead] = first(*units[u + ahead])
        q1 = mids.pop(u)
        q2 = cols([rows(q1[i], q1[i + 1], q1[i + 2], i + 1) for i in range(2)], 1)
        base = (j * fields + f) * 2
        for r in range(2):
            flat[pl.ds(base + r, part, stride=2), :] = q2[r] * fac[r, f : f + part]
        o_ref[base : base + 2 * part] = flat[base : base + 2 * part, :].astype(BF16)


def params():
    return pltpu.CompilerParams(vmem_limit_bytes=40 << 20)


def cost(flops):
    return pl.CostEstimate(flops=flops, bytes_accessed=10**6, transcendentals=0)


def call(kernel, outs, scratch=(), flops=10**8, specs=None):
    return pl.pallas_call(
        kernel,
        out_shape=outs,
        **({} if specs is None else {"in_specs": specs}),
        scratch_shapes=list(scratch),
        compiler_params=params(),
        cost_estimate=cost(flops),
    )


def swap(x, first):
    pairs = []
    for low in range(first, lax.axis_size("space") - 1, 2):
        pairs += [(low, low + 1), (low + 1, low)]
    return lax.ppermute(x, "space", pairs)


def block_at(first, i):
    return first + i, 0


def shards(
    ensemble,
    obs_value,
    obs_error,
    obs_cell,
    obs_species,
    patch_index,
    patch_count,
    courant_x,
    courant_y,
    dep_velocity,
    surface_factor,
):
    local, fields, tile_rows, columns = ensemble.shape
    levels = fields // dep_velocity.shape[0]
    n_obs = obs_cell.shape[1]
    per = patch_index.shape[1]
    maxobs = patch_index.shape[2]
    groups_mem = 8

    sizes = (6, 2)
    flat = ensemble.reshape(local * fields * tile_rows, columns)
    hbm = pl.BlockSpec(memory_space=pltpu.HBM)
    equiv = pl.pallas_call(
        equivalents_kernel,
        out_shape=jax.ShapeDtypeStruct((groups_mem, local, n_obs), F32),
        in_specs=[hbm] * 3,
        scratch_shapes=[
            pltpu.VMEM((local, fields * tile_rows, columns), BF16),
            pltpu.VMEM((2, 1, n_obs), jnp.int32),
            pltpu.SemaphoreType.DMA((2 + local,)),
        ],
        compiler_params=pltpu.CompilerParams(vmem_limit_bytes=67000000),
        cost_estimate=cost(10**8),
    )(flat, obs_cell, obs_species)
    everywhere = lax.all_to_all(equiv, "mem", 0, 0, tiled=True)
    payload, info = call(
        payload_kernel,
        [
            jax.ShapeDtypeStruct((groups_mem, 320, 128), BF16),
            jax.ShapeDtypeStruct((16, n_obs), F32),
        ],
        [pltpu.VMEM(flat.shape, F32), pltpu.VMEM((2048, 128), F32), pltpu.VMEM((512, 128), F32)],
        flops=10**8,
    )(flat, obs_cell, obs_value, obs_error, courant_x, courant_y)
    packed = jnp.concatenate([everywhere.reshape(groups_mem * local, n_obs), info], axis=0)
    payload, packed = lax.optimization_barrier((payload, packed))
    near_a, near_b = swap(packed, 0), swap(packed, 1)
    state = lax.all_to_all(payload, "mem", 0, 0, tiled=True)
    odd = (lax.axis_index("space") % 2).reshape(1, 1)

    used = jnp.arange(maxobs, dtype=jnp.int32)[None, :] < patch_count[0][:, None]
    idx = jnp.where(used, patch_index[0], -1).reshape(1, per * maxobs)
    cell_id = lax.axis_index("mem") * per + jnp.arange(per, dtype=jnp.int32)
    cell_id = jnp.broadcast_to(cell_id[:, None], (per, maxobs)).reshape(1, per * maxobs)
    pos = jnp.concatenate([cell_id // columns, cell_id % columns], axis=0).astype(F32)

    smem = pl.BlockSpec(memory_space=pltpu.SMEM)
    groups = per // 4
    hi, lo = call(
        weights_kernel,
        [jax.ShapeDtypeStruct((groups, 64, 256), BF16)] * 2,
        [
            pltpu.VMEM((2 * groups, 64, 128), F32),
            pltpu.VMEM((2 * groups, 64, 128), F32),
            pltpu.VMEM((2 * groups, 64, 128), F32),
            pltpu.VMEM((2 * groups, 16, 128), F32),
            pltpu.VMEM((2 * groups, 8, 128), F32),
        ],
        flops=10**10,
        specs=[smem] + [VMEM] * 5,
    )(odd, near_a, packed, near_b, idx, pos)
    back = call(
        transform_kernel,
        [jax.ShapeDtypeStruct((groups_mem, local, 40, 128), BF16)],
        [pltpu.VMEM((2, 64 * per, 128), F32)],
        flops=10**9,
    )(hi, lo, state)[0]
    returned = lax.all_to_all(back, "mem", 0, 0, tiled=True)
    parts = call(
        relayout_kernel,
        [jax.ShapeDtypeStruct((tile_rows, n, fields, columns), BF16) for n in sizes],
        flops=10**8,
    )(returned)
    halos = [(swap(x, 0), swap(x, 1)) for x in parts]

    done, block = None, 2 * tile_rows * fields
    start = 0
    for n, x, (side_a, side_b) in zip(sizes, parts, halos):
        operands = [odd, side_a, x, side_b, near_a, packed, near_b]
        operands += [dep_velocity.reshape(1, -1), surface_factor]
        in_specs = [smem] + [VMEM] * 8
        if done is not None:
            operands.append(done)
            in_specs.append(pl.BlockSpec(memory_space=pl.ANY))
        done = pl.pallas_call(
            advect_kernel,
            out_shape=jax.ShapeDtypeStruct(flat.shape, BF16),
            grid=(n // 2,),
            in_specs=in_specs,
            out_specs=pl.BlockSpec((block, columns), functools.partial(block_at, start // 2)),
            scratch_shapes=[
                pltpu.VMEM((tile_rows, fields, columns), F32),
                pltpu.VMEM((block, columns), F32),
            ],
            input_output_aliases={} if start == 0 else {9: 0},
            compiler_params=params(),
            cost_estimate=cost(10**9),
        )(*operands)
        start += n
    return done.reshape(local, fields, tile_rows, columns)


def solution(mesh):
    in_specs = (
        P("mem", None, "space", None),
        P("space", None),
        P("space", None),
        P("space", None),
        P("space", None),
        P("space", "mem", None),
        P("space", "mem"),
        P(None, "space", None),
        P(None, "space", None),
        P(),
        P("space", None),
    )
    out_specs = P("mem", None, "space", None)
    return jax.shard_map(shards, mesh=mesh, in_specs=in_specs, out_specs=out_specs, check_vma=False)
```

```python
import functools
import math

import jax
import jax.numpy as jnp
from jax import lax
from jax.experimental import pallas as pl
from jax.experimental.pallas import tpu as pltpu
from jax.sharding import PartitionSpec as P

NEWTON = 8
SUBSTEPS = 2
LOC = 1
F32 = jnp.float32
BF16 = jnp.bfloat16
VMEM = pl.BlockSpec(memory_space=pltpu.VMEM)


def iota(shape, dim):
    return lax.broadcasted_iota(jnp.int32, shape, dim)


def split2(x):
    hi = x.astype(BF16)
    return hi, (x - hi.astype(F32)).astype(BF16)


def split3(x):
    hi = x.astype(BF16).astype(F32)
    mid = (x - hi).astype(BF16).astype(F32)
    return hi, mid, x - hi - mid


def mm(a, b):
    return jnp.dot(a, b, preferred_element_type=F32)


def mm_nt(a, b):
    return lax.dot_general(a, b, (((1,), (1,)), ((), ())), preferred_element_type=F32)


def block_rows(x, width):
    lane = iota(x.shape, 1) // width
    zero = jnp.zeros_like(x)
    return jnp.concatenate(
        [jnp.where(lane == b, x, zero) for b in range(x.shape[1] // width)], axis=0
    )


def product(a2, b2, dot=mm):
    rows = a2[0].shape[0]
    first = dot(jnp.concatenate(a2, axis=0), b2[0])
    return first[:rows] + first[rows:] + dot(a2[0], b2[1])


def blocks2(x, width):
    hi, lo = split2(x)
    return block_rows(hi, width), block_rows(lo, width)


def side_by_side(x):
    return jnp.concatenate(split2(x), axis=1)


def paired(x, masks):
    cols = [jnp.concatenate([part * masks[0], part * masks[1]], axis=0) for part in split2(x)]
    once = jnp.concatenate(cols, axis=1)
    return jnp.concatenate([once, once], axis=0)


def pair_product(a, b):
    out = mm(a, b)
    return out[:, :128] + out[:, 128:]


def by_parity(is_odd, a, b):
    return jnp.where(is_odd, a, b), jnp.where(is_odd, b, a)


def weights_kernel(odd, near_a, own, near_b, idx_ref, pos_ref, hi_ref, lo_ref, t_ref, z_ref, m_ref, q_ref, tr_ref):
    members, maxobs = 64, 32
    pairs = t_ref.shape[0]
    is_odd = odd[0, 0] == 1
    low, high = by_parity(is_odd, near_a[...], near_b[...])
    parts = [low, own[...], high]
    equiv = jnp.concatenate([p[:members] for p in parts], axis=1)
    info = jnp.concatenate([p[members : members + 8] for p in parts], axis=1)
    n_obs = info.shape[1]
    tile = n_obs // 3
    row_obs = info[2:3] + ((iota((1, n_obs), 1) // tile).astype(F32) - 1.0) * 2.0
    sub = iota((8, n_obs), 0)
    rows = [*split3(info[0:1]), *split3(info[1:2]), row_obs, info[3:4]]
    table = jnp.zeros((8, n_obs), F32)
    for r, line in enumerate(rows):
        table = jnp.where(sub == r, line, table)
    lhs = jnp.concatenate([equiv, table, jnp.zeros((8, n_obs), F32)], axis=0).astype(BF16)

    eye = (iota((members, 128), 0) == iota((members, 128), 1) % 64).astype(F32)
    eye2 = jnp.concatenate([eye, eye], axis=1)
    spread = (iota((128, 256), 0) // maxobs == iota((128, 256), 1) // 64).astype(BF16)
    lane = iota((members, 128), 1)
    masks = [(lane < 64).astype(F32).astype(BF16), (lane >= 64).astype(F32).astype(BF16)]
    quarters = range(pairs // 4)
    sls = [slice(n * 256, n * 256 + 256) for n in quarters]
    gots = []
    for sl in sls:
        onehot = (iota((n_obs, 256), 0) == idx_ref[:, sl]).astype(F32).astype(BF16)
        gots.append(mm(lhs, onehot))
    grams = []
    for sl, got in zip(sls, gots):
        raw = got[:members]
        mean = jnp.sum(raw, axis=0, keepdims=True) * (1.0 / members)
        dev = raw - mean
        value = got[64:65] + got[65:66] + got[66:67]
        error = got[67:68] + got[68:69] + got[69:70]
        active = idx_ref[:, sl] >= 0
        d2 = (got[70:71] - pos_ref[0:1, sl]) ** 2 + (got[71:72] - pos_ref[1:2, sl]) ** 2
        rho = jnp.where(
            active, jnp.exp(-d2 / (2.0 * LOC * LOC)) / jnp.where(active, error, 1.0), 0.0
        )
        scaled = dev * rho
        pull = rho * (value - mean)
        power = jnp.sum(dev * scaled, axis=0, keepdims=True)
        for part in range(2):
            gs = slice(part * 128, part * 128 + 128)
            lhs_g = jnp.concatenate(
                [scaled[:, gs], jnp.broadcast_to(pull[:, gs], (16, 128))], axis=0
            )
            both = product(split2(lhs_g), blocks2(dev[:, gs], maxobs), mm_nt)
            sub16 = iota((16, 128), 0)
            p_hi, p_mid, p_lo = split3(power[:, gs])
            power3 = jnp.where(
                sub16 == 0, p_hi, jnp.where(sub16 == 1, p_mid, jnp.where(sub16 == 2, p_lo, 0.0))
            )
            grams.append((both, mm(power3.astype(BF16), spread)))
    for g, (both, powers) in enumerate(grams):
        trace = (members - 1.0) * members + jnp.sum(powers, axis=0, keepdims=True)
        pmat = (both[:members] + (members - 1.0) * eye2) * (1.0 / trace)
        for k in range(2):
            ks = slice(k * 128, k * 128 + 128)
            p = g * 2 + k
            t_ref[p] = pmat[:, ks]
            q_ref[p] = both[members : members + 16, ks]
            tr_ref[p] = jnp.broadcast_to(trace[:, ks], (8, 128))
    for p in range(pairs):
        middle = 1.5 * eye - 0.5 * t_ref[p]
        rows_m = jnp.concatenate([middle, q_ref[p]], axis=0)
        out = pair_product(side_by_side(rows_m), paired(middle, masks))
        z_ref[p] = middle
        q_ref[p] = out[members:]
        m_ref[p] = out[:members]
    for p in range(pairs):
        t_ref[p] = pair_product(side_by_side(t_ref[p]), paired(m_ref[p], masks))

    def step(_, carry):
        for p in range(pairs):
            middle = 1.5 * eye - 0.5 * t_ref[p]
            rows_m = jnp.concatenate([middle, z_ref[p], q_ref[p]], axis=0)
            out = pair_product(side_by_side(rows_m), paired(middle, masks))
            m_ref[p] = out[:members]
            z_ref[p] = out[members : 2 * members]
            q_ref[p] = out[2 * members :]
        for p in range(pairs):
            t_ref[p] = pair_product(side_by_side(t_ref[p]), paired(m_ref[p], masks))
        return carry

    lax.fori_loop(0, NEWTON - 2, step, 0)
    for p in range(pairs):
        middle = 1.5 * eye - 0.5 * t_ref[p]
        rows_z = jnp.concatenate([z_ref[p], q_ref[p]], axis=0)
        out = pair_product(side_by_side(rows_z), paired(middle, masks))
        z_ref[p] = out[:members]
        q_ref[p] = out[members:]
    for p in range(pairs):
        root = z_ref[p]
        trace = tr_ref[p][:1]
        pulled = pair_product(side_by_side(q_ref[p]), paired(root, masks))[:1] / trace
        scale = math.sqrt(members - 1.0) / jnp.sqrt(trace)
        p0 = (members - 1.0) / trace
        z0 = jnp.ones_like(p0)
        for _ in range(NEWTON):
            m0 = 1.5 - 0.5 * z0 * p0
            p0 = p0 * m0
            z0 = m0 * z0
        full = scale * root + (pulled + (1.0 - scale * z0) * (1.0 / members))
        hi, lo = split2(full)
        ks = slice((p % 2) * 128, (p % 2) * 128 + 128)
        hi_ref[p // 2, :, ks] = hi
        lo_ref[p // 2, :, ks] = lo


def equivalents_kernel(ens, cell, kind, o_ref, held, picks, sems):
    span = ens.shape[0] // 8
    n_obs = cell.shape[1]
    jobs = [(cell, picks.at[0]), (kind, picks.at[1])]
    jobs += [(ens.at[pl.ds(m * span, span)], held.at[m]) for m in range(8)]
    copies = [pltpu.make_async_copy(src, dst, sems.at[n]) for n, (src, dst) in enumerate(jobs)]
    for copy in copies:
        copy.start()
    copies[0].wait()
    copies[1].wait()
    cells = picks[0]
    row = (cells >= 128).astype(jnp.int32)
    pick = (iota((128, n_obs), 0) == cells - 128 * row).astype(F32).astype(BF16)
    wanted = iota((span, n_obs), 0) == picks[1] * 8 + row
    rows = []
    for m in range(0, 8, 2):
        copies[2 + m].wait()
        copies[3 + m].wait()
        found = [mm(held[m + k], pick) for k in range(2)]
        rows += [jnp.sum(jnp.where(wanted, x, 0.0), axis=0, keepdims=True) for x in found]
    full = jnp.concatenate(rows, axis=0)
    for d in range(o_ref.shape[0]):
        o_ref[d] = full


def payload_kernel(
    ens, cell, value, error, wind_x, wind_y, o_ref, info, flat, main, rest, held, ints, floats, winds, sems
):
    local = 8
    span = ens.shape[0] // local
    fields = span // 2
    jobs = [(ens.at[pl.ds(m * span, span)], held.at[pl.ds(m * span, span)]) for m in range(local)]
    jobs += [(cell, ints), (value, floats.at[0]), (error, floats.at[1])]
    jobs += [(wind_x, winds.at[0]), (wind_y, winds.at[1])]
    copies = [pltpu.make_async_copy(src, dst, sems.at[n]) for n, (src, dst) in enumerate(jobs)]
    for copy in copies:
        copy.start()
    ident = (iota((128, 128), 0) == iota((128, 128), 1)).astype(F32).astype(BF16)
    lane = iota((8, 128), 1) // 32
    for m in range(local):
        copies[m].wait()
        flat[m * span : m * span + span] = held[m * span : m * span + span].astype(F32)

    def turned(n):
        row, m = n // local, n % local
        x = flat[pl.ds(m * 2 * fields + row, fields, stride=2), :].astype(BF16)
        return mm_nt(ident, jnp.concatenate([x[:128]] + [x[128:]] * 4, axis=0))

    ahead = 3
    queue = [turned(n) for n in range(ahead)]
    for n in range(2 * local):
        row, m = n // local, n % local
        if n + ahead < 2 * local:
            queue.append(turned(n + ahead))
        out = queue.pop(0)
        main[pl.ds(row * 1024 + m, 128, stride=local), :] = out[:, :128]
        for q in range(4):
            tail = jnp.zeros((8, 128), F32)
            for cc in range(4):
                at = q * 32 + cc * 8
                tail = jnp.where(lane == cc, out[at : at + 8, 128:], tail)
            rest[pl.ds((row * 4 + q) * 64 + m, 8, stride=local), :] = tail
    for dest in range(8):
        o_ref[dest, :256] = main[dest * 256 : dest * 256 + 256, :].astype(BF16)
        o_ref[dest, 256:] = rest[dest * 64 : dest * 64 + 64, :].astype(BF16)
    for copy in copies[local:]:
        copy.wait()
    cells = ints[...]
    n_obs = cells.shape[1]
    row = (cells >= 128).astype(jnp.int32)
    sub = iota((8, n_obs), 0)
    lines = [floats[0], floats[1], row.astype(F32), (cells - 128 * row).astype(F32)]
    top = jnp.zeros((8, n_obs), F32)
    for r, line in enumerate(lines):
        top = jnp.where(sub == r, line, top)
    info[:8] = top
    for axis in range(2):
        for level in range(4):
            for half in range(2):
                info[8 + axis * 4 + level : 9 + axis * 4 + level, half * 128 : half * 128 + 128] = (
                    winds[axis, level, half : half + 1]
                )


def transform_kernel(hi_ref, lo_ref, x_ref, *refs):
    outs, scr = refs[:-1], refs[-1]
    groups = hi_ref.shape[0]
    per = 32

    def members_of(base):
        x = x_ref[:, base : base + 16].astype(F32)
        return [x[:, k * 8 : k * 8 + 8].reshape(64, 128) for k in range(2)]

    lane64 = iota((64, 128), 1)
    masks = [(lane64 < 64).astype(F32).astype(BF16), (lane64 >= 64).astype(F32).astype(BF16)]

    def solved(p):
        ks = slice((p % 2) * 128, (p % 2) * 128 + 128)
        hi, lo = hi_ref[p // 2, :, ks], lo_ref[p // 2, :, ks]
        lhs = jnp.concatenate(
            [jnp.concatenate([hi * k, lo * k], axis=1) for k in masks], axis=0
        )
        x = jnp.concatenate(
            [
                jnp.concatenate(members_of(p * 16), axis=0),
                jnp.concatenate(members_of(256 + (p % 4) * 16), axis=0),
            ],
            axis=1,
        ).astype(BF16)
        return mm(lhs, jnp.concatenate([x, x], axis=0))

    ahead = 3
    count = 2 * groups
    results = {p: solved(p) for p in range(ahead)}
    for p in range(count):
        if p + ahead < count:
            results[p + ahead] = solved(p + ahead)
        out = results.pop(p)
        for c in range(2):
            val = out[c * 64 : c * 64 + 64]
            scr[0, pl.ds(p * 2 + c, 64, stride=per), :] = val[:, :128]
            scr[1, pl.ds(p * 2 + c, 64, stride=per), :] = val[:, 128:]
    lane = iota((8, 128), 1) // 32
    chunk = 8 // len(outs)
    for ml in range(8):
        for dest in range(8):
            base = (dest * 8 + ml) * per
            main = scr[0, base : base + per, :]
            rest = jnp.zeros((8, 128), F32)
            for cc in range(4):
                rest = jnp.where(lane == cc, scr[1, base + cc * 8 : base + cc * 8 + 8, :], rest)
            outs[ml // chunk][dest, ml % chunk] = jnp.concatenate(
                [main, rest, jnp.zeros_like(rest)], axis=0
            ).astype(BF16)[:40]


def relayout_kernel(x_ref, *outs):
    fields = outs[0].shape[2]
    places = [(o, k) for o in outs for k in range(o.shape[1])]
    f, at = iota((fields, 256), 0), iota((fields, 256), 1)
    ident = (((at < 128) & (f == at)) | ((at >= 128) & (f - 128 == at % 32))).astype(F32)
    ident = ident.astype(BF16)
    lane = iota((8, 128), 1) // 32
    for row in range(2):
        for ml in range(x_ref.shape[1]):
            mains, rests = [], []
            for q in range(4):
                block = x_ref[row * 4 + q, ml].astype(F32)
                mains.append(block[:32])
                rests += [jnp.where(lane == cc, block[32:40], 0.0) for cc in range(4)]
            full = jnp.concatenate(
                [jnp.concatenate(mains, axis=0), jnp.concatenate(rests, axis=0)], axis=1
            ).astype(BF16)
            out, k = places[ml]
            out[row, k] = mm_nt(ident, full).astype(BF16)


def advect_kernel(start, odd, a_ref, own_ref, b_ref, ca_ref, co_ref, cb_ref, dep_ref, surf_ref, *refs):
    o_ref, fac, flat, ready, sems = refs[-5:]
    fields = own_ref.shape[2]
    is_odd = odd[0, 0] == 1
    lane = iota((8, 128), 1)
    wind_low, wind_high = by_parity(is_odd, ca_ref[72:80], cb_ref[72:80])
    wind_own = co_ref[72:80]

    def coeffs(wind, axis, row):
        c = wind[axis * 4 : axis * 4 + 4, row * 128 : row * 128 + 128]
        c = jnp.concatenate([c, c], axis=0)
        half, sq = 0.5 * c, 0.5 * c * c
        return half + sq, 1.0 - c * c, sq - half

    courant = [(wind_low, 1), (wind_own, 0), (wind_own, 1), (wind_high, 0)]
    cy = [coeffs(w, 1, k) for w, k in courant]
    cx = []
    for w, k in courant:
        a, b, c = coeffs(w, 0, k)
        cx.append((jnp.where(lane == 0, 0.0, a), b, jnp.where(lane == 127, 0.0, c)))

    own_level = iota((fields, dep_ref.shape[1]), 0) == 4 * iota((fields, dep_ref.shape[1]), 1)
    rate = jnp.sum(jnp.where(own_level, dep_ref[...], 0.0), axis=1, keepdims=True)
    for row in range(2):
        fac[row] = jnp.exp(-rate * surf_ref[row : row + 1, :])

    shift_in, shift_out = iota((256, 256), 0) % 128, iota((256, 256), 1)
    shift = (
        ((shift_out < 128) & (shift_in == shift_out - 1))
        | ((shift_out >= 128) & (shift_in == shift_out - 127))
    ).astype(F32).astype(BF16)
    part = 80

    def scale(c, q):
        return (q.reshape(part // 8, 8, 128) * c[None]).reshape(part, 128)

    def rows(south, mid, north, k):
        a, b, c = cy[k]
        return scale(a, south) + scale(b, mid) + scale(c, north)

    def cols(planes, first):
        both = mm(
            jnp.concatenate([jnp.concatenate(split2(q), axis=1) for q in planes], axis=0), shift
        )
        outs = []
        for n, q in enumerate(planes):
            a, b, c = cx[first + n]
            near = both[n * part : n * part + part]
            outs.append(scale(a, near[:, :128]) + scale(b, q) + scale(c, near[:, 128:]))
        return outs

    members, span = own_ref.shape[1], 2 * fields
    units = [(m, f) for m in range(members) for f in range(0, fields, part)]

    def first(m, f):
        near = [
            by_parity(is_odd, a_ref[k, m, f : f + part], b_ref[k, m, f : f + part])
            for k in range(2)
        ]
        q = [near[0][0], near[1][0], own_ref[0, m, f : f + part]]
        q += [own_ref[1, m, f : f + part], near[0][1], near[1][1]]
        q = [x.astype(F32) for x in q]
        return cols([rows(q[i], q[i + 1], q[i + 2], i) for i in range(4)], 0)

    ahead = 2
    mids = {u: first(*units[u]) for u in range(ahead)}
    copies = []
    for u, (m, f) in enumerate(units):
        if u + ahead < len(units):
            mids[u + ahead] = first(*units[u + ahead])
        q1 = mids.pop(u)
        q2 = cols([rows(q1[i], q1[i + 1], q1[i + 2], i + 1) for i in range(2)], 1)
        base = m * span + 2 * f
        for r in range(2):
            flat[pl.ds(base + r, part, stride=2), :] = q2[r] * fac[r, f : f + part]
        ready[base : base + 2 * part] = flat[base : base + 2 * part, :].astype(BF16)
        if f + part == fields:
            copy = pltpu.make_async_copy(
                ready.at[pl.ds(m * span, span)],
                o_ref.at[pl.ds((start + m) * span, span)],
                sems.at[m],
            )
            copy.start()
            copies.append(copy)
    for copy in copies:
        copy.wait()


def params():
    return pltpu.CompilerParams(vmem_limit_bytes=40 << 20)


def cost(flops):
    return pl.CostEstimate(flops=flops, bytes_accessed=10**6, transcendentals=0)


def call(kernel, outs, scratch=(), flops=10**8, specs=None):
    return pl.pallas_call(
        kernel,
        out_shape=outs,
        **({} if specs is None else {"in_specs": specs}),
        scratch_shapes=list(scratch),
        compiler_params=params(),
        cost_estimate=cost(flops),
    )


def swap(x, first):
    pairs = []
    for low in range(first, lax.axis_size("space") - 1, 2):
        pairs += [(low, low + 1), (low + 1, low)]
    return lax.ppermute(x, "space", pairs)


def shards(
    ensemble,
    obs_value,
    obs_error,
    obs_cell,
    obs_species,
    patch_index,
    patch_count,
    courant_x,
    courant_y,
    dep_velocity,
    surface_factor,
):
    local, fields, tile_rows, columns = ensemble.shape
    levels = fields // dep_velocity.shape[0]
    n_obs = obs_cell.shape[1]
    per = patch_index.shape[1]
    maxobs = patch_index.shape[2]
    groups_mem = 8

    sizes = (4, 4)
    flat = ensemble.reshape(local * fields * tile_rows, columns)
    hbm = pl.BlockSpec(memory_space=pltpu.HBM)
    equiv = pl.pallas_call(
        equivalents_kernel,
        out_shape=jax.ShapeDtypeStruct((groups_mem, local, n_obs), F32),
        in_specs=[hbm] * 3,
        scratch_shapes=[
            pltpu.VMEM((local, fields * tile_rows, columns), BF16),
            pltpu.VMEM((2, 1, n_obs), jnp.int32),
            pltpu.SemaphoreType.DMA((2 + local,)),
        ],
        compiler_params=pltpu.CompilerParams(vmem_limit_bytes=67000000),
        cost_estimate=cost(10**8),
    )(flat, obs_cell, obs_species)
    everywhere = lax.all_to_all(equiv, "mem", 0, 0, tiled=True)
    payload, info = pl.pallas_call(
        payload_kernel,
        out_shape=[
            jax.ShapeDtypeStruct((groups_mem, 320, 128), BF16),
            jax.ShapeDtypeStruct((16, n_obs), F32),
        ],
        in_specs=[hbm] * 6,
        scratch_shapes=[
            pltpu.VMEM(flat.shape, F32),
            pltpu.VMEM((2048, 128), F32),
            pltpu.VMEM((512, 128), F32),
            pltpu.VMEM(flat.shape, BF16),
            pltpu.VMEM((1, n_obs), jnp.int32),
            pltpu.VMEM((2, 1, n_obs), F32),
            pltpu.VMEM((2, levels, tile_rows, columns), F32),
            pltpu.SemaphoreType.DMA((local + 5,)),
        ],
        compiler_params=pltpu.CompilerParams(vmem_limit_bytes=66900000),
        cost_estimate=cost(10**8),
    )(flat, obs_cell, obs_value, obs_error, courant_x, courant_y)
    packed = jnp.concatenate([everywhere.reshape(groups_mem * local, n_obs), info], axis=0)
    payload, packed, patch_index, patch_count = lax.optimization_barrier(
        (payload, packed, patch_index, patch_count)
    )
    near_a, near_b = swap(packed, 0), swap(packed, 1)
    state = lax.all_to_all(payload, "mem", 0, 0, tiled=True)
    odd = (lax.axis_index("space") % 2).reshape(1, 1)

    used = jnp.arange(maxobs, dtype=jnp.int32)[None, :] < patch_count[0][:, None]
    idx = jnp.where(used, patch_index[0], -1).reshape(1, per * maxobs)
    cell_id = lax.axis_index("mem") * per + jnp.arange(per, dtype=jnp.int32)
    cell_id = jnp.broadcast_to(cell_id[:, None], (per, maxobs)).reshape(1, per * maxobs)
    pos = jnp.concatenate([cell_id // columns, cell_id % columns], axis=0).astype(F32)

    smem = pl.BlockSpec(memory_space=pltpu.SMEM)
    groups = per // 4
    hi, lo = call(
        weights_kernel,
        [jax.ShapeDtypeStruct((groups, 64, 256), BF16)] * 2,
        [
            pltpu.VMEM((2 * groups, 64, 128), F32),
            pltpu.VMEM((2 * groups, 64, 128), F32),
            pltpu.VMEM((2 * groups, 64, 128), F32),
            pltpu.VMEM((2 * groups, 16, 128), F32),
            pltpu.VMEM((2 * groups, 8, 128), F32),
        ],
        flops=10**7,
        specs=[smem] + [VMEM] * 5,
    )(odd, near_a, packed, near_b, idx, pos)
    back = call(
        transform_kernel,
        [jax.ShapeDtypeStruct((groups_mem, local, 40, 128), BF16)],
        [pltpu.VMEM((2, 64 * per, 128), F32)],
        flops=10**9,
    )(hi, lo, state)[0]
    returned = lax.all_to_all(back, "mem", 0, 0, tiled=True)
    parts = call(
        relayout_kernel,
        [jax.ShapeDtypeStruct((tile_rows, n, fields, columns), BF16) for n in sizes],
        flops=10**8,
    )(returned)
    halos = [(swap(x, 0), swap(x, 1)) for x in parts]

    done, start = None, 0
    for n, x, (side_a, side_b) in zip(sizes, parts, halos):
        operands = [odd, side_a, x, side_b, near_a, packed, near_b]
        operands += [dep_velocity.reshape(1, -1), surface_factor]
        in_specs = [smem] + [VMEM] * 8
        if done is not None:
            operands.append(done)
            in_specs.append(hbm)
        span = n * fields * tile_rows
        done = pl.pallas_call(
            functools.partial(advect_kernel, start),
            out_shape=jax.ShapeDtypeStruct(flat.shape, BF16),
            in_specs=in_specs,
            out_specs=hbm,
            scratch_shapes=[
                pltpu.VMEM((tile_rows, fields, columns), F32),
                pltpu.VMEM((span, columns), F32),
                pltpu.VMEM((span, columns), BF16),
                pltpu.SemaphoreType.DMA((n,)),
            ],
            input_output_aliases={} if start == 0 else {9: 0},
            compiler_params=params(),
            cost_estimate=cost(10**9),
        )(*operands)
        start += n
    return done.reshape(local, fields, tile_rows, columns)


def solution(mesh):
    in_specs = (
        P("mem", None, "space", None),
        P("space", None),
        P("space", None),
        P("space", None),
        P("space", None),
        P("space", "mem", None),
        P("space", "mem"),
        P(None, "space", None),
        P(None, "space", None),
        P(),
        P("space", None),
    )
    out_specs = P("mem", None, "space", None)
    return jax.shard_map(shards, mesh=mesh, in_specs=in_specs, out_specs=out_specs, check_vma=False)
```

```python
import functools
import math

import jax
import jax.numpy as jnp
from jax import lax
from jax.experimental import pallas as pl
from jax.experimental.pallas import tpu as pltpu
from jax.sharding import PartitionSpec as P

NEWTON = 8
SUBSTEPS = 2
LOC = 1
F32 = jnp.float32
BF16 = jnp.bfloat16
VMEM = pl.BlockSpec(memory_space=pltpu.VMEM)


def iota(shape, dim):
    return lax.broadcasted_iota(jnp.int32, shape, dim)


def split2(x):
    hi = x.astype(BF16)
    return hi, (x - hi.astype(F32)).astype(BF16)


def split3(x):
    hi = x.astype(BF16).astype(F32)
    mid = (x - hi).astype(BF16).astype(F32)
    return hi, mid, x - hi - mid


def mm(a, b):
    return jnp.dot(a, b, preferred_element_type=F32)


def mm_nt(a, b):
    return lax.dot_general(a, b, (((1,), (1,)), ((), ())), preferred_element_type=F32)


def block_rows(x, width):
    lane = iota(x.shape, 1) // width
    zero = jnp.zeros_like(x)
    return jnp.concatenate(
        [jnp.where(lane == b, x, zero) for b in range(x.shape[1] // width)], axis=0
    )


def product(a2, b2, dot=mm):
    rows = a2[0].shape[0]
    first = dot(jnp.concatenate(a2, axis=0), b2[0])
    return first[:rows] + first[rows:] + dot(a2[0], b2[1])


def blocks2(x, width):
    hi, lo = split2(x)
    return block_rows(hi, width), block_rows(lo, width)


def side_by_side(x):
    return jnp.concatenate(split2(x), axis=1)


def paired(x, masks):
    cols = [jnp.concatenate([part * masks[0], part * masks[1]], axis=0) for part in split2(x)]
    once = jnp.concatenate(cols, axis=1)
    return jnp.concatenate([once, once], axis=0)


def pair_product(a, b):
    out = mm(a, b)
    return out[:, :128] + out[:, 128:]


def by_parity(is_odd, a, b):
    return jnp.where(is_odd, a, b), jnp.where(is_odd, b, a)


def weights_kernel(odd, near_a, own, near_b, idx_ref, pos_ref, hi_ref, lo_ref, t_ref, z_ref, m_ref, q_ref, tr_ref):
    members, maxobs = 64, 32
    pairs = t_ref.shape[0]
    is_odd = odd[0, 0] == 1
    low, high = by_parity(is_odd, near_a[...], near_b[...])
    parts = [low, own[...], high]
    equiv = jnp.concatenate([p[:members] for p in parts], axis=1)
    info = jnp.concatenate([p[members : members + 8] for p in parts], axis=1)
    n_obs = info.shape[1]
    tile = n_obs // 3
    row_obs = info[2:3] + ((iota((1, n_obs), 1) // tile).astype(F32) - 1.0) * 2.0
    sub = iota((8, n_obs), 0)
    rows = [*split3(info[0:1]), *split3(info[1:2]), row_obs, info[3:4]]
    table = jnp.zeros((8, n_obs), F32)
    for r, line in enumerate(rows):
        table = jnp.where(sub == r, line, table)
    lhs = jnp.concatenate([equiv, table, jnp.zeros((8, n_obs), F32)], axis=0).astype(BF16)

    eye = (iota((members, 128), 0) == iota((members, 128), 1) % 64).astype(F32)
    eye2 = jnp.concatenate([eye, eye], axis=1)
    spread = (iota((128, 256), 0) // maxobs == iota((128, 256), 1) // 64).astype(BF16)
    lane = iota((members, 128), 1)
    masks = [(lane < 64).astype(F32).astype(BF16), (lane >= 64).astype(F32).astype(BF16)]
    quarters = range(pairs // 4)
    sls = [slice(n * 256, n * 256 + 256) for n in quarters]
    gots = []
    for sl in sls:
        onehot = (iota((n_obs, 256), 0) == idx_ref[:, sl]).astype(F32).astype(BF16)
        gots.append(mm(lhs, onehot))
    grams = []
    for sl, got in zip(sls, gots):
        raw = got[:members]
        mean = jnp.sum(raw, axis=0, keepdims=True) * (1.0 / members)
        dev = raw - mean
        value = got[64:65] + got[65:66] + got[66:67]
        error = got[67:68] + got[68:69] + got[69:70]
        active = idx_ref[:, sl] >= 0
        d2 = (got[70:71] - pos_ref[0:1, sl]) ** 2 + (got[71:72] - pos_ref[1:2, sl]) ** 2
        rho = jnp.where(
            active, jnp.exp(-d2 / (2.0 * LOC * LOC)) / jnp.where(active, error, 1.0), 0.0
        )
        scaled = dev * rho
        pull = rho * (value - mean)
        power = jnp.sum(dev * scaled, axis=0, keepdims=True)
        for part in range(2):
            gs = slice(part * 128, part * 128 + 128)
            lhs_g = jnp.concatenate(
                [scaled[:, gs], jnp.broadcast_to(pull[:, gs], (16, 128))], axis=0
            )
            both = product(split2(lhs_g), blocks2(dev[:, gs], maxobs), mm_nt)
            sub16 = iota((16, 128), 0)
            p_hi, p_mid, p_lo = split3(power[:, gs])
            power3 = jnp.where(
                sub16 == 0, p_hi, jnp.where(sub16 == 1, p_mid, jnp.where(sub16 == 2, p_lo, 0.0))
            )
            grams.append((both, mm(power3.astype(BF16), spread)))
    for g, (both, powers) in enumerate(grams):
        trace = (members - 1.0) * members + jnp.sum(powers, axis=0, keepdims=True)
        pmat = (both[:members] + (members - 1.0) * eye2) * (1.0 / trace)
        for k in range(2):
            ks = slice(k * 128, k * 128 + 128)
            p = g * 2 + k
            t_ref[p] = pmat[:, ks]
            q_ref[p] = both[members : members + 16, ks]
            tr_ref[p] = jnp.broadcast_to(trace[:, ks], (8, 128))
    for p in range(pairs):
        middle = 1.5 * eye - 0.5 * t_ref[p]
        rows_m = jnp.concatenate([middle, q_ref[p]], axis=0)
        out = pair_product(side_by_side(rows_m), paired(middle, masks))
        z_ref[p] = middle
        q_ref[p] = out[members:]
        m_ref[p] = out[:members]
    for p in range(pairs):
        t_ref[p] = pair_product(side_by_side(t_ref[p]), paired(m_ref[p], masks))

    def step(_, carry):
        for p in range(pairs):
            middle = 1.5 * eye - 0.5 * t_ref[p]
            rows_m = jnp.concatenate([middle, z_ref[p], q_ref[p]], axis=0)
            out = pair_product(side_by_side(rows_m), paired(middle, masks))
            m_ref[p] = out[:members]
            z_ref[p] = out[members : 2 * members]
            q_ref[p] = out[2 * members :]
        for p in range(pairs):
            t_ref[p] = pair_product(side_by_side(t_ref[p]), paired(m_ref[p], masks))
        return carry

    lax.fori_loop(0, NEWTON - 2, step, 0)
    for p in range(pairs):
        middle = 1.5 * eye - 0.5 * t_ref[p]
        rows_z = jnp.concatenate([z_ref[p], q_ref[p]], axis=0)
        out = pair_product(side_by_side(rows_z), paired(middle, masks))
        z_ref[p] = out[:members]
        q_ref[p] = out[members:]
    for p in range(pairs):
        root = z_ref[p]
        trace = tr_ref[p][:1]
        pulled = pair_product(side_by_side(q_ref[p]), paired(root, masks))[:1] / trace
        scale = math.sqrt(members - 1.0) / jnp.sqrt(trace)
        p0 = (members - 1.0) / trace
        z0 = jnp.ones_like(p0)
        for _ in range(NEWTON):
            m0 = 1.5 - 0.5 * z0 * p0
            p0 = p0 * m0
            z0 = m0 * z0
        full = scale * root + (pulled + (1.0 - scale * z0) * (1.0 / members))
        hi, lo = split2(full)
        ks = slice((p % 2) * 128, (p % 2) * 128 + 128)
        hi_ref[p // 2, :, ks] = hi
        lo_ref[p // 2, :, ks] = lo


def equivalents_kernel(ens, cell, kind, o_ref, held, picks, sems):
    span = ens.shape[0] // 8
    n_obs = cell.shape[1]
    jobs = [(cell, picks.at[0]), (kind, picks.at[1])]
    jobs += [(ens.at[pl.ds(m * span, span)], held.at[m]) for m in range(8)]
    copies = [pltpu.make_async_copy(src, dst, sems.at[n]) for n, (src, dst) in enumerate(jobs)]
    for copy in copies:
        copy.start()
    copies[0].wait()
    copies[1].wait()
    cells = picks[0]
    row = (cells >= 128).astype(jnp.int32)
    pick = (iota((128, n_obs), 0) == cells - 128 * row).astype(F32).astype(BF16)
    wanted = iota((span, n_obs), 0) == picks[1] * 8 + row
    rows = []
    for m in range(0, 8, 2):
        copies[2 + m].wait()
        copies[3 + m].wait()
        found = [mm(held[m + k], pick) for k in range(2)]
        rows += [jnp.sum(jnp.where(wanted, x, 0.0), axis=0, keepdims=True) for x in found]
    full = jnp.concatenate(rows, axis=0)
    for d in range(o_ref.shape[0]):
        o_ref[d] = full


def payload_kernel(
    ens, cell, value, error, wind_x, wind_y, o_ref, info, flat, main, rest, held, ints, floats, winds, sems
):
    local = 8
    span = ens.shape[0] // local
    fields = span // 2
    jobs = [(ens.at[pl.ds(m * span, span)], held.at[pl.ds(m * span, span)]) for m in range(local)]
    jobs += [(cell, ints), (value, floats.at[0]), (error, floats.at[1])]
    jobs += [(wind_x, winds.at[0]), (wind_y, winds.at[1])]
    copies = [pltpu.make_async_copy(src, dst, sems.at[n]) for n, (src, dst) in enumerate(jobs)]
    for copy in copies:
        copy.start()
    ident = (iota((128, 128), 0) == iota((128, 128), 1)).astype(F32).astype(BF16)
    lane = iota((8, 128), 1) // 32
    for m in range(local):
        copies[m].wait()
        flat[m * span : m * span + span] = held[m * span : m * span + span].astype(F32)

    def turned(n):
        row, m = n // local, n % local
        x = flat[pl.ds(m * 2 * fields + row, fields, stride=2), :].astype(BF16)
        return mm_nt(ident, jnp.concatenate([x[:128]] + [x[128:]] * 4, axis=0))

    ahead = 3
    queue = [turned(n) for n in range(ahead)]
    for n in range(2 * local):
        row, m = n // local, n % local
        if n + ahead < 2 * local:
            queue.append(turned(n + ahead))
        out = queue.pop(0)
        main[pl.ds(row * 1024 + m, 128, stride=local), :] = out[:, :128]
        for q in range(4):
            tail = jnp.zeros((8, 128), F32)
            for cc in range(4):
                at = q * 32 + cc * 8
                tail = jnp.where(lane == cc, out[at : at + 8, 128:], tail)
            rest[pl.ds((row * 4 + q) * 64 + m, 8, stride=local), :] = tail
    for dest in range(8):
        o_ref[dest, :256] = main[dest * 256 : dest * 256 + 256, :].astype(BF16)
        o_ref[dest, 256:] = rest[dest * 64 : dest * 64 + 64, :].astype(BF16)
    for copy in copies[local:]:
        copy.wait()
    cells = ints[...]
    n_obs = cells.shape[1]
    row = (cells >= 128).astype(jnp.int32)
    sub = iota((8, n_obs), 0)
    lines = [floats[0], floats[1], row.astype(F32), (cells - 128 * row).astype(F32)]
    top = jnp.zeros((8, n_obs), F32)
    for r, line in enumerate(lines):
        top = jnp.where(sub == r, line, top)
    info[:8] = top
    for axis in range(2):
        for level in range(4):
            for half in range(2):
                info[8 + axis * 4 + level : 9 + axis * 4 + level, half * 128 : half * 128 + 128] = (
                    winds[axis, level, half : half + 1]
                )


def transform_kernel(hi_ref, lo_ref, x_ref, *refs):
    outs, scr = refs[:-1], refs[-1]
    groups = hi_ref.shape[0]
    per = 32

    def members_of(base):
        x = x_ref[:, base : base + 16].astype(F32)
        return [x[:, k * 8 : k * 8 + 8].reshape(64, 128) for k in range(2)]

    lane64 = iota((64, 128), 1)
    masks = [(lane64 < 64).astype(F32).astype(BF16), (lane64 >= 64).astype(F32).astype(BF16)]

    def solved(p):
        ks = slice((p % 2) * 128, (p % 2) * 128 + 128)
        hi, lo = hi_ref[p // 2, :, ks], lo_ref[p // 2, :, ks]
        lhs = jnp.concatenate(
            [jnp.concatenate([hi * k, lo * k], axis=1) for k in masks], axis=0
        )
        x = jnp.concatenate(
            [
                jnp.concatenate(members_of(p * 16), axis=0),
                jnp.concatenate(members_of(256 + (p % 4) * 16), axis=0),
            ],
            axis=1,
        ).astype(BF16)
        return mm(lhs, jnp.concatenate([x, x], axis=0))

    ahead = 3
    count = 2 * groups
    results = {p: solved(p) for p in range(ahead)}
    for p in range(count):
        if p + ahead < count:
            results[p + ahead] = solved(p + ahead)
        out = results.pop(p)
        for c in range(2):
            val = out[c * 64 : c * 64 + 64]
            scr[0, pl.ds(p * 2 + c, 64, stride=per), :] = val[:, :128]
            scr[1, pl.ds(p * 2 + c, 64, stride=per), :] = val[:, 128:]
    lane = iota((8, 128), 1) // 32
    chunk = 8 // len(outs)
    for ml in range(8):
        for dest in range(8):
            base = (dest * 8 + ml) * per
            main = scr[0, base : base + per, :]
            rest = jnp.zeros((8, 128), F32)
            for cc in range(4):
                rest = jnp.where(lane == cc, scr[1, base + cc * 8 : base + cc * 8 + 8, :], rest)
            outs[ml // chunk][dest, ml % chunk] = jnp.concatenate(
                [main, rest, jnp.zeros_like(rest)], axis=0
            ).astype(BF16)[:40]


def relayout_kernel(x_ref, *outs):
    fields = outs[0].shape[2]
    places = [(o, k) for o in outs for k in range(o.shape[1])]
    f, at = iota((fields, 256), 0), iota((fields, 256), 1)
    ident = (((at < 128) & (f == at)) | ((at >= 128) & (f - 128 == at % 32))).astype(F32)
    ident = ident.astype(BF16)
    lane = iota((8, 128), 1) // 32
    for row in range(2):
        for ml in range(x_ref.shape[1]):
            mains, rests = [], []
            for q in range(4):
                block = x_ref[row * 4 + q, ml].astype(F32)
                mains.append(block[:32])
                rests += [jnp.where(lane == cc, block[32:40], 0.0) for cc in range(4)]
            full = jnp.concatenate(
                [jnp.concatenate(mains, axis=0), jnp.concatenate(rests, axis=0)], axis=1
            ).astype(BF16)
            out, k = places[ml]
            out[row, k] = mm_nt(ident, full).astype(BF16)


PART = 80


def scale(c, q):
    return (q.reshape(PART // 8, 8, 128) * c[None]).reshape(PART, 128)


def shift_matrix():
    source, to = iota((256, 256), 0) % 128, iota((256, 256), 1)
    west = (to < 128) & (source == to - 1)
    east = (to >= 128) & (source == to - 127)
    return (west | east).astype(F32).astype(BF16)


def columns_step(planes, winds, shift):
    both = mm(jnp.concatenate([side_by_side(q) for q in planes], axis=0), shift)
    outs = []
    for n, (q, (a, b, c)) in enumerate(zip(planes, winds)):
        near = both[n * PART : n * PART + PART]
        outs.append(scale(a, near[:, :128]) + scale(b, q) + scale(c, near[:, 128:]))
    return outs


def side_coeffs(is_high, own_wind, side_wind):
    lane = iota((8, 128), 1)

    def coeffs(c):
        c = jnp.concatenate([c, c], axis=0)
        half, sq = 0.5 * c, 0.5 * c * c
        return half + sq, 1.0 - c * c, sq - half

    result = []
    for wind, row_high in ((own_wind, 1), (side_wind, 0)):
        rows = (wind[:, :128], wind[:, 128:])
        w = jnp.where(is_high, rows[row_high], rows[1 - row_high])
        south, mid, north = coeffs(w[4:8])
        along_rows = (jnp.where(is_high, south, north), mid, jnp.where(is_high, north, south))
        west, mid, east = coeffs(w[:4])
        along_cols = (jnp.where(lane == 0, 0.0, west), mid, jnp.where(lane == 127, 0.0, east))
        result.append((along_rows, along_cols))
    return result


def rows_step(inner, mid, outer, c):
    return scale(c[0], inner) + scale(c[1], mid) + scale(c[2], outer)


def side_rows(is_high, side_ref, own_ref, m, f, coeffs):
    load = lambda ref, k: ref[k, m, f : f + PART]
    near, far = by_parity(is_high, load(side_ref, 0), load(side_ref, 1))
    close, other = by_parity(is_high, load(own_ref, 1), load(own_ref, 0))
    near, far, close, other = [x.astype(F32) for x in (near, far, close, other)]
    return [
        rows_step(other, close, near, coeffs[0][0]),
        rows_step(close, near, far, coeffs[1][0]),
    ]


def all_units(own_ref):
    return [(m, f) for m in range(own_ref.shape[1]) for f in range(0, own_ref.shape[2], PART)]


def first_side_kernel(odd, side_ref, own_ref, side_wind, own_wind, o_ref):
    is_high = odd[0, 0] == 0
    coeffs = side_coeffs(is_high, own_wind[72:80], side_wind[72:80])
    shift = shift_matrix()
    for m, f in all_units(own_ref):
        planes = side_rows(is_high, side_ref, own_ref, m, f, coeffs)
        outs = columns_step(planes, [c[1] for c in coeffs], shift)
        o_ref[0, m, f : f + PART] = outs[0]
        o_ref[1, m, f : f + PART] = outs[1]


def advect_kernel(odd, b_ref, own_ref, a_mid, ca_ref, co_ref, cb_ref, dep_ref, surf_ref, *refs):
    o_ref, fac, flat, ready, sems = refs
    members, fields = own_ref.shape[1], own_ref.shape[2]
    span = 2 * fields
    is_odd = odd[0, 0] == 1
    coeffs_a = side_coeffs(jnp.logical_not(is_odd), co_ref[72:80], ca_ref[72:80])
    coeffs_b = side_coeffs(is_odd, co_ref[72:80], cb_ref[72:80])
    shift = shift_matrix()
    own_level = iota((fields, dep_ref.shape[1]), 0) == 4 * iota((fields, dep_ref.shape[1]), 1)
    rate = jnp.sum(jnp.where(own_level, dep_ref[...], 0.0), axis=1, keepdims=True)
    for row in range(2):
        fac[row] = jnp.exp(-rate * surf_ref[row : row + 1, :])
    units = all_units(own_ref)

    def first(m, f):
        planes = side_rows(is_odd, b_ref, own_ref, m, f, coeffs_b)
        return columns_step(planes, [c[1] for c in coeffs_b], shift)

    ahead = 2
    mids = {u: first(*units[u]) for u in range(ahead)}
    copies = []
    for u, (m, f) in enumerate(units):
        if u + ahead < len(units):
            mids[u + ahead] = first(*units[u + ahead])
        own_b, out_b = mids.pop(u)
        own_a, out_a = a_mid[0, m, f : f + PART], a_mid[1, m, f : f + PART]
        planes = [
            rows_step(own_b, own_a, out_a, coeffs_a[0][0]),
            rows_step(own_a, own_b, out_b, coeffs_b[0][0]),
        ]
        ends = by_parity(is_odd, *columns_step(planes, [coeffs_a[0][1], coeffs_b[0][1]], shift))
        base = m * span + 2 * f
        for r in range(2):
            flat[pl.ds(base + r, PART, stride=2), :] = ends[r] * fac[r, f : f + PART]
        ready[base : base + 2 * PART] = flat[base : base + 2 * PART, :].astype(BF16)
        if f + PART == fields:
            rows = pl.ds(m * span, span)
            copy = pltpu.make_async_copy(ready.at[rows], o_ref.at[rows], sems.at[m])
            copy.start()
            copies.append(copy)
    for copy in copies:
        copy.wait()


def params():
    return pltpu.CompilerParams(vmem_limit_bytes=40 << 20)


def cost(flops):
    return pl.CostEstimate(flops=flops, bytes_accessed=10**6, transcendentals=0)


def call(kernel, outs, scratch=(), flops=10**8, specs=None):
    return pl.pallas_call(
        kernel,
        out_shape=outs,
        **({} if specs is None else {"in_specs": specs}),
        scratch_shapes=list(scratch),
        compiler_params=params(),
        cost_estimate=cost(flops),
    )


def swap(x, first):
    pairs = []
    for low in range(first, lax.axis_size("space") - 1, 2):
        pairs += [(low, low + 1), (low + 1, low)]
    return lax.ppermute(x, "space", pairs)


def shards(
    ensemble,
    obs_value,
    obs_error,
    obs_cell,
    obs_species,
    patch_index,
    patch_count,
    courant_x,
    courant_y,
    dep_velocity,
    surface_factor,
):
    local, fields, tile_rows, columns = ensemble.shape
    levels = fields // dep_velocity.shape[0]
    n_obs = obs_cell.shape[1]
    per = patch_index.shape[1]
    maxobs = patch_index.shape[2]
    groups_mem = 8

    flat = ensemble.reshape(local * fields * tile_rows, columns)
    hbm = pl.BlockSpec(memory_space=pltpu.HBM)
    equiv = pl.pallas_call(
        equivalents_kernel,
        out_shape=jax.ShapeDtypeStruct((groups_mem, local, n_obs), F32),
        in_specs=[hbm] * 3,
        scratch_shapes=[
            pltpu.VMEM((local, fields * tile_rows, columns), BF16),
            pltpu.VMEM((2, 1, n_obs), jnp.int32),
            pltpu.SemaphoreType.DMA((2 + local,)),
        ],
        compiler_params=pltpu.CompilerParams(vmem_limit_bytes=67000000),
        cost_estimate=cost(10**8),
    )(flat, obs_cell, obs_species)
    everywhere = lax.all_to_all(equiv, "mem", 0, 0, tiled=True)
    payload, info = pl.pallas_call(
        payload_kernel,
        out_shape=[
            jax.ShapeDtypeStruct((groups_mem, 320, 128), BF16),
            jax.ShapeDtypeStruct((16, n_obs), F32),
        ],
        in_specs=[hbm] * 6,
        scratch_shapes=[
            pltpu.VMEM(flat.shape, F32),
            pltpu.VMEM((2048, 128), F32),
            pltpu.VMEM((512, 128), F32),
            pltpu.VMEM(flat.shape, BF16),
            pltpu.VMEM((1, n_obs), jnp.int32),
            pltpu.VMEM((2, 1, n_obs), F32),
            pltpu.VMEM((2, levels, tile_rows, columns), F32),
            pltpu.SemaphoreType.DMA((local + 5,)),
        ],
        compiler_params=pltpu.CompilerParams(vmem_limit_bytes=66600000),
        cost_estimate=cost(10**8),
    )(flat, obs_cell, obs_value, obs_error, courant_x, courant_y)
    packed = jnp.concatenate([everywhere.reshape(groups_mem * local, n_obs), info], axis=0)
    payload, packed, patch_index, patch_count = lax.optimization_barrier(
        (payload, packed, patch_index, patch_count)
    )
    near_a, near_b = swap(packed, 0), swap(packed, 1)
    state = lax.all_to_all(payload, "mem", 0, 0, tiled=True)
    odd = (lax.axis_index("space") % 2).reshape(1, 1)

    used = jnp.arange(maxobs, dtype=jnp.int32)[None, :] < patch_count[0][:, None]
    idx = jnp.where(used, patch_index[0], -1).reshape(1, per * maxobs)
    cell_id = lax.axis_index("mem") * per + jnp.arange(per, dtype=jnp.int32)
    cell_id = jnp.broadcast_to(cell_id[:, None], (per, maxobs)).reshape(1, per * maxobs)
    pos = jnp.concatenate([cell_id // columns, cell_id % columns], axis=0).astype(F32)

    smem = pl.BlockSpec(memory_space=pltpu.SMEM)
    groups = per // 4
    hi, lo = call(
        weights_kernel,
        [jax.ShapeDtypeStruct((groups, 64, 256), BF16)] * 2,
        [
            pltpu.VMEM((2 * groups, 64, 128), F32),
            pltpu.VMEM((2 * groups, 64, 128), F32),
            pltpu.VMEM((2 * groups, 64, 128), F32),
            pltpu.VMEM((2 * groups, 16, 128), F32),
            pltpu.VMEM((2 * groups, 8, 128), F32),
        ],
        flops=10**10,
        specs=[smem] + [VMEM] * 5,
    )(odd, near_a, packed, near_b, idx, pos)
    back = call(
        transform_kernel,
        [jax.ShapeDtypeStruct((groups_mem, local, 40, 128), BF16)],
        [pltpu.VMEM((2, 64 * per, 128), F32)],
        flops=10**9,
    )(hi, lo, state)[0]
    returned = lax.all_to_all(back, "mem", 0, 0, tiled=True)
    plane_shape = (tile_rows, local, fields, columns)
    planes = call(
        relayout_kernel, [jax.ShapeDtypeStruct(plane_shape, BF16)], flops=10**8
    )(returned)[0]
    side_a, side_b = swap(planes, 0), swap(planes, 1)
    a_mid = call(
        first_side_kernel,
        jax.ShapeDtypeStruct(plane_shape, F32),
        flops=10**8,
        specs=[smem] + [VMEM] * 4,
    )(odd, side_a, planes, near_a, packed)
    done = pl.pallas_call(
        advect_kernel,
        out_shape=jax.ShapeDtypeStruct(flat.shape, BF16),
        in_specs=[smem] + [VMEM] * 8,
        out_specs=hbm,
        scratch_shapes=[
            pltpu.VMEM((tile_rows, fields, columns), F32),
            pltpu.VMEM(flat.shape, F32),
            pltpu.VMEM(flat.shape, BF16),
            pltpu.SemaphoreType.DMA((local,)),
        ],
        compiler_params=params(),
        cost_estimate=cost(10**9),
    )(
        odd, side_b, planes, a_mid, near_a, packed, near_b,
        dep_velocity.reshape(1, -1), surface_factor,
    )
    return done.reshape(local, fields, tile_rows, columns)


def solution(mesh):
    in_specs = (
        P("mem", None, "space", None),
        P("space", None),
        P("space", None),
        P("space", None),
        P("space", None),
        P("space", "mem", None),
        P("space", "mem"),
        P(None, "space", None),
        P(None, "space", None),
        P(),
        P("space", None),
    )
    out_specs = P("mem", None, "space", None)
    return jax.shard_map(shards, mesh=mesh, in_specs=in_specs, out_specs=out_specs, check_vma=False)
```

```python
import functools
import math

import jax
import jax.numpy as jnp
from jax import lax
from jax.experimental import pallas as pl
from jax.experimental.pallas import tpu as pltpu
from jax.sharding import PartitionSpec as P

NEWTON = 8
SUBSTEPS = 2
LOC = 1
F32 = jnp.float32
BF16 = jnp.bfloat16
VMEM = pl.BlockSpec(memory_space=pltpu.VMEM)


def iota(shape, dim):
    return lax.broadcasted_iota(jnp.int32, shape, dim)


def split2(x):
    hi = x.astype(BF16)
    return hi, (x - hi.astype(F32)).astype(BF16)


def split3(x):
    hi = x.astype(BF16).astype(F32)
    mid = (x - hi).astype(BF16).astype(F32)
    return hi, mid, x - hi - mid


def mm(a, b):
    return jnp.dot(a, b, preferred_element_type=F32)


def mm_nt(a, b):
    return lax.dot_general(a, b, (((1,), (1,)), ((), ())), preferred_element_type=F32)


def block_rows(x, width):
    lane = iota(x.shape, 1) // width
    zero = jnp.zeros_like(x)
    return jnp.concatenate(
        [jnp.where(lane == b, x, zero) for b in range(x.shape[1] // width)], axis=0
    )


def product(a2, b2, dot=mm):
    rows = a2[0].shape[0]
    first = dot(jnp.concatenate(a2, axis=0), b2[0])
    return first[:rows] + first[rows:] + dot(a2[0], b2[1])


def blocks2(x, width):
    hi, lo = split2(x)
    return block_rows(hi, width), block_rows(lo, width)


def side_by_side(x):
    return jnp.concatenate(split2(x), axis=1)


def paired(x, masks):
    cols = [jnp.concatenate([part * masks[0], part * masks[1]], axis=0) for part in split2(x)]
    once = jnp.concatenate(cols, axis=1)
    return jnp.concatenate([once, once], axis=0)


def pair_product(a, b):
    out = mm(a, b)
    return out[:, :128] + out[:, 128:]


def by_parity(is_odd, a, b):
    return jnp.where(is_odd, a, b), jnp.where(is_odd, b, a)


def weights_kernel(odd, near_a, own, near_b, idx_ref, pos_ref, hi_ref, lo_ref, t_ref, z_ref, m_ref, q_ref, tr_ref):
    members, maxobs = 64, 32
    pairs = t_ref.shape[0]
    is_odd = odd[0, 0] == 1
    low, high = by_parity(is_odd, near_a[...], near_b[...])
    parts = [low, own[...], high]
    equiv = jnp.concatenate([p[:members] for p in parts], axis=1)
    info = jnp.concatenate([p[members : members + 8] for p in parts], axis=1)
    n_obs = info.shape[1]
    tile = n_obs // 3
    row_obs = info[2:3] + ((iota((1, n_obs), 1) // tile).astype(F32) - 1.0) * 2.0
    sub = iota((8, n_obs), 0)
    rows = [*split3(info[0:1]), *split3(info[1:2]), row_obs, info[3:4]]
    table = jnp.zeros((8, n_obs), F32)
    for r, line in enumerate(rows):
        table = jnp.where(sub == r, line, table)
    lhs = jnp.concatenate([equiv, table, jnp.zeros((8, n_obs), F32)], axis=0).astype(BF16)

    eye = (iota((members, 128), 0) == iota((members, 128), 1) % 64).astype(F32)
    eye2 = jnp.concatenate([eye, eye], axis=1)
    spread = (iota((128, 256), 0) // maxobs == iota((128, 256), 1) // 64).astype(BF16)
    lane = iota((members, 128), 1)
    masks = [(lane < 64).astype(F32).astype(BF16), (lane >= 64).astype(F32).astype(BF16)]
    quarters = range(pairs // 4)
    sls = [slice(n * 256, n * 256 + 256) for n in quarters]
    gots = []
    for sl in sls:
        onehot = (iota((n_obs, 256), 0) == idx_ref[:, sl]).astype(F32).astype(BF16)
        gots.append(mm(lhs, onehot))
    grams = []
    for sl, got in zip(sls, gots):
        raw = got[:members]
        mean = jnp.sum(raw, axis=0, keepdims=True) * (1.0 / members)
        dev = raw - mean
        value = got[64:65] + got[65:66] + got[66:67]
        error = got[67:68] + got[68:69] + got[69:70]
        active = idx_ref[:, sl] >= 0
        d2 = (got[70:71] - pos_ref[0:1, sl]) ** 2 + (got[71:72] - pos_ref[1:2, sl]) ** 2
        rho = jnp.where(
            active, jnp.exp(-d2 / (2.0 * LOC * LOC)) / jnp.where(active, error, 1.0), 0.0
        )
        scaled = dev * rho
        pull = rho * (value - mean)
        power = jnp.sum(dev * scaled, axis=0, keepdims=True)
        for part in range(2):
            gs = slice(part * 128, part * 128 + 128)
            lhs_g = jnp.concatenate(
                [scaled[:, gs], jnp.broadcast_to(pull[:, gs], (16, 128))], axis=0
            )
            both = product(split2(lhs_g), blocks2(dev[:, gs], maxobs), mm_nt)
            sub16 = iota((16, 128), 0)
            p_hi, p_mid, p_lo = split3(power[:, gs])
            power3 = jnp.where(
                sub16 == 0, p_hi, jnp.where(sub16 == 1, p_mid, jnp.where(sub16 == 2, p_lo, 0.0))
            )
            grams.append((both, mm(power3.astype(BF16), spread)))
    for g, (both, powers) in enumerate(grams):
        trace = (members - 1.0) * members + jnp.sum(powers, axis=0, keepdims=True)
        pmat = (both[:members] + (members - 1.0) * eye2) * (1.0 / trace)
        for k in range(2):
            ks = slice(k * 128, k * 128 + 128)
            p = g * 2 + k
            t_ref[p] = pmat[:, ks]
            q_ref[p] = both[members : members + 16, ks]
            tr_ref[p] = jnp.broadcast_to(trace[:, ks], (8, 128))
    for p in range(pairs):
        middle = 1.5 * eye - 0.5 * t_ref[p]
        rows_m = jnp.concatenate([middle, q_ref[p]], axis=0)
        out = pair_product(side_by_side(rows_m), paired(middle, masks))
        z_ref[p] = middle
        q_ref[p] = out[members:]
        m_ref[p] = out[:members]
    for p in range(pairs):
        t_ref[p] = pair_product(side_by_side(t_ref[p]), paired(m_ref[p], masks))

    def step(_, carry):
        for p in range(pairs):
            middle = 1.5 * eye - 0.5 * t_ref[p]
            rows_m = jnp.concatenate([middle, z_ref[p], q_ref[p]], axis=0)
            out = pair_product(side_by_side(rows_m), paired(middle, masks))
            m_ref[p] = out[:members]
            z_ref[p] = out[members : 2 * members]
            q_ref[p] = out[2 * members :]
        for p in range(pairs):
            t_ref[p] = pair_product(side_by_side(t_ref[p]), paired(m_ref[p], masks))
        return carry

    lax.fori_loop(0, NEWTON - 2, step, 0)
    for p in range(pairs):
        middle = 1.5 * eye - 0.5 * t_ref[p]
        rows_z = jnp.concatenate([z_ref[p], q_ref[p]], axis=0)
        out = pair_product(side_by_side(rows_z), paired(middle, masks))
        z_ref[p] = out[:members]
        q_ref[p] = out[members:]
    for p in range(pairs):
        root = z_ref[p]
        trace = tr_ref[p][:1]
        pulled = pair_product(side_by_side(q_ref[p]), paired(root, masks))[:1] / trace
        scale = math.sqrt(members - 1.0) / jnp.sqrt(trace)
        p0 = (members - 1.0) / trace
        z0 = jnp.ones_like(p0)
        for _ in range(NEWTON):
            m0 = 1.5 - 0.5 * z0 * p0
            p0 = p0 * m0
            z0 = m0 * z0
        full = scale * root + (pulled + (1.0 - scale * z0) * (1.0 / members))
        hi, lo = split2(full)
        ks = slice((p % 2) * 128, (p % 2) * 128 + 128)
        hi_ref[p // 2, :, ks] = hi
        lo_ref[p // 2, :, ks] = lo


def equivalents_kernel(ens, cell, kind, o_ref, held, picks, sems):
    species, n_obs = ens.shape[1], cell.shape[1]
    jobs = [(cell, picks.at[0]), (kind, picks.at[1])]
    jobs += [(ens.at[m, :, 0], held.at[m]) for m in range(8)]
    copies = [pltpu.make_async_copy(src, dst, sems.at[n]) for n, (src, dst) in enumerate(jobs)]
    for copy in copies:
        copy.start()
    copies[0].wait()
    copies[1].wait()
    cells = picks[0]
    row = (cells >= 128).astype(jnp.int32)
    pick = (iota((128, n_obs), 0) == cells - 128 * row).astype(F32).astype(BF16)
    wanted = iota((2 * species, n_obs), 0) == picks[1] * 2 + row
    rows = []
    for m in range(0, 8, 2):
        copies[2 + m].wait()
        copies[3 + m].wait()
        found = [mm(held[m + k].reshape(2 * species, 128), pick) for k in range(2)]
        rows += [jnp.sum(jnp.where(wanted, x, 0.0), axis=0, keepdims=True) for x in found]
    full = jnp.concatenate(rows, axis=0)
    for d in range(o_ref.shape[0]):
        o_ref[d] = full


def payload_kernel(ens, cell, value, error, wind_x, wind_y, o_ref, info, flat, main, rest):
    local = 8
    fields = ens.shape[0] // (2 * local)
    ident = (iota((128, 128), 0) == iota((128, 128), 1)).astype(F32).astype(BF16)
    lane = iota((8, 128), 1) // 32
    flat[...] = ens[...].astype(F32)

    def turned(n):
        row, m = n // local, n % local
        x = flat[pl.ds(m * 2 * fields + row, fields, stride=2), :].astype(BF16)
        return mm_nt(ident, jnp.concatenate([x[:128]] + [x[128:]] * 4, axis=0))

    ahead = 3
    queue = [turned(n) for n in range(ahead)]
    for n in range(2 * local):
        row, m = n // local, n % local
        if n + ahead < 2 * local:
            queue.append(turned(n + ahead))
        out = queue.pop(0)
        main[pl.ds(row * 1024 + m, 128, stride=local), :] = out[:, :128]
        for q in range(4):
            tail = jnp.zeros((8, 128), F32)
            for cc in range(4):
                at = q * 32 + cc * 8
                tail = jnp.where(lane == cc, out[at : at + 8, 128:], tail)
            rest[pl.ds((row * 4 + q) * 64 + m, 8, stride=local), :] = tail
    for dest in range(8):
        o_ref[dest, :256] = main[dest * 256 : dest * 256 + 256, :].astype(BF16)
        o_ref[dest, 256:] = rest[dest * 64 : dest * 64 + 64, :].astype(BF16)
    cells = cell[...]
    n_obs = cells.shape[1]
    row = (cells >= 128).astype(jnp.int32)
    sub = iota((8, n_obs), 0)
    lines = [value[...], error[...], row.astype(F32), (cells - 128 * row).astype(F32)]
    top = jnp.zeros((8, n_obs), F32)
    for r, line in enumerate(lines):
        top = jnp.where(sub == r, line, top)
    info[:8] = top
    for axis, wind in enumerate((wind_x, wind_y)):
        for level in range(4):
            for half in range(2):
                info[8 + axis * 4 + level : 9 + axis * 4 + level, half * 128 : half * 128 + 128] = (
                    wind[level, half : half + 1]
                )


def transform_kernel(hi_ref, lo_ref, x_ref, *refs):
    outs, scr = refs[:-1], refs[-1]
    groups = hi_ref.shape[0]
    per = 32

    def members_of(base):
        x = x_ref[:, base : base + 16].astype(F32)
        return [x[:, k * 8 : k * 8 + 8].reshape(64, 128) for k in range(2)]

    lane64 = iota((64, 128), 1)
    masks = [(lane64 < 64).astype(F32).astype(BF16), (lane64 >= 64).astype(F32).astype(BF16)]

    def solved(p):
        ks = slice((p % 2) * 128, (p % 2) * 128 + 128)
        hi, lo = hi_ref[p // 2, :, ks], lo_ref[p // 2, :, ks]
        lhs = jnp.concatenate(
            [jnp.concatenate([hi * k, lo * k], axis=1) for k in masks], axis=0
        )
        x = jnp.concatenate(
            [
                jnp.concatenate(members_of(p * 16), axis=0),
                jnp.concatenate(members_of(256 + (p % 4) * 16), axis=0),
            ],
            axis=1,
        ).astype(BF16)
        return mm(lhs, jnp.concatenate([x, x], axis=0))

    ahead = 3
    count = 2 * groups
    results = {p: solved(p) for p in range(ahead)}
    for p in range(count):
        if p + ahead < count:
            results[p + ahead] = solved(p + ahead)
        out = results.pop(p)
        for c in range(2):
            val = out[c * 64 : c * 64 + 64]
            scr[0, pl.ds(p * 2 + c, 64, stride=per), :] = val[:, :128]
            scr[1, pl.ds(p * 2 + c, 64, stride=per), :] = val[:, 128:]
    lane = iota((8, 128), 1) // 32
    chunk = 8 // len(outs)
    for ml in range(8):
        for dest in range(8):
            base = (dest * 8 + ml) * per
            main = scr[0, base : base + per, :]
            rest = jnp.zeros((8, 128), F32)
            for cc in range(4):
                rest = jnp.where(lane == cc, scr[1, base + cc * 8 : base + cc * 8 + 8, :], rest)
            outs[ml // chunk][dest, ml % chunk] = jnp.concatenate(
                [main, rest, jnp.zeros_like(rest)], axis=0
            ).astype(BF16)[:40]


def relayout_kernel(x_ref, *outs):
    fields = outs[0].shape[2]
    places = [(o, k) for o in outs for k in range(o.shape[1])]
    f, at = iota((fields, 256), 0), iota((fields, 256), 1)
    ident = (((at < 128) & (f == at)) | ((at >= 128) & (f - 128 == at % 32))).astype(F32)
    ident = ident.astype(BF16)
    lane = iota((8, 128), 1) // 32
    for row in range(2):
        for ml in range(x_ref.shape[1]):
            mains, rests = [], []
            for q in range(4):
                block = x_ref[row * 4 + q, ml].astype(F32)
                mains.append(block[:32])
                rests += [jnp.where(lane == cc, block[32:40], 0.0) for cc in range(4)]
            full = jnp.concatenate(
                [jnp.concatenate(mains, axis=0), jnp.concatenate(rests, axis=0)], axis=1
            ).astype(BF16)
            out, k = places[ml]
            out[row, k] = mm_nt(ident, full).astype(BF16)


PART = 80


def scale(c, q):
    return (q.reshape(PART // 8, 8, 128) * c[None]).reshape(PART, 128)


def shift_matrix():
    source, to = iota((256, 256), 0) % 128, iota((256, 256), 1)
    west = (to < 128) & (source == to - 1)
    east = (to >= 128) & (source == to - 127)
    return (west | east).astype(F32).astype(BF16)


def columns_step(planes, winds, shift):
    both = mm(jnp.concatenate([side_by_side(q) for q in planes], axis=0), shift)
    outs = []
    for n, (q, (a, b, c)) in enumerate(zip(planes, winds)):
        near = both[n * PART : n * PART + PART]
        outs.append(scale(a, near[:, :128]) + scale(b, q) + scale(c, near[:, 128:]))
    return outs


def side_coeffs(is_high, own_wind, side_wind):
    lane = iota((8, 128), 1)

    def coeffs(c):
        c = jnp.concatenate([c, c], axis=0)
        half, sq = 0.5 * c, 0.5 * c * c
        return half + sq, 1.0 - c * c, sq - half

    result = []
    for wind, row_high in ((own_wind, 1), (side_wind, 0)):
        rows = (wind[:, :128], wind[:, 128:])
        w = jnp.where(is_high, rows[row_high], rows[1 - row_high])
        south, mid, north = coeffs(w[4:8])
        along_rows = (jnp.where(is_high, south, north), mid, jnp.where(is_high, north, south))
        west, mid, east = coeffs(w[:4])
        along_cols = (jnp.where(lane == 0, 0.0, west), mid, jnp.where(lane == 127, 0.0, east))
        result.append((along_rows, along_cols))
    return result


def rows_step(inner, mid, outer, c):
    return scale(c[0], inner) + scale(c[1], mid) + scale(c[2], outer)


def side_rows(is_high, side_ref, own_ref, m, f, coeffs):
    load = lambda ref, k: ref[k, m, f : f + PART]
    near, far = by_parity(is_high, load(side_ref, 0), load(side_ref, 1))
    close, other = by_parity(is_high, load(own_ref, 1), load(own_ref, 0))
    near, far, close, other = [x.astype(F32) for x in (near, far, close, other)]
    return [
        rows_step(other, close, near, coeffs[0][0]),
        rows_step(close, near, far, coeffs[1][0]),
    ]


def all_units(own_ref):
    return [(m, f) for m in range(own_ref.shape[1]) for f in range(0, own_ref.shape[2], PART)]


def first_side_kernel(odd, side_ref, own_ref, side_wind, own_wind, o_ref):
    is_high = odd[0, 0] == 0
    coeffs = side_coeffs(is_high, own_wind[72:80], side_wind[72:80])
    shift = shift_matrix()
    for m, f in all_units(own_ref):
        planes = side_rows(is_high, side_ref, own_ref, m, f, coeffs)
        outs = columns_step(planes, [c[1] for c in coeffs], shift)
        o_ref[0, m, f : f + PART] = outs[0]
        o_ref[1, m, f : f + PART] = outs[1]


def advect_kernel(odd, b_ref, own_ref, a_mid, ca_ref, co_ref, cb_ref, dep_ref, surf_ref, *refs):
    o_ref, fac, flat, ready, sems = refs
    members, fields = own_ref.shape[1], own_ref.shape[2]
    span = 2 * fields
    is_odd = odd[0, 0] == 1
    coeffs_a = side_coeffs(jnp.logical_not(is_odd), co_ref[72:80], ca_ref[72:80])
    coeffs_b = side_coeffs(is_odd, co_ref[72:80], cb_ref[72:80])
    shift = shift_matrix()
    own_level = iota((fields, dep_ref.shape[1]), 0) == 4 * iota((fields, dep_ref.shape[1]), 1)
    rate = jnp.sum(jnp.where(own_level, dep_ref[...], 0.0), axis=1, keepdims=True)
    for row in range(2):
        fac[row] = jnp.exp(-rate * surf_ref[row : row + 1, :])
    units = all_units(own_ref)

    def first(m, f):
        planes = side_rows(is_odd, b_ref, own_ref, m, f, coeffs_b)
        return columns_step(planes, [c[1] for c in coeffs_b], shift)

    ahead = 2
    mids = {u: first(*units[u]) for u in range(ahead)}
    copies = []
    for u, (m, f) in enumerate(units):
        if u + ahead < len(units):
            mids[u + ahead] = first(*units[u + ahead])
        own_b, out_b = mids.pop(u)
        own_a, out_a = a_mid[0, m, f : f + PART], a_mid[1, m, f : f + PART]
        planes = [
            rows_step(own_b, own_a, out_a, coeffs_a[0][0]),
            rows_step(own_a, own_b, out_b, coeffs_b[0][0]),
        ]
        ends = by_parity(is_odd, *columns_step(planes, [coeffs_a[0][1], coeffs_b[0][1]], shift))
        base = m * span + 2 * f
        for r in range(2):
            flat[pl.ds(base + r, PART, stride=2), :] = ends[r] * fac[r, f : f + PART]
        ready[base : base + 2 * PART] = flat[base : base + 2 * PART, :].astype(BF16)
        if f + PART == fields:
            rows = pl.ds(m * span, span)
            copy = pltpu.make_async_copy(ready.at[rows], o_ref.at[rows], sems.at[m])
            copy.start()
            copies.append(copy)
    for copy in copies:
        copy.wait()


def params():
    return pltpu.CompilerParams(vmem_limit_bytes=40 << 20)


def cost(flops):
    return pl.CostEstimate(flops=flops, bytes_accessed=10**6, transcendentals=0)


def call(kernel, outs, scratch=(), flops=10**8, specs=None):
    return pl.pallas_call(
        kernel,
        out_shape=outs,
        **({} if specs is None else {"in_specs": specs}),
        scratch_shapes=list(scratch),
        compiler_params=params(),
        cost_estimate=cost(flops),
    )


def swap(x, first):
    pairs = []
    for low in range(first, lax.axis_size("space") - 1, 2):
        pairs += [(low, low + 1), (low + 1, low)]
    return lax.ppermute(x, "space", pairs)


def shards(
    ensemble,
    obs_value,
    obs_error,
    obs_cell,
    obs_species,
    patch_index,
    patch_count,
    courant_x,
    courant_y,
    dep_velocity,
    surface_factor,
):
    local, fields, tile_rows, columns = ensemble.shape
    levels = fields // dep_velocity.shape[0]
    n_obs = obs_cell.shape[1]
    per = patch_index.shape[1]
    maxobs = patch_index.shape[2]
    groups_mem = 8

    flat = ensemble.reshape(local * fields * tile_rows, columns)
    hbm = pl.BlockSpec(memory_space=pltpu.HBM)
    equiv = pl.pallas_call(
        equivalents_kernel,
        out_shape=jax.ShapeDtypeStruct((groups_mem, local, n_obs), F32),
        in_specs=[hbm] * 3,
        scratch_shapes=[
            pltpu.VMEM((local, fields // levels, tile_rows, columns), BF16),
            pltpu.VMEM((2, 1, n_obs), jnp.int32),
            pltpu.SemaphoreType.DMA((2 + local,)),
        ],
        compiler_params=pltpu.CompilerParams(vmem_limit_bytes=67000000),
        cost_estimate=cost(10**8),
    )(
        ensemble.reshape(local, fields // levels, levels, tile_rows, columns), obs_cell, obs_species
    )
    everywhere = lax.all_to_all(equiv, "mem", 0, 0, tiled=True)
    payload, info = call(
        payload_kernel,
        [
            jax.ShapeDtypeStruct((groups_mem, 320, 128), BF16),
            jax.ShapeDtypeStruct((16, n_obs), F32),
        ],
        [pltpu.VMEM(flat.shape, F32), pltpu.VMEM((2048, 128), F32), pltpu.VMEM((512, 128), F32)],
        flops=10**8,
    )(flat, obs_cell, obs_value, obs_error, courant_x, courant_y)
    packed = jnp.concatenate([everywhere.reshape(groups_mem * local, n_obs), info], axis=0)
    payload, packed, patch_index, patch_count = lax.optimization_barrier(
        (payload, packed, patch_index, patch_count)
    )
    near_a, near_b = swap(packed, 0), swap(packed, 1)
    state = lax.all_to_all(payload, "mem", 0, 0, tiled=True)
    odd = (lax.axis_index("space") % 2).reshape(1, 1)

    used = jnp.arange(maxobs, dtype=jnp.int32)[None, :] < patch_count[0][:, None]
    idx = jnp.where(used, patch_index[0], -1).reshape(1, per * maxobs)
    cell_id = lax.axis_index("mem") * per + jnp.arange(per, dtype=jnp.int32)
    cell_id = jnp.broadcast_to(cell_id[:, None], (per, maxobs)).reshape(1, per * maxobs)
    pos = jnp.concatenate([cell_id // columns, cell_id % columns], axis=0).astype(F32)

    smem = pl.BlockSpec(memory_space=pltpu.SMEM)
    groups = per // 4
    hi, lo = call(
        weights_kernel,
        [jax.ShapeDtypeStruct((groups, 64, 256), BF16)] * 2,
        [
            pltpu.VMEM((2 * groups, 64, 128), F32),
            pltpu.VMEM((2 * groups, 64, 128), F32),
            pltpu.VMEM((2 * groups, 64, 128), F32),
            pltpu.VMEM((2 * groups, 16, 128), F32),
            pltpu.VMEM((2 * groups, 8, 128), F32),
        ],
        flops=10**10,
        specs=[smem] + [VMEM] * 5,
    )(odd, near_a, packed, near_b, idx, pos)
    back = call(
        transform_kernel,
        [jax.ShapeDtypeStruct((groups_mem, local, 40, 128), BF16)],
        [pltpu.VMEM((2, 64 * per, 128), F32)],
        flops=10**9,
    )(hi, lo, state)[0]
    returned = lax.all_to_all(back, "mem", 0, 0, tiled=True)
    plane_shape = (tile_rows, local, fields, columns)
    planes = call(
        relayout_kernel, [jax.ShapeDtypeStruct(plane_shape, BF16)], flops=10**8
    )(returned)[0]
    side_a, side_b = swap(planes, 0), swap(planes, 1)
    a_mid = call(
        first_side_kernel,
        jax.ShapeDtypeStruct(plane_shape, F32),
        flops=10**8,
        specs=[smem] + [VMEM] * 4,
    )(odd, side_a, planes, near_a, packed)
    done = pl.pallas_call(
        advect_kernel,
        out_shape=jax.ShapeDtypeStruct(flat.shape, BF16),
        in_specs=[smem] + [VMEM] * 8,
        out_specs=hbm,
        scratch_shapes=[
            pltpu.VMEM((tile_rows, fields, columns), F32),
            pltpu.VMEM(flat.shape, F32),
            pltpu.VMEM(flat.shape, BF16),
            pltpu.SemaphoreType.DMA((local,)),
        ],
        compiler_params=params(),
        cost_estimate=cost(10**9),
    )(
        odd, side_b, planes, a_mid, near_a, packed, near_b,
        dep_velocity.reshape(1, -1), surface_factor,
    )
    return done.reshape(local, fields, tile_rows, columns)


def solution(mesh):
    in_specs = (
        P("mem", None, "space", None),
        P("space", None),
        P("space", None),
        P("space", None),
        P("space", None),
        P("space", "mem", None),
        P("space", "mem"),
        P(None, "space", None),
        P(None, "space", None),
        P(),
        P("space", None),
    )
    out_specs = P("mem", None, "space", None)
    return jax.shard_map(shards, mesh=mesh, in_specs=in_specs, out_specs=out_specs, check_vma=False)
```

```python
import functools
import math

import jax
import jax.numpy as jnp
from jax import lax
from jax.experimental import pallas as pl
from jax.experimental.pallas import tpu as pltpu
from jax.sharding import PartitionSpec as P

NEWTON = 8
SUBSTEPS = 2
LOC = 1
F32 = jnp.float32
BF16 = jnp.bfloat16
VMEM = pl.BlockSpec(memory_space=pltpu.VMEM)


def iota(shape, dim):
    return lax.broadcasted_iota(jnp.int32, shape, dim)


def split2(x):
    hi = x.astype(BF16)
    return hi, (x - hi.astype(F32)).astype(BF16)


def split3(x):
    hi = x.astype(BF16).astype(F32)
    mid = (x - hi).astype(BF16).astype(F32)
    return hi, mid, x - hi - mid


def mm(a, b):
    return jnp.dot(a, b, preferred_element_type=F32)


def mm_nt(a, b):
    return lax.dot_general(a, b, (((1,), (1,)), ((), ())), preferred_element_type=F32)


def block_rows(x, width):
    lane = iota(x.shape, 1) // width
    zero = jnp.zeros_like(x)
    return jnp.concatenate(
        [jnp.where(lane == b, x, zero) for b in range(x.shape[1] // width)], axis=0
    )


def product(a2, b2, dot=mm):
    rows = a2[0].shape[0]
    first = dot(jnp.concatenate(a2, axis=0), b2[0])
    return first[:rows] + first[rows:] + dot(a2[0], b2[1])


def blocks2(x, width):
    hi, lo = split2(x)
    return block_rows(hi, width), block_rows(lo, width)


def side_by_side(x):
    return jnp.concatenate(split2(x), axis=1)


def paired(x, masks):
    cols = [jnp.concatenate([part * masks[0], part * masks[1]], axis=0) for part in split2(x)]
    once = jnp.concatenate(cols, axis=1)
    return jnp.concatenate([once, once], axis=0)


def pair_product(a, b):
    out = mm(a, b)
    return out[:, :128] + out[:, 128:]


def by_parity(is_odd, a, b):
    return jnp.where(is_odd, a, b), jnp.where(is_odd, b, a)


def weights_kernel(odd, near_a, own, near_b, idx_ref, pos_ref, hi_ref, lo_ref, t_ref, z_ref, m_ref, q_ref, tr_ref):
    members, maxobs = 64, 32
    pairs = t_ref.shape[0]
    is_odd = odd[0, 0] == 1
    low, high = by_parity(is_odd, near_a[...], near_b[...])
    parts = [low, own[...], high]
    equiv = jnp.concatenate([p[:members] for p in parts], axis=1)
    info = jnp.concatenate([p[members : members + 8] for p in parts], axis=1)
    n_obs = info.shape[1]
    tile = n_obs // 3
    row_obs = info[2:3] + ((iota((1, n_obs), 1) // tile).astype(F32) - 1.0) * 2.0
    sub = iota((8, n_obs), 0)
    rows = [*split3(info[0:1]), *split3(info[1:2]), row_obs, info[3:4]]
    table = jnp.zeros((8, n_obs), F32)
    for r, line in enumerate(rows):
        table = jnp.where(sub == r, line, table)
    lhs = jnp.concatenate([equiv, table, jnp.zeros((8, n_obs), F32)], axis=0).astype(BF16)

    eye = (iota((members, 128), 0) == iota((members, 128), 1) % 64).astype(F32)
    eye2 = jnp.concatenate([eye, eye], axis=1)
    spread = (iota((128, 256), 0) // maxobs == iota((128, 256), 1) // 64).astype(BF16)
    lane = iota((members, 128), 1)
    masks = [(lane < 64).astype(F32).astype(BF16), (lane >= 64).astype(F32).astype(BF16)]
    quarters = range(pairs // 4)
    sls = [slice(n * 256, n * 256 + 256) for n in quarters]
    gots = []
    for sl in sls:
        onehot = (iota((n_obs, 256), 0) == idx_ref[:, sl]).astype(F32).astype(BF16)
        gots.append(mm(lhs, onehot))
    grams = []
    for sl, got in zip(sls, gots):
        raw = got[:members]
        mean = jnp.sum(raw, axis=0, keepdims=True) * (1.0 / members)
        dev = raw - mean
        value = got[64:65] + got[65:66] + got[66:67]
        error = got[67:68] + got[68:69] + got[69:70]
        active = idx_ref[:, sl] >= 0
        d2 = (got[70:71] - pos_ref[0:1, sl]) ** 2 + (got[71:72] - pos_ref[1:2, sl]) ** 2
        rho = jnp.where(
            active, jnp.exp(-d2 / (2.0 * LOC * LOC)) / jnp.where(active, error, 1.0), 0.0
        )
        scaled = dev * rho
        pull = rho * (value - mean)
        power = jnp.sum(dev * scaled, axis=0, keepdims=True)
        for part in range(2):
            gs = slice(part * 128, part * 128 + 128)
            lhs_g = jnp.concatenate(
                [scaled[:, gs], jnp.broadcast_to(pull[:, gs], (16, 128))], axis=0
            )
            both = product(split2(lhs_g), blocks2(dev[:, gs], maxobs), mm_nt)
            sub16 = iota((16, 128), 0)
            p_hi, p_mid, p_lo = split3(power[:, gs])
            power3 = jnp.where(
                sub16 == 0, p_hi, jnp.where(sub16 == 1, p_mid, jnp.where(sub16 == 2, p_lo, 0.0))
            )
            grams.append((both, mm(power3.astype(BF16), spread)))
    for g, (both, powers) in enumerate(grams):
        trace = (members - 1.0) * members + jnp.sum(powers, axis=0, keepdims=True)
        pmat = (both[:members] + (members - 1.0) * eye2) * (1.0 / trace)
        for k in range(2):
            ks = slice(k * 128, k * 128 + 128)
            p = g * 2 + k
            t_ref[p] = pmat[:, ks]
            q_ref[p] = both[members : members + 16, ks]
            tr_ref[p] = jnp.broadcast_to(trace[:, ks], (8, 128))
    for p in range(pairs):
        middle = 1.5 * eye - 0.5 * t_ref[p]
        rows_m = jnp.concatenate([middle, q_ref[p]], axis=0)
        out = pair_product(side_by_side(rows_m), paired(middle, masks))
        z_ref[p] = middle
        q_ref[p] = out[members:]
        m_ref[p] = out[:members]
    for p in range(pairs):
        t_ref[p] = pair_product(side_by_side(t_ref[p]), paired(m_ref[p], masks))

    def step(_, carry):
        for p in range(pairs):
            middle = 1.5 * eye - 0.5 * t_ref[p]
            rows_m = jnp.concatenate([middle, z_ref[p], q_ref[p]], axis=0)
            out = pair_product(side_by_side(rows_m), paired(middle, masks))
            m_ref[p] = out[:members]
            z_ref[p] = out[members : 2 * members]
            q_ref[p] = out[2 * members :]
        for p in range(pairs):
            t_ref[p] = pair_product(side_by_side(t_ref[p]), paired(m_ref[p], masks))
        return carry

    lax.fori_loop(0, NEWTON - 2, step, 0)
    for p in range(pairs):
        middle = 1.5 * eye - 0.5 * t_ref[p]
        rows_z = jnp.concatenate([z_ref[p], q_ref[p]], axis=0)
        out = pair_product(side_by_side(rows_z), paired(middle, masks))
        z_ref[p] = out[:members]
        q_ref[p] = out[members:]
    for p in range(pairs):
        root = z_ref[p]
        trace = tr_ref[p][:1]
        pulled = pair_product(side_by_side(q_ref[p]), paired(root, masks))[:1] / trace
        scale = math.sqrt(members - 1.0) / jnp.sqrt(trace)
        p0 = (members - 1.0) / trace
        z0 = jnp.ones_like(p0)
        for _ in range(NEWTON):
            m0 = 1.5 - 0.5 * z0 * p0
            p0 = p0 * m0
            z0 = m0 * z0
        full = scale * root + (pulled + (1.0 - scale * z0) * (1.0 / members))
        hi, lo = split2(full)
        ks = slice((p % 2) * 128, (p % 2) * 128 + 128)
        hi_ref[p // 2, :, ks] = hi
        lo_ref[p // 2, :, ks] = lo


def equivalents_kernel(ens, cell, kind, o_ref, held, picks, sems):
    species, n_obs = ens.shape[1], cell.shape[1]
    jobs = [(cell, picks.at[0]), (kind, picks.at[1])]
    jobs += [(ens.at[m, :, 0], held.at[m]) for m in range(8)]
    copies = [pltpu.make_async_copy(src, dst, sems.at[n]) for n, (src, dst) in enumerate(jobs)]
    for copy in copies:
        copy.start()
    copies[0].wait()
    copies[1].wait()
    cells = picks[0]
    row = (cells >= 128).astype(jnp.int32)
    pick = (iota((128, n_obs), 0) == cells - 128 * row).astype(F32).astype(BF16)
    wanted = iota((2 * species, n_obs), 0) == picks[1] * 2 + row
    rows = []
    for m in range(0, 8, 2):
        copies[2 + m].wait()
        copies[3 + m].wait()
        found = [mm(held[m + k].reshape(2 * species, 128), pick) for k in range(2)]
        rows += [jnp.sum(jnp.where(wanted, x, 0.0), axis=0, keepdims=True) for x in found]
    full = jnp.concatenate(rows, axis=0)
    for d in range(o_ref.shape[0]):
        o_ref[d] = full


def payload_kernel(ens, cell, value, error, wind_x, wind_y, o_ref, info, flat, main, rest):
    local = 8
    fields = ens.shape[0] // (2 * local)
    ident = (iota((128, 128), 0) == iota((128, 128), 1)).astype(F32).astype(BF16)
    lane = iota((8, 128), 1) // 32
    flat[...] = ens[...].astype(F32)

    def turned(n):
        row, m = n // local, n % local
        x = flat[pl.ds(m * 2 * fields + row, fields, stride=2), :].astype(BF16)
        return mm_nt(ident, jnp.concatenate([x[:128]] + [x[128:]] * 4, axis=0))

    ahead = 3
    queue = [turned(n) for n in range(ahead)]
    for n in range(2 * local):
        row, m = n // local, n % local
        if n + ahead < 2 * local:
            queue.append(turned(n + ahead))
        out = queue.pop(0)
        main[pl.ds(row * 1024 + m, 128, stride=local), :] = out[:, :128]
        for q in range(4):
            tail = jnp.zeros((8, 128), F32)
            for cc in range(4):
                at = q * 32 + cc * 8
                tail = jnp.where(lane == cc, out[at : at + 8, 128:], tail)
            rest[pl.ds((row * 4 + q) * 64 + m, 8, stride=local), :] = tail
    for dest in range(8):
        o_ref[dest, :256] = main[dest * 256 : dest * 256 + 256, :].astype(BF16)
        o_ref[dest, 256:] = rest[dest * 64 : dest * 64 + 64, :].astype(BF16)
    cells = cell[...]
    n_obs = cells.shape[1]
    row = (cells >= 128).astype(jnp.int32)
    sub = iota((8, n_obs), 0)
    lines = [value[...], error[...], row.astype(F32), (cells - 128 * row).astype(F32)]
    top = jnp.zeros((8, n_obs), F32)
    for r, line in enumerate(lines):
        top = jnp.where(sub == r, line, top)
    info[:8] = top
    for axis, wind in enumerate((wind_x, wind_y)):
        for level in range(4):
            for half in range(2):
                info[8 + axis * 4 + level : 9 + axis * 4 + level, half * 128 : half * 128 + 128] = (
                    wind[level, half : half + 1]
                )


def transform_kernel(hi_ref, lo_ref, x_ref, *refs):
    outs, scr = refs[:-1], refs[-1]
    groups = hi_ref.shape[0]
    per = 32

    def members_of(base):
        x = x_ref[:, base : base + 16].astype(F32)
        return [x[:, k * 8 : k * 8 + 8].reshape(64, 128) for k in range(2)]

    lane64 = iota((64, 128), 1)
    masks = [(lane64 < 64).astype(F32).astype(BF16), (lane64 >= 64).astype(F32).astype(BF16)]

    def solved(p):
        ks = slice((p % 2) * 128, (p % 2) * 128 + 128)
        hi, lo = hi_ref[p // 2, :, ks], lo_ref[p // 2, :, ks]
        lhs = jnp.concatenate(
            [jnp.concatenate([hi * k, lo * k], axis=1) for k in masks], axis=0
        )
        x = jnp.concatenate(
            [
                jnp.concatenate(members_of(p * 16), axis=0),
                jnp.concatenate(members_of(256 + (p % 4) * 16), axis=0),
            ],
            axis=1,
        ).astype(BF16)
        return mm(lhs, jnp.concatenate([x, x], axis=0))

    ahead = 3
    count = 2 * groups
    results = {p: solved(p) for p in range(ahead)}
    for p in range(count):
        if p + ahead < count:
            results[p + ahead] = solved(p + ahead)
        out = results.pop(p)
        for c in range(2):
            val = out[c * 64 : c * 64 + 64]
            scr[0, pl.ds(p * 2 + c, 64, stride=per), :] = val[:, :128]
            scr[1, pl.ds(p * 2 + c, 64, stride=per), :] = val[:, 128:]
    lane = iota((8, 128), 1) // 32
    chunk = 8 // len(outs)
    for ml in range(8):
        for dest in range(8):
            base = (dest * 8 + ml) * per
            main = scr[0, base : base + per, :]
            rest = jnp.zeros((8, 128), F32)
            for cc in range(4):
                rest = jnp.where(lane == cc, scr[1, base + cc * 8 : base + cc * 8 + 8, :], rest)
            outs[ml // chunk][dest, ml % chunk] = jnp.concatenate(
                [main, rest, jnp.zeros_like(rest)], axis=0
            ).astype(BF16)[:40]


def relayout_kernel(x_ref, *outs):
    fields = outs[0].shape[2]
    places = [(o, k) for o in outs for k in range(o.shape[1])]
    f, at = iota((fields, 256), 0), iota((fields, 256), 1)
    ident = (((at < 128) & (f == at)) | ((at >= 128) & (f - 128 == at % 32))).astype(F32)
    ident = ident.astype(BF16)
    lane = iota((8, 128), 1) // 32
    for row in range(2):
        for ml in range(x_ref.shape[1]):
            mains, rests = [], []
            for q in range(4):
                block = x_ref[row * 4 + q, ml].astype(F32)
                mains.append(block[:32])
                rests += [jnp.where(lane == cc, block[32:40], 0.0) for cc in range(4)]
            full = jnp.concatenate(
                [jnp.concatenate(mains, axis=0), jnp.concatenate(rests, axis=0)], axis=1
            ).astype(BF16)
            out, k = places[ml]
            out[row, k] = mm_nt(ident, full).astype(BF16)


def advect_kernel(start, odd, a_ref, own_ref, b_ref, ca_ref, co_ref, cb_ref, dep_ref, surf_ref, *refs):
    o_ref, fac, flat, ready, sems = refs[-5:]
    fields = own_ref.shape[2]
    is_odd = odd[0, 0] == 1
    lane = iota((8, 128), 1)
    wind_low, wind_high = by_parity(is_odd, ca_ref[72:80], cb_ref[72:80])
    wind_own = co_ref[72:80]

    def coeffs(wind, axis, row):
        c = wind[axis * 4 : axis * 4 + 4, row * 128 : row * 128 + 128]
        c = jnp.concatenate([c, c], axis=0)
        half, sq = 0.5 * c, 0.5 * c * c
        return half + sq, 1.0 - c * c, sq - half

    courant = [(wind_low, 1), (wind_own, 0), (wind_own, 1), (wind_high, 0)]
    cy = [coeffs(w, 1, k) for w, k in courant]
    cx = []
    for w, k in courant:
        a, b, c = coeffs(w, 0, k)
        cx.append((jnp.where(lane == 0, 0.0, a), b, jnp.where(lane == 127, 0.0, c)))

    own_level = iota((fields, dep_ref.shape[1]), 0) == 4 * iota((fields, dep_ref.shape[1]), 1)
    rate = jnp.sum(jnp.where(own_level, dep_ref[...], 0.0), axis=1, keepdims=True)
    for row in range(2):
        fac[row] = jnp.exp(-rate * surf_ref[row : row + 1, :])

    shift_in, shift_out = iota((256, 256), 0) % 128, iota((256, 256), 1)
    shift = (
        ((shift_out < 128) & (shift_in == shift_out - 1))
        | ((shift_out >= 128) & (shift_in == shift_out - 127))
    ).astype(F32).astype(BF16)
    part = 80

    def scale(c, q):
        return (q.reshape(part // 8, 8, 128) * c[None]).reshape(part, 128)

    def rows(south, mid, north, k):
        a, b, c = cy[k]
        return scale(a, south) + scale(b, mid) + scale(c, north)

    def cols(planes, first):
        both = mm(
            jnp.concatenate([jnp.concatenate(split2(q), axis=1) for q in planes], axis=0), shift
        )
        outs = []
        for n, q in enumerate(planes):
            a, b, c = cx[first + n]
            near = both[n * part : n * part + part]
            outs.append(scale(a, near[:, :128]) + scale(b, q) + scale(c, near[:, 128:]))
        return outs

    members, span = own_ref.shape[1], 2 * fields
    units = [(m, f) for m in range(members) for f in range(0, fields, part)]

    def first(m, f):
        near = [
            by_parity(is_odd, a_ref[k, m, f : f + part], b_ref[k, m, f : f + part])
            for k in range(2)
        ]
        q = [near[0][0], near[1][0], own_ref[0, m, f : f + part]]
        q += [own_ref[1, m, f : f + part], near[0][1], near[1][1]]
        q = [x.astype(F32) for x in q]
        return cols([rows(q[i], q[i + 1], q[i + 2], i) for i in range(4)], 0)

    ahead = 2
    mids = {u: first(*units[u]) for u in range(ahead)}
    copies = []
    for u, (m, f) in enumerate(units):
        if u + ahead < len(units):
            mids[u + ahead] = first(*units[u + ahead])
        q1 = mids.pop(u)
        q2 = cols([rows(q1[i], q1[i + 1], q1[i + 2], i + 1) for i in range(2)], 1)
        base = m * span + 2 * f
        for r in range(2):
            flat[pl.ds(base + r, part, stride=2), :] = q2[r] * fac[r, f : f + part]
        ready[base : base + 2 * part] = flat[base : base + 2 * part, :].astype(BF16)
        if f + part == fields:
            copy = pltpu.make_async_copy(
                ready.at[pl.ds(m * span, span)],
                o_ref.at[pl.ds((start + m) * span, span)],
                sems.at[m],
            )
            copy.start()
            copies.append(copy)
    for copy in copies:
        copy.wait()


def params():
    return pltpu.CompilerParams(vmem_limit_bytes=40 << 20)


def cost(flops):
    return pl.CostEstimate(flops=flops, bytes_accessed=10**6, transcendentals=0)


def call(kernel, outs, scratch=(), flops=10**8, specs=None):
    return pl.pallas_call(
        kernel,
        out_shape=outs,
        **({} if specs is None else {"in_specs": specs}),
        scratch_shapes=list(scratch),
        compiler_params=params(),
        cost_estimate=cost(flops),
    )


def swap(x, first):
    pairs = []
    for low in range(first, lax.axis_size("space") - 1, 2):
        pairs += [(low, low + 1), (low + 1, low)]
    return lax.ppermute(x, "space", pairs)


def shards(
    ensemble,
    obs_value,
    obs_error,
    obs_cell,
    obs_species,
    patch_index,
    patch_count,
    courant_x,
    courant_y,
    dep_velocity,
    surface_factor,
):
    local, fields, tile_rows, columns = ensemble.shape
    levels = fields // dep_velocity.shape[0]
    n_obs = obs_cell.shape[1]
    per = patch_index.shape[1]
    maxobs = patch_index.shape[2]
    groups_mem = 8

    sizes = (8,)
    flat = ensemble.reshape(local * fields * tile_rows, columns)
    hbm = pl.BlockSpec(memory_space=pltpu.HBM)
    equiv = pl.pallas_call(
        equivalents_kernel,
        out_shape=jax.ShapeDtypeStruct((groups_mem, local, n_obs), F32),
        in_specs=[hbm] * 3,
        scratch_shapes=[
            pltpu.VMEM((local, fields // levels, tile_rows, columns), BF16),
            pltpu.VMEM((2, 1, n_obs), jnp.int32),
            pltpu.SemaphoreType.DMA((2 + local,)),
        ],
        compiler_params=pltpu.CompilerParams(vmem_limit_bytes=67000000),
        cost_estimate=cost(10**8),
    )(
        ensemble.reshape(local, fields // levels, levels, tile_rows, columns), obs_cell, obs_species
    )
    everywhere = lax.all_to_all(equiv, "mem", 0, 0, tiled=True)
    payload, info = call(
        payload_kernel,
        [
            jax.ShapeDtypeStruct((groups_mem, 320, 128), BF16),
            jax.ShapeDtypeStruct((16, n_obs), F32),
        ],
        [pltpu.VMEM(flat.shape, F32), pltpu.VMEM((2048, 128), F32), pltpu.VMEM((512, 128), F32)],
        flops=10**8,
    )(flat, obs_cell, obs_value, obs_error, courant_x, courant_y)
    packed = jnp.concatenate([everywhere.reshape(groups_mem * local, n_obs), info], axis=0)
    payload, packed, patch_index, patch_count = lax.optimization_barrier(
        (payload, packed, patch_index, patch_count)
    )
    near_a, near_b = swap(packed, 0), swap(packed, 1)
    state = lax.all_to_all(payload, "mem", 0, 0, tiled=True)
    odd = (lax.axis_index("space") % 2).reshape(1, 1)

    used = jnp.arange(maxobs, dtype=jnp.int32)[None, :] < patch_count[0][:, None]
    idx = jnp.where(used, patch_index[0], -1).reshape(1, per * maxobs)
    cell_id = lax.axis_index("mem") * per + jnp.arange(per, dtype=jnp.int32)
    cell_id = jnp.broadcast_to(cell_id[:, None], (per, maxobs)).reshape(1, per * maxobs)
    pos = jnp.concatenate([cell_id // columns, cell_id % columns], axis=0).astype(F32)

    smem = pl.BlockSpec(memory_space=pltpu.SMEM)
    groups = per // 4
    hi, lo = call(
        weights_kernel,
        [jax.ShapeDtypeStruct((groups, 64, 256), BF16)] * 2,
        [
            pltpu.VMEM((2 * groups, 64, 128), F32),
            pltpu.VMEM((2 * groups, 64, 128), F32),
            pltpu.VMEM((2 * groups, 64, 128), F32),
            pltpu.VMEM((2 * groups, 16, 128), F32),
            pltpu.VMEM((2 * groups, 8, 128), F32),
        ],
        flops=10**10,
        specs=[smem] + [VMEM] * 5,
    )(odd, near_a, packed, near_b, idx, pos)
    back = call(
        transform_kernel,
        [jax.ShapeDtypeStruct((groups_mem, local, 40, 128), BF16)],
        [pltpu.VMEM((2, 64 * per, 128), F32)],
        flops=10**9,
    )(hi, lo, state)[0]
    returned = lax.all_to_all(back, "mem", 0, 0, tiled=True)
    parts = call(
        relayout_kernel,
        [jax.ShapeDtypeStruct((tile_rows, n, fields, columns), BF16) for n in sizes],
        flops=10**8,
    )(returned)
    halos = [(swap(x, 0), swap(x, 1)) for x in parts]

    done, start = None, 0
    for n, x, (side_a, side_b) in zip(sizes, parts, halos):
        operands = [odd, side_a, x, side_b, near_a, packed, near_b]
        operands += [dep_velocity.reshape(1, -1), surface_factor]
        in_specs = [smem] + [VMEM] * 8
        if done is not None:
            operands.append(done)
            in_specs.append(hbm)
        span = n * fields * tile_rows
        done = pl.pallas_call(
            functools.partial(advect_kernel, start),
            out_shape=jax.ShapeDtypeStruct(flat.shape, BF16),
            in_specs=in_specs,
            out_specs=hbm,
            scratch_shapes=[
                pltpu.VMEM((tile_rows, fields, columns), F32),
                pltpu.VMEM((span, columns), F32),
                pltpu.VMEM((span, columns), BF16),
                pltpu.SemaphoreType.DMA((n,)),
            ],
            input_output_aliases={} if start == 0 else {9: 0},
            compiler_params=params(),
            cost_estimate=cost(10**9),
        )(*operands)
        start += n
    return done.reshape(local, fields, tile_rows, columns)


def solution(mesh):
    in_specs = (
        P("mem", None, "space", None),
        P("space", None),
        P("space", None),
        P("space", None),
        P("space", None),
        P("space", "mem", None),
        P("space", "mem"),
        P(None, "space", None),
        P(None, "space", None),
        P(),
        P("space", None),
    )
    out_specs = P("mem", None, "space", None)
    return jax.shard_map(shards, mesh=mesh, in_specs=in_specs, out_specs=out_specs, check_vma=False)
```

```python
import functools
import math

import jax
import jax.numpy as jnp
from jax import lax
from jax.experimental import pallas as pl
from jax.experimental.pallas import tpu as pltpu
from jax.sharding import PartitionSpec as P

NEWTON = 8
SUBSTEPS = 2
LOC = 1
F32 = jnp.float32
BF16 = jnp.bfloat16
VMEM = pl.BlockSpec(memory_space=pltpu.VMEM)


def iota(shape, dim):
    return lax.broadcasted_iota(jnp.int32, shape, dim)


def split2(x):
    hi = x.astype(BF16)
    return hi, (x - hi.astype(F32)).astype(BF16)


def split3(x):
    hi = x.astype(BF16).astype(F32)
    mid = (x - hi).astype(BF16).astype(F32)
    return hi, mid, x - hi - mid


def mm(a, b):
    return jnp.dot(a, b, preferred_element_type=F32)


def mm_nt(a, b):
    return lax.dot_general(a, b, (((1,), (1,)), ((), ())), preferred_element_type=F32)


def block_rows(x, width):
    lane = iota(x.shape, 1) // width
    zero = jnp.zeros_like(x)
    return jnp.concatenate(
        [jnp.where(lane == b, x, zero) for b in range(x.shape[1] // width)], axis=0
    )


def product(a2, b2, dot=mm):
    rows = a2[0].shape[0]
    first = dot(jnp.concatenate(a2, axis=0), b2[0])
    return first[:rows] + first[rows:] + dot(a2[0], b2[1])


def blocks2(x, width):
    hi, lo = split2(x)
    return block_rows(hi, width), block_rows(lo, width)


def side_by_side(x):
    return jnp.concatenate(split2(x), axis=1)


def paired(x, masks):
    cols = [jnp.concatenate([part * masks[0], part * masks[1]], axis=0) for part in split2(x)]
    once = jnp.concatenate(cols, axis=1)
    return jnp.concatenate([once, once], axis=0)


def pair_product(a, b):
    out = mm(a, b)
    return out[:, :128] + out[:, 128:]


def by_parity(is_odd, a, b):
    return jnp.where(is_odd, a, b), jnp.where(is_odd, b, a)


def weights_kernel(odd, near_a, own, near_b, idx_ref, pos_ref, hi_ref, lo_ref, t_ref, z_ref, m_ref, q_ref, tr_ref):
    members, maxobs = 64, 32
    pairs = t_ref.shape[0]
    is_odd = odd[0, 0] == 1
    low, high = by_parity(is_odd, near_a[...], near_b[...])
    parts = [low, own[...], high]
    equiv = jnp.concatenate([p[:members] for p in parts], axis=1)
    info = jnp.concatenate([p[members : members + 8] for p in parts], axis=1)
    n_obs = info.shape[1]
    tile = n_obs // 3
    row_obs = info[2:3] + ((iota((1, n_obs), 1) // tile).astype(F32) - 1.0) * 2.0
    sub = iota((8, n_obs), 0)
    rows = [*split3(info[0:1]), *split3(info[1:2]), row_obs, info[3:4]]
    table = jnp.zeros((8, n_obs), F32)
    for r, line in enumerate(rows):
        table = jnp.where(sub == r, line, table)
    lhs = jnp.concatenate([equiv, table, jnp.zeros((8, n_obs), F32)], axis=0).astype(BF16)

    eye = (iota((members, 128), 0) == iota((members, 128), 1) % 64).astype(F32)
    eye2 = jnp.concatenate([eye, eye], axis=1)
    spread = (iota((128, 256), 0) // maxobs == iota((128, 256), 1) // 64).astype(BF16)
    lane = iota((members, 128), 1)
    masks = [(lane < 64).astype(F32).astype(BF16), (lane >= 64).astype(F32).astype(BF16)]
    quarters = range(pairs // 4)
    sls = [slice(n * 256, n * 256 + 256) for n in quarters]
    gots = []
    for sl in sls:
        onehot = (iota((n_obs, 256), 0) == idx_ref[:, sl]).astype(F32).astype(BF16)
        gots.append(mm(lhs, onehot))
    grams = []
    for sl, got in zip(sls, gots):
        raw = got[:members]
        mean = jnp.sum(raw, axis=0, keepdims=True) * (1.0 / members)
        dev = raw - mean
        value = got[64:65] + got[65:66] + got[66:67]
        error = got[67:68] + got[68:69] + got[69:70]
        active = idx_ref[:, sl] >= 0
        d2 = (got[70:71] - pos_ref[0:1, sl]) ** 2 + (got[71:72] - pos_ref[1:2, sl]) ** 2
        rho = jnp.where(
            active, jnp.exp(-d2 / (2.0 * LOC * LOC)) / jnp.where(active, error, 1.0), 0.0
        )
        scaled = dev * rho
        pull = rho * (value - mean)
        power = jnp.sum(dev * scaled, axis=0, keepdims=True)
        for part in range(2):
            gs = slice(part * 128, part * 128 + 128)
            lhs_g = jnp.concatenate(
                [scaled[:, gs], jnp.broadcast_to(pull[:, gs], (16, 128))], axis=0
            )
            both = product(split2(lhs_g), blocks2(dev[:, gs], maxobs), mm_nt)
            sub16 = iota((16, 128), 0)
            p_hi, p_mid, p_lo = split3(power[:, gs])
            power3 = jnp.where(
                sub16 == 0, p_hi, jnp.where(sub16 == 1, p_mid, jnp.where(sub16 == 2, p_lo, 0.0))
            )
            grams.append((both, mm(power3.astype(BF16), spread)))
    for g, (both, powers) in enumerate(grams):
        trace = (members - 1.0) * members + jnp.sum(powers, axis=0, keepdims=True)
        pmat = (both[:members] + (members - 1.0) * eye2) * (1.0 / trace)
        for k in range(2):
            ks = slice(k * 128, k * 128 + 128)
            p = g * 2 + k
            t_ref[p] = pmat[:, ks]
            q_ref[p] = both[members : members + 16, ks]
            tr_ref[p] = jnp.broadcast_to(trace[:, ks], (8, 128))
    for p in range(pairs):
        middle = 1.5 * eye - 0.5 * t_ref[p]
        rows_m = jnp.concatenate([middle, q_ref[p]], axis=0)
        out = pair_product(side_by_side(rows_m), paired(middle, masks))
        z_ref[p] = middle
        q_ref[p] = out[members:]
        m_ref[p] = out[:members]
    for p in range(pairs):
        t_ref[p] = pair_product(side_by_side(t_ref[p]), paired(m_ref[p], masks))

    def step(_, carry):
        for p in range(pairs):
            middle = 1.5 * eye - 0.5 * t_ref[p]
            rows_m = jnp.concatenate([middle, z_ref[p], q_ref[p]], axis=0)
            out = pair_product(side_by_side(rows_m), paired(middle, masks))
            m_ref[p] = out[:members]
            z_ref[p] = out[members : 2 * members]
            q_ref[p] = out[2 * members :]
        for p in range(pairs):
            t_ref[p] = pair_product(side_by_side(t_ref[p]), paired(m_ref[p], masks))
        return carry

    lax.fori_loop(0, NEWTON - 2, step, 0)
    for p in range(pairs):
        middle = 1.5 * eye - 0.5 * t_ref[p]
        rows_z = jnp.concatenate([z_ref[p], q_ref[p]], axis=0)
        out = pair_product(side_by_side(rows_z), paired(middle, masks))
        z_ref[p] = out[:members]
        q_ref[p] = out[members:]
    for p in range(pairs):
        root = z_ref[p]
        trace = tr_ref[p][:1]
        pulled = pair_product(side_by_side(q_ref[p]), paired(root, masks))[:1] / trace
        scale = math.sqrt(members - 1.0) / jnp.sqrt(trace)
        p0 = (members - 1.0) / trace
        z0 = jnp.ones_like(p0)
        for _ in range(NEWTON):
            m0 = 1.5 - 0.5 * z0 * p0
            p0 = p0 * m0
            z0 = m0 * z0
        full = scale * root + (pulled + (1.0 - scale * z0) * (1.0 / members))
        hi, lo = split2(full)
        ks = slice((p % 2) * 128, (p % 2) * 128 + 128)
        hi_ref[p // 2, :, ks] = hi
        lo_ref[p // 2, :, ks] = lo


def equivalents_kernel(ens, cell, kind, o_ref, held, picks, sems):
    species, n_obs = ens.shape[1], cell.shape[1]
    jobs = [(cell, picks.at[0]), (kind, picks.at[1])]
    jobs += [(ens.at[m, :, 0], held.at[m]) for m in range(8)]
    copies = [pltpu.make_async_copy(src, dst, sems.at[n]) for n, (src, dst) in enumerate(jobs)]
    for copy in copies:
        copy.start()
    copies[0].wait()
    copies[1].wait()
    cells = picks[0]
    row = (cells >= 128).astype(jnp.int32)
    pick = (iota((128, n_obs), 0) == cells - 128 * row).astype(F32).astype(BF16)
    wanted = iota((2 * species, n_obs), 0) == picks[1] * 2 + row
    rows = []
    for m in range(0, 8, 2):
        copies[2 + m].wait()
        copies[3 + m].wait()
        found = [mm(held[m + k].reshape(2 * species, 128), pick) for k in range(2)]
        rows += [jnp.sum(jnp.where(wanted, x, 0.0), axis=0, keepdims=True) for x in found]
    full = jnp.concatenate(rows, axis=0)
    for d in range(o_ref.shape[0]):
        o_ref[d] = full


def payload_kernel(ens, cell, value, error, wind_x, wind_y, o_ref, info, flat, main, rest):
    local = 8
    fields = ens.shape[0] // (2 * local)
    ident = (iota((128, 128), 0) == iota((128, 128), 1)).astype(F32).astype(BF16)
    lane = iota((8, 128), 1) // 32
    flat[...] = ens[...].astype(F32)

    def turned(n):
        row, m = n // local, n % local
        x = flat[pl.ds(m * 2 * fields + row, fields, stride=2), :].astype(BF16)
        return mm_nt(ident, jnp.concatenate([x[:128]] + [x[128:]] * 4, axis=0))

    ahead = 3
    queue = [turned(n) for n in range(ahead)]
    for n in range(2 * local):
        row, m = n // local, n % local
        if n + ahead < 2 * local:
            queue.append(turned(n + ahead))
        out = queue.pop(0)
        main[pl.ds(row * 1024 + m, 128, stride=local), :] = out[:, :128]
        for q in range(4):
            tail = jnp.zeros((8, 128), F32)
            for cc in range(4):
                at = q * 32 + cc * 8
                tail = jnp.where(lane == cc, out[at : at + 8, 128:], tail)
            rest[pl.ds((row * 4 + q) * 64 + m, 8, stride=local), :] = tail
    for dest in range(8):
        o_ref[dest, :256] = main[dest * 256 : dest * 256 + 256, :].astype(BF16)
        o_ref[dest, 256:] = rest[dest * 64 : dest * 64 + 64, :].astype(BF16)
    cells = cell[...]
    n_obs = cells.shape[1]
    row = (cells >= 128).astype(jnp.int32)
    sub = iota((8, n_obs), 0)
    lines = [value[...], error[...], row.astype(F32), (cells - 128 * row).astype(F32)]
    top = jnp.zeros((8, n_obs), F32)
    for r, line in enumerate(lines):
        top = jnp.where(sub == r, line, top)
    info[:8] = top
    for axis, wind in enumerate((wind_x, wind_y)):
        for level in range(4):
            for half in range(2):
                info[8 + axis * 4 + level : 9 + axis * 4 + level, half * 128 : half * 128 + 128] = (
                    wind[level, half : half + 1]
                )


def transform_kernel(hi_ref, lo_ref, x_ref, *refs):
    outs, scr = refs[:-1], refs[-1]
    groups = hi_ref.shape[0]
    per = 32

    def members_of(base):
        x = x_ref[:, base : base + 16].astype(F32)
        return [x[:, k * 8 : k * 8 + 8].reshape(64, 128) for k in range(2)]

    lane64 = iota((64, 128), 1)
    masks = [(lane64 < 64).astype(F32).astype(BF16), (lane64 >= 64).astype(F32).astype(BF16)]

    def solved(p):
        ks = slice((p % 2) * 128, (p % 2) * 128 + 128)
        hi, lo = hi_ref[p // 2, :, ks], lo_ref[p // 2, :, ks]
        lhs = jnp.concatenate(
            [jnp.concatenate([hi * k, lo * k], axis=1) for k in masks], axis=0
        )
        x = jnp.concatenate(
            [
                jnp.concatenate(members_of(p * 16), axis=0),
                jnp.concatenate(members_of(256 + (p % 4) * 16), axis=0),
            ],
            axis=1,
        ).astype(BF16)
        return mm(lhs, jnp.concatenate([x, x], axis=0))

    ahead = 3
    count = 2 * groups
    results = {p: solved(p) for p in range(ahead)}
    for p in range(count):
        if p + ahead < count:
            results[p + ahead] = solved(p + ahead)
        out = results.pop(p)
        for c in range(2):
            val = out[c * 64 : c * 64 + 64]
            scr[0, pl.ds(p * 2 + c, 64, stride=per), :] = val[:, :128]
            scr[1, pl.ds(p * 2 + c, 64, stride=per), :] = val[:, 128:]
    lane = iota((8, 128), 1) // 32
    chunk = 8 // len(outs)
    for ml in range(8):
        for dest in range(8):
            base = (dest * 8 + ml) * per
            main = scr[0, base : base + per, :]
            rest = jnp.zeros((8, 128), F32)
            for cc in range(4):
                rest = jnp.where(lane == cc, scr[1, base + cc * 8 : base + cc * 8 + 8, :], rest)
            outs[ml // chunk][dest, ml % chunk] = jnp.concatenate(
                [main, rest, jnp.zeros_like(rest)], axis=0
            ).astype(BF16)[:40]


def relayout_kernel(x_ref, *outs):
    fields = outs[0].shape[2]
    places = [(o, k) for o in outs for k in range(o.shape[1])]
    f, at = iota((fields, 256), 0), iota((fields, 256), 1)
    ident = (((at < 128) & (f == at)) | ((at >= 128) & (f - 128 == at % 32))).astype(F32)
    ident = ident.astype(BF16)
    lane = iota((8, 128), 1) // 32
    for row in range(2):
        for ml in range(x_ref.shape[1]):
            mains, rests = [], []
            for q in range(4):
                block = x_ref[row * 4 + q, ml].astype(F32)
                mains.append(block[:32])
                rests += [jnp.where(lane == cc, block[32:40], 0.0) for cc in range(4)]
            full = jnp.concatenate(
                [jnp.concatenate(mains, axis=0), jnp.concatenate(rests, axis=0)], axis=1
            ).astype(BF16)
            out, k = places[ml]
            out[row, k] = mm_nt(ident, full).astype(BF16)


PART = 80


def scale(c, q):
    return (q.reshape(PART // 8, 8, 128) * c[None]).reshape(PART, 128)


def shift_matrix():
    source, to = iota((256, 256), 0) % 128, iota((256, 256), 1)
    west = (to < 128) & (source == to - 1)
    east = (to >= 128) & (source == to - 127)
    return (west | east).astype(F32).astype(BF16)


def columns_step(planes, winds, shift):
    both = mm(jnp.concatenate([side_by_side(q) for q in planes], axis=0), shift)
    outs = []
    for n, (q, (a, b, c)) in enumerate(zip(planes, winds)):
        near = both[n * PART : n * PART + PART]
        outs.append(scale(a, near[:, :128]) + scale(b, q) + scale(c, near[:, 128:]))
    return outs


def side_coeffs(is_high, own_wind, side_wind):
    lane = iota((8, 128), 1)

    def coeffs(c):
        c = jnp.concatenate([c, c], axis=0)
        half, sq = 0.5 * c, 0.5 * c * c
        return half + sq, 1.0 - c * c, sq - half

    result = []
    for wind, row_high in ((own_wind, 1), (side_wind, 0)):
        rows = (wind[:, :128], wind[:, 128:])
        w = jnp.where(is_high, rows[row_high], rows[1 - row_high])
        south, mid, north = coeffs(w[4:8])
        along_rows = (jnp.where(is_high, south, north), mid, jnp.where(is_high, north, south))
        west, mid, east = coeffs(w[:4])
        along_cols = (jnp.where(lane == 0, 0.0, west), mid, jnp.where(lane == 127, 0.0, east))
        result.append((along_rows, along_cols))
    return result


def rows_step(inner, mid, outer, c):
    return scale(c[0], inner) + scale(c[1], mid) + scale(c[2], outer)


def side_rows(is_high, side_ref, own_ref, m, f, coeffs):
    load = lambda ref, k: ref[k, m, f : f + PART]
    near, far = by_parity(is_high, load(side_ref, 0), load(side_ref, 1))
    close, other = by_parity(is_high, load(own_ref, 1), load(own_ref, 0))
    near, far, close, other = [x.astype(F32) for x in (near, far, close, other)]
    return [
        rows_step(other, close, near, coeffs[0][0]),
        rows_step(close, near, far, coeffs[1][0]),
    ]


def all_units(own_ref):
    return [(m, f) for m in range(own_ref.shape[1]) for f in range(0, own_ref.shape[2], PART)]


def first_side_kernel(odd, side_ref, own_ref, side_wind, own_wind, o_ref):
    is_high = odd[0, 0] == 1
    coeffs = side_coeffs(is_high, own_wind[72:80], side_wind[72:80])
    shift = shift_matrix()
    for m, f in all_units(own_ref):
        planes = side_rows(is_high, side_ref, own_ref, m, f, coeffs)
        outs = columns_step(planes, [c[1] for c in coeffs], shift)
        o_ref[0, m, f : f + PART] = outs[0]
        o_ref[1, m, f : f + PART] = outs[1]


def advect_kernel(odd, a_ref, own_ref, b_mid, ca_ref, co_ref, cb_ref, dep_ref, surf_ref, *refs):
    o_ref, fac, flat, ready, sems = refs
    members, fields = own_ref.shape[1], own_ref.shape[2]
    span = 2 * fields
    is_odd = odd[0, 0] == 1
    coeffs_a = side_coeffs(jnp.logical_not(is_odd), co_ref[72:80], ca_ref[72:80])
    coeffs_b = side_coeffs(is_odd, co_ref[72:80], cb_ref[72:80])
    shift = shift_matrix()
    own_level = iota((fields, dep_ref.shape[1]), 0) == 4 * iota((fields, dep_ref.shape[1]), 1)
    rate = jnp.sum(jnp.where(own_level, dep_ref[...], 0.0), axis=1, keepdims=True)
    for row in range(2):
        fac[row] = jnp.exp(-rate * surf_ref[row : row + 1, :])
    units = all_units(own_ref)

    def first(m, f):
        high = jnp.logical_not(is_odd)
        planes = side_rows(high, a_ref, own_ref, m, f, coeffs_a)
        return columns_step(planes, [c[1] for c in coeffs_a], shift)

    ahead = 2
    mids = {u: first(*units[u]) for u in range(ahead)}
    copies = []
    for u, (m, f) in enumerate(units):
        if u + ahead < len(units):
            mids[u + ahead] = first(*units[u + ahead])
        own_a, out_a = mids.pop(u)
        own_b, out_b = b_mid[0, m, f : f + PART], b_mid[1, m, f : f + PART]
        planes = [
            rows_step(own_b, own_a, out_a, coeffs_a[0][0]),
            rows_step(own_a, own_b, out_b, coeffs_b[0][0]),
        ]
        ends = by_parity(is_odd, *columns_step(planes, [coeffs_a[0][1], coeffs_b[0][1]], shift))
        base = m * span + 2 * f
        for r in range(2):
            flat[pl.ds(base + r, PART, stride=2), :] = ends[r] * fac[r, f : f + PART]
        ready[base : base + 2 * PART] = flat[base : base + 2 * PART, :].astype(BF16)
        if f + PART == fields:
            rows = pl.ds(m * span, span)
            copy = pltpu.make_async_copy(ready.at[rows], o_ref.at[rows], sems.at[m])
            copy.start()
            copies.append(copy)
    for copy in copies:
        copy.wait()


def params():
    return pltpu.CompilerParams(vmem_limit_bytes=40 << 20)


def cost(flops):
    return pl.CostEstimate(flops=flops, bytes_accessed=10**6, transcendentals=0)


def call(kernel, outs, scratch=(), flops=10**8, specs=None):
    return pl.pallas_call(
        kernel,
        out_shape=outs,
        **({} if specs is None else {"in_specs": specs}),
        scratch_shapes=list(scratch),
        compiler_params=params(),
        cost_estimate=cost(flops),
    )


def swap(x, first):
    pairs = []
    for low in range(first, lax.axis_size("space") - 1, 2):
        pairs += [(low, low + 1), (low + 1, low)]
    return lax.ppermute(x, "space", pairs)


def shards(
    ensemble,
    obs_value,
    obs_error,
    obs_cell,
    obs_species,
    patch_index,
    patch_count,
    courant_x,
    courant_y,
    dep_velocity,
    surface_factor,
):
    local, fields, tile_rows, columns = ensemble.shape
    levels = fields // dep_velocity.shape[0]
    n_obs = obs_cell.shape[1]
    per = patch_index.shape[1]
    maxobs = patch_index.shape[2]
    groups_mem = 8

    flat = ensemble.reshape(local * fields * tile_rows, columns)
    hbm = pl.BlockSpec(memory_space=pltpu.HBM)
    equiv = pl.pallas_call(
        equivalents_kernel,
        out_shape=jax.ShapeDtypeStruct((groups_mem, local, n_obs), F32),
        in_specs=[hbm] * 3,
        scratch_shapes=[
            pltpu.VMEM((local, fields // levels, tile_rows, columns), BF16),
            pltpu.VMEM((2, 1, n_obs), jnp.int32),
            pltpu.SemaphoreType.DMA((2 + local,)),
        ],
        compiler_params=pltpu.CompilerParams(vmem_limit_bytes=67000000),
        cost_estimate=cost(10**8),
    )(
        ensemble.reshape(local, fields // levels, levels, tile_rows, columns), obs_cell, obs_species
    )
    everywhere = lax.all_to_all(equiv, "mem", 0, 0, tiled=True)
    payload, info = call(
        payload_kernel,
        [
            jax.ShapeDtypeStruct((groups_mem, 320, 128), BF16),
            jax.ShapeDtypeStruct((16, n_obs), F32),
        ],
        [pltpu.VMEM(flat.shape, F32), pltpu.VMEM((2048, 128), F32), pltpu.VMEM((512, 128), F32)],
        flops=10**8,
    )(flat, obs_cell, obs_value, obs_error, courant_x, courant_y)
    packed = jnp.concatenate([everywhere.reshape(groups_mem * local, n_obs), info], axis=0)
    payload, packed, patch_index, patch_count = lax.optimization_barrier(
        (payload, packed, patch_index, patch_count)
    )
    near_a, near_b = swap(packed, 0), swap(packed, 1)
    state = lax.all_to_all(payload, "mem", 0, 0, tiled=True)
    odd = (lax.axis_index("space") % 2).reshape(1, 1)

    used = jnp.arange(maxobs, dtype=jnp.int32)[None, :] < patch_count[0][:, None]
    idx = jnp.where(used, patch_index[0], -1).reshape(1, per * maxobs)
    cell_id = lax.axis_index("mem") * per + jnp.arange(per, dtype=jnp.int32)
    cell_id = jnp.broadcast_to(cell_id[:, None], (per, maxobs)).reshape(1, per * maxobs)
    pos = jnp.concatenate([cell_id // columns, cell_id % columns], axis=0).astype(F32)

    smem = pl.BlockSpec(memory_space=pltpu.SMEM)
    groups = per // 4
    hi, lo = call(
        weights_kernel,
        [jax.ShapeDtypeStruct((groups, 64, 256), BF16)] * 2,
        [
            pltpu.VMEM((2 * groups, 64, 128), F32),
            pltpu.VMEM((2 * groups, 64, 128), F32),
            pltpu.VMEM((2 * groups, 64, 128), F32),
            pltpu.VMEM((2 * groups, 16, 128), F32),
            pltpu.VMEM((2 * groups, 8, 128), F32),
        ],
        flops=10**10,
        specs=[smem] + [VMEM] * 5,
    )(odd, near_a, packed, near_b, idx, pos)
    back = call(
        transform_kernel,
        [jax.ShapeDtypeStruct((groups_mem, local, 40, 128), BF16)],
        [pltpu.VMEM((2, 64 * per, 128), F32)],
        flops=10**9,
    )(hi, lo, state)[0]
    returned = lax.all_to_all(back, "mem", 0, 0, tiled=True)
    plane_shape = (tile_rows, local, fields, columns)
    planes = call(
        relayout_kernel, [jax.ShapeDtypeStruct(plane_shape, BF16)], flops=10**8
    )(returned)[0]
    side_b = swap(planes, 1)
    side_a = swap(planes, 0)
    b_mid = call(
        first_side_kernel,
        jax.ShapeDtypeStruct(plane_shape, F32),
        flops=10**8,
        specs=[smem] + [VMEM] * 4,
    )(odd, side_b, planes, near_b, packed)
    done = pl.pallas_call(
        advect_kernel,
        out_shape=jax.ShapeDtypeStruct(flat.shape, BF16),
        in_specs=[smem] + [VMEM] * 8,
        out_specs=hbm,
        scratch_shapes=[
            pltpu.VMEM((tile_rows, fields, columns), F32),
            pltpu.VMEM(flat.shape, F32),
            pltpu.VMEM(flat.shape, BF16),
            pltpu.SemaphoreType.DMA((local,)),
        ],
        compiler_params=params(),
        cost_estimate=cost(10**9),
    )(
        odd, side_a, planes, b_mid, near_a, packed, near_b,
        dep_velocity.reshape(1, -1), surface_factor,
    )
    return done.reshape(local, fields, tile_rows, columns)


def solution(mesh):
    in_specs = (
        P("mem", None, "space", None),
        P("space", None),
        P("space", None),
        P("space", None),
        P("space", None),
        P("space", "mem", None),
        P("space", "mem"),
        P(None, "space", None),
        P(None, "space", None),
        P(),
        P("space", None),
    )
    out_specs = P("mem", None, "space", None)
    return jax.shard_map(shards, mesh=mesh, in_specs=in_specs, out_specs=out_specs, check_vma=False)
```

```python
import functools
import math

import jax
import jax.numpy as jnp
from jax import lax
from jax.experimental import pallas as pl
from jax.experimental.pallas import tpu as pltpu
from jax.sharding import PartitionSpec as P

NEWTON = 8
SUBSTEPS = 2
LOC = 1
F32 = jnp.float32
BF16 = jnp.bfloat16
VMEM = pl.BlockSpec(memory_space=pltpu.VMEM)


def iota(shape, dim):
    return lax.broadcasted_iota(jnp.int32, shape, dim)


def split2(x):
    hi = x.astype(BF16)
    return hi, (x - hi.astype(F32)).astype(BF16)


def split3(x):
    hi = x.astype(BF16).astype(F32)
    mid = (x - hi).astype(BF16).astype(F32)
    return hi, mid, x - hi - mid


def mm(a, b):
    return jnp.dot(a, b, preferred_element_type=F32)


def mm_nt(a, b):
    return lax.dot_general(a, b, (((1,), (1,)), ((), ())), preferred_element_type=F32)


def block_rows(x, width):
    lane = iota(x.shape, 1) // width
    zero = jnp.zeros_like(x)
    return jnp.concatenate(
        [jnp.where(lane == b, x, zero) for b in range(x.shape[1] // width)], axis=0
    )


def product(a2, b2, dot=mm):
    rows = a2[0].shape[0]
    first = dot(jnp.concatenate(a2, axis=0), b2[0])
    return first[:rows] + first[rows:] + dot(a2[0], b2[1])


def blocks2(x, width):
    hi, lo = split2(x)
    return block_rows(hi, width), block_rows(lo, width)


def side_by_side(x):
    return jnp.concatenate(split2(x), axis=1)


def paired(x, masks):
    cols = [jnp.concatenate([part * masks[0], part * masks[1]], axis=0) for part in split2(x)]
    once = jnp.concatenate(cols, axis=1)
    return jnp.concatenate([once, once], axis=0)


def pair_product(a, b):
    out = mm(a, b)
    return out[:, :128] + out[:, 128:]


def by_parity(is_odd, a, b):
    return jnp.where(is_odd, a, b), jnp.where(is_odd, b, a)


def weights_kernel(odd, near_a, own, near_b, idx_ref, pos_ref, hi_ref, lo_ref, t_ref, z_ref, m_ref, q_ref, tr_ref):
    members, maxobs = 64, 32
    pairs = t_ref.shape[0]
    is_odd = odd[0, 0] == 1
    low, high = by_parity(is_odd, near_a[...], near_b[...])
    parts = [low, own[...], high]
    equiv = jnp.concatenate([p[:members] for p in parts], axis=1)
    info = jnp.concatenate([p[members : members + 8] for p in parts], axis=1)
    n_obs = info.shape[1]
    tile = n_obs // 3
    row_obs = info[2:3] + ((iota((1, n_obs), 1) // tile).astype(F32) - 1.0) * 2.0
    sub = iota((8, n_obs), 0)
    rows = [*split3(info[0:1]), *split3(info[1:2]), row_obs, info[3:4]]
    table = jnp.zeros((8, n_obs), F32)
    for r, line in enumerate(rows):
        table = jnp.where(sub == r, line, table)
    lhs = jnp.concatenate([equiv, table, jnp.zeros((8, n_obs), F32)], axis=0).astype(BF16)

    eye = (iota((members, 128), 0) == iota((members, 128), 1) % 64).astype(F32)
    eye2 = jnp.concatenate([eye, eye], axis=1)
    spread = (iota((128, 256), 0) // maxobs == iota((128, 256), 1) // 64).astype(BF16)
    lane = iota((members, 128), 1)
    masks = [(lane < 64).astype(F32).astype(BF16), (lane >= 64).astype(F32).astype(BF16)]
    quarters = range(pairs // 4)
    sls = [slice(n * 256, n * 256 + 256) for n in quarters]
    gots = []
    for sl in sls:
        onehot = (iota((n_obs, 256), 0) == idx_ref[:, sl]).astype(F32).astype(BF16)
        gots.append(mm(lhs, onehot))
    grams = []
    for sl, got in zip(sls, gots):
        raw = got[:members]
        mean = jnp.sum(raw, axis=0, keepdims=True) * (1.0 / members)
        dev = raw - mean
        value = got[64:65] + got[65:66] + got[66:67]
        error = got[67:68] + got[68:69] + got[69:70]
        active = idx_ref[:, sl] >= 0
        d2 = (got[70:71] - pos_ref[0:1, sl]) ** 2 + (got[71:72] - pos_ref[1:2, sl]) ** 2
        rho = jnp.where(
            active, jnp.exp(-d2 / (2.0 * LOC * LOC)) / jnp.where(active, error, 1.0), 0.0
        )
        scaled = dev * rho
        pull = rho * (value - mean)
        power = jnp.sum(dev * scaled, axis=0, keepdims=True)
        for part in range(2):
            gs = slice(part * 128, part * 128 + 128)
            lhs_g = jnp.concatenate(
                [scaled[:, gs], jnp.broadcast_to(pull[:, gs], (16, 128))], axis=0
            )
            both = product(split2(lhs_g), blocks2(dev[:, gs], maxobs), mm_nt)
            sub16 = iota((16, 128), 0)
            p_hi, p_mid, p_lo = split3(power[:, gs])
            power3 = jnp.where(
                sub16 == 0, p_hi, jnp.where(sub16 == 1, p_mid, jnp.where(sub16 == 2, p_lo, 0.0))
            )
            grams.append((both, mm(power3.astype(BF16), spread)))
    for g, (both, powers) in enumerate(grams):
        trace = (members - 1.0) * members + jnp.sum(powers, axis=0, keepdims=True)
        pmat = (both[:members] + (members - 1.0) * eye2) * (1.0 / trace)
        for k in range(2):
            ks = slice(k * 128, k * 128 + 128)
            p = g * 2 + k
            t_ref[p] = pmat[:, ks]
            q_ref[p] = both[members : members + 16, ks]
            tr_ref[p] = jnp.broadcast_to(trace[:, ks], (8, 128))
    for p in range(pairs):
        middle = 1.5 * eye - 0.5 * t_ref[p]
        rows_m = jnp.concatenate([middle, q_ref[p]], axis=0)
        out = pair_product(side_by_side(rows_m), paired(middle, masks))
        z_ref[p] = middle
        q_ref[p] = out[members:]
        m_ref[p] = out[:members]
    for p in range(pairs):
        t_ref[p] = pair_product(side_by_side(t_ref[p]), paired(m_ref[p], masks))

    def step(_, carry):
        for p in range(pairs):
            middle = 1.5 * eye - 0.5 * t_ref[p]
            rows_m = jnp.concatenate([middle, z_ref[p], q_ref[p]], axis=0)
            out = pair_product(side_by_side(rows_m), paired(middle, masks))
            m_ref[p] = out[:members]
            z_ref[p] = out[members : 2 * members]
            q_ref[p] = out[2 * members :]
        for p in range(pairs):
            t_ref[p] = pair_product(side_by_side(t_ref[p]), paired(m_ref[p], masks))
        return carry

    lax.fori_loop(0, NEWTON - 2, step, 0)
    for p in range(pairs):
        middle = 1.5 * eye - 0.5 * t_ref[p]
        rows_z = jnp.concatenate([z_ref[p], q_ref[p]], axis=0)
        out = pair_product(side_by_side(rows_z), paired(middle, masks))
        z_ref[p] = out[:members]
        q_ref[p] = out[members:]
    for p in range(pairs):
        root = z_ref[p]
        trace = tr_ref[p][:1]
        pulled = pair_product(side_by_side(q_ref[p]), paired(root, masks))[:1] / trace
        scale = math.sqrt(members - 1.0) / jnp.sqrt(trace)
        p0 = (members - 1.0) / trace
        z0 = jnp.ones_like(p0)
        for _ in range(NEWTON):
            m0 = 1.5 - 0.5 * z0 * p0
            p0 = p0 * m0
            z0 = m0 * z0
        full = scale * root + (pulled + (1.0 - scale * z0) * (1.0 / members))
        hi, lo = split2(full)
        ks = slice((p % 2) * 128, (p % 2) * 128 + 128)
        hi_ref[p // 2, :, ks] = hi
        lo_ref[p // 2, :, ks] = lo


def equivalents_kernel(ens, cell, kind, o_ref, held, picks, sems):
    species, n_obs = ens.shape[1], cell.shape[1]
    jobs = [(cell, picks.at[0]), (kind, picks.at[1])]
    jobs += [(ens.at[m, :, 0], held.at[m]) for m in range(8)]
    copies = [pltpu.make_async_copy(src, dst, sems.at[n]) for n, (src, dst) in enumerate(jobs)]
    for copy in copies:
        copy.start()
    copies[0].wait()
    copies[1].wait()
    cells = picks[0]
    row = (cells >= 128).astype(jnp.int32)
    pick = (iota((128, n_obs), 0) == cells - 128 * row).astype(F32).astype(BF16)
    wanted = iota((2 * species, n_obs), 0) == picks[1] * 2 + row
    rows = []
    for m in range(0, 8, 2):
        copies[2 + m].wait()
        copies[3 + m].wait()
        found = [mm(held[m + k].reshape(2 * species, 128), pick) for k in range(2)]
        rows += [jnp.sum(jnp.where(wanted, x, 0.0), axis=0, keepdims=True) for x in found]
    full = jnp.concatenate(rows, axis=0)
    for d in range(o_ref.shape[0]):
        o_ref[d] = full


def payload_kernel(ens, cell, value, error, wind_x, wind_y, o_ref, info, flat, main, rest):
    local = 8
    fields = ens.shape[0] // (2 * local)
    ident = (iota((128, 128), 0) == iota((128, 128), 1)).astype(F32).astype(BF16)
    lane = iota((8, 128), 1) // 32
    flat[...] = ens[...].astype(F32)

    def turned(n):
        row, m = n // local, n % local
        x = flat[pl.ds(m * 2 * fields + row, fields, stride=2), :].astype(BF16)
        return mm_nt(ident, jnp.concatenate([x[:128]] + [x[128:]] * 4, axis=0))

    ahead = 3
    queue = [turned(n) for n in range(ahead)]
    for n in range(2 * local):
        row, m = n // local, n % local
        if n + ahead < 2 * local:
            queue.append(turned(n + ahead))
        out = queue.pop(0)
        main[pl.ds(row * 1024 + m, 128, stride=local), :] = out[:, :128]
        for q in range(4):
            tail = jnp.zeros((8, 128), F32)
            for cc in range(4):
                at = q * 32 + cc * 8
                tail = jnp.where(lane == cc, out[at : at + 8, 128:], tail)
            rest[pl.ds((row * 4 + q) * 64 + m, 8, stride=local), :] = tail
    for dest in range(8):
        o_ref[dest, :256] = main[dest * 256 : dest * 256 + 256, :].astype(BF16)
        o_ref[dest, 256:] = rest[dest * 64 : dest * 64 + 64, :].astype(BF16)
    cells = cell[...]
    n_obs = cells.shape[1]
    row = (cells >= 128).astype(jnp.int32)
    sub = iota((8, n_obs), 0)
    lines = [value[...], error[...], row.astype(F32), (cells - 128 * row).astype(F32)]
    top = jnp.zeros((8, n_obs), F32)
    for r, line in enumerate(lines):
        top = jnp.where(sub == r, line, top)
    info[:8] = top
    for axis, wind in enumerate((wind_x, wind_y)):
        for level in range(4):
            for half in range(2):
                info[8 + axis * 4 + level : 9 + axis * 4 + level, half * 128 : half * 128 + 128] = (
                    wind[level, half : half + 1]
                )


def transform_kernel(hi_ref, lo_ref, x_ref, *refs):
    outs, scr = refs[:-1], refs[-1]
    groups = hi_ref.shape[0]
    per = 32

    def members_of(base):
        x = x_ref[:, base : base + 16].astype(F32)
        return [x[:, k * 8 : k * 8 + 8].reshape(64, 128) for k in range(2)]

    lane64 = iota((64, 128), 1)
    masks = [(lane64 < 64).astype(F32).astype(BF16), (lane64 >= 64).astype(F32).astype(BF16)]

    def solved(p):
        ks = slice((p % 2) * 128, (p % 2) * 128 + 128)
        hi, lo = hi_ref[p // 2, :, ks], lo_ref[p // 2, :, ks]
        lhs = jnp.concatenate(
            [jnp.concatenate([hi * k, lo * k], axis=1) for k in masks], axis=0
        )
        x = jnp.concatenate(
            [
                jnp.concatenate(members_of(p * 16), axis=0),
                jnp.concatenate(members_of(256 + (p % 4) * 16), axis=0),
            ],
            axis=1,
        ).astype(BF16)
        return mm(lhs, jnp.concatenate([x, x], axis=0))

    ahead = 3
    count = 2 * groups
    results = {p: solved(p) for p in range(ahead)}
    for p in range(count):
        if p + ahead < count:
            results[p + ahead] = solved(p + ahead)
        out = results.pop(p)
        for c in range(2):
            val = out[c * 64 : c * 64 + 64]
            scr[0, pl.ds(p * 2 + c, 64, stride=per), :] = val[:, :128]
            scr[1, pl.ds(p * 2 + c, 64, stride=per), :] = val[:, 128:]
    lane = iota((8, 128), 1) // 32
    chunk = 8 // len(outs)
    for ml in range(8):
        for dest in range(8):
            base = (dest * 8 + ml) * per
            main = scr[0, base : base + per, :]
            rest = jnp.zeros((8, 128), F32)
            for cc in range(4):
                rest = jnp.where(lane == cc, scr[1, base + cc * 8 : base + cc * 8 + 8, :], rest)
            outs[ml // chunk][dest, ml % chunk] = jnp.concatenate(
                [main, rest, jnp.zeros_like(rest)], axis=0
            ).astype(BF16)[:40]


def relayout_kernel(x_ref, *outs):
    fields = outs[0].shape[2]
    places = [(o, k) for o in outs for k in range(o.shape[1])]
    f, at = iota((fields, 256), 0), iota((fields, 256), 1)
    ident = (((at < 128) & (f == at)) | ((at >= 128) & (f - 128 == at % 32))).astype(F32)
    ident = ident.astype(BF16)
    lane = iota((8, 128), 1) // 32
    for row in range(2):
        for ml in range(x_ref.shape[1]):
            mains, rests = [], []
            for q in range(4):
                block = x_ref[row * 4 + q, ml].astype(F32)
                mains.append(block[:32])
                rests += [jnp.where(lane == cc, block[32:40], 0.0) for cc in range(4)]
            full = jnp.concatenate(
                [jnp.concatenate(mains, axis=0), jnp.concatenate(rests, axis=0)], axis=1
            ).astype(BF16)
            out, k = places[ml]
            out[row, k] = mm_nt(ident, full).astype(BF16)


def advect_kernel(start, odd, a_ref, own_ref, b_ref, ca_ref, co_ref, cb_ref, dep_ref, surf_ref, *refs):
    o_ref, fac, flat, ready, sems = refs[-5:]
    fields = own_ref.shape[2]
    is_odd = odd[0, 0] == 1
    lane = iota((8, 128), 1)
    wind_low, wind_high = by_parity(is_odd, ca_ref[72:80], cb_ref[72:80])
    wind_own = co_ref[72:80]

    def coeffs(wind, axis, row):
        c = wind[axis * 4 : axis * 4 + 4, row * 128 : row * 128 + 128]
        c = jnp.concatenate([c, c], axis=0)
        half, sq = 0.5 * c, 0.5 * c * c
        return half + sq, 1.0 - c * c, sq - half

    courant = [(wind_low, 1), (wind_own, 0), (wind_own, 1), (wind_high, 0)]
    cy = [coeffs(w, 1, k) for w, k in courant]
    cx = []
    for w, k in courant:
        a, b, c = coeffs(w, 0, k)
        cx.append((jnp.where(lane == 0, 0.0, a), b, jnp.where(lane == 127, 0.0, c)))

    own_level = iota((fields, dep_ref.shape[1]), 0) == 4 * iota((fields, dep_ref.shape[1]), 1)
    rate = jnp.sum(jnp.where(own_level, dep_ref[...], 0.0), axis=1, keepdims=True)
    for row in range(2):
        fac[row] = jnp.exp(-rate * surf_ref[row : row + 1, :])

    shift_in, shift_out = iota((256, 256), 0) % 128, iota((256, 256), 1)
    shift = (
        ((shift_out < 128) & (shift_in == shift_out - 1))
        | ((shift_out >= 128) & (shift_in == shift_out - 127))
    ).astype(F32).astype(BF16)
    part = 160

    def scale(c, q):
        return (q.reshape(part // 8, 8, 128) * c[None]).reshape(part, 128)

    def rows(south, mid, north, k):
        a, b, c = cy[k]
        return scale(a, south) + scale(b, mid) + scale(c, north)

    def cols(planes, first):
        both = mm(
            jnp.concatenate([jnp.concatenate(split2(q), axis=1) for q in planes], axis=0), shift
        )
        outs = []
        for n, q in enumerate(planes):
            a, b, c = cx[first + n]
            near = both[n * part : n * part + part]
            outs.append(scale(a, near[:, :128]) + scale(b, q) + scale(c, near[:, 128:]))
        return outs

    members, span = own_ref.shape[1], 2 * fields
    units = [(m, f) for m in range(members) for f in range(0, fields, part)]

    def first(m, f):
        near = [
            by_parity(is_odd, a_ref[k, m, f : f + part], b_ref[k, m, f : f + part])
            for k in range(2)
        ]
        q = [near[0][0], near[1][0], own_ref[0, m, f : f + part]]
        q += [own_ref[1, m, f : f + part], near[0][1], near[1][1]]
        q = [x.astype(F32) for x in q]
        return cols([rows(q[i], q[i + 1], q[i + 2], i) for i in range(4)], 0)

    ahead = 1
    mids = {u: first(*units[u]) for u in range(ahead)}
    copies = []
    for u, (m, f) in enumerate(units):
        if u + ahead < len(units):
            mids[u + ahead] = first(*units[u + ahead])
        q1 = mids.pop(u)
        q2 = cols([rows(q1[i], q1[i + 1], q1[i + 2], i + 1) for i in range(2)], 1)
        base = m * span + 2 * f
        for r in range(2):
            flat[pl.ds(base + r, part, stride=2), :] = q2[r] * fac[r, f : f + part]
        ready[base : base + 2 * part] = flat[base : base + 2 * part, :].astype(BF16)
        if f + part == fields:
            copy = pltpu.make_async_copy(
                ready.at[pl.ds(m * span, span)],
                o_ref.at[pl.ds((start + m) * span, span)],
                sems.at[m],
            )
            copy.start()
            copies.append(copy)
    for copy in copies:
        copy.wait()


def params():
    return pltpu.CompilerParams(vmem_limit_bytes=40 << 20)


def cost(flops):
    return pl.CostEstimate(flops=flops, bytes_accessed=10**6, transcendentals=0)


def call(kernel, outs, scratch=(), flops=10**8, specs=None):
    return pl.pallas_call(
        kernel,
        out_shape=outs,
        **({} if specs is None else {"in_specs": specs}),
        scratch_shapes=list(scratch),
        compiler_params=params(),
        cost_estimate=cost(flops),
    )


def swap(x, first):
    pairs = []
    for low in range(first, lax.axis_size("space") - 1, 2):
        pairs += [(low, low + 1), (low + 1, low)]
    return lax.ppermute(x, "space", pairs)


def shards(
    ensemble,
    obs_value,
    obs_error,
    obs_cell,
    obs_species,
    patch_index,
    patch_count,
    courant_x,
    courant_y,
    dep_velocity,
    surface_factor,
):
    local, fields, tile_rows, columns = ensemble.shape
    levels = fields // dep_velocity.shape[0]
    n_obs = obs_cell.shape[1]
    per = patch_index.shape[1]
    maxobs = patch_index.shape[2]
    groups_mem = 8

    sizes = (8,)
    flat = ensemble.reshape(local * fields * tile_rows, columns)
    hbm = pl.BlockSpec(memory_space=pltpu.HBM)
    equiv = pl.pallas_call(
        equivalents_kernel,
        out_shape=jax.ShapeDtypeStruct((groups_mem, local, n_obs), F32),
        in_specs=[hbm] * 3,
        scratch_shapes=[
            pltpu.VMEM((local, fields // levels, tile_rows, columns), BF16),
            pltpu.VMEM((2, 1, n_obs), jnp.int32),
            pltpu.SemaphoreType.DMA((2 + local,)),
        ],
        compiler_params=pltpu.CompilerParams(vmem_limit_bytes=67000000),
        cost_estimate=cost(10**8),
    )(
        ensemble.reshape(local, fields // levels, levels, tile_rows, columns), obs_cell, obs_species
    )
    everywhere = lax.all_to_all(equiv, "mem", 0, 0, tiled=True)
    payload, info = call(
        payload_kernel,
        [
            jax.ShapeDtypeStruct((groups_mem, 320, 128), BF16),
            jax.ShapeDtypeStruct((16, n_obs), F32),
        ],
        [pltpu.VMEM(flat.shape, F32), pltpu.VMEM((2048, 128), F32), pltpu.VMEM((512, 128), F32)],
        flops=10**8,
    )(flat, obs_cell, obs_value, obs_error, courant_x, courant_y)
    packed = jnp.concatenate([everywhere.reshape(groups_mem * local, n_obs), info], axis=0)
    payload, packed, patch_index, patch_count = lax.optimization_barrier(
        (payload, packed, patch_index, patch_count)
    )
    near_a, near_b = swap(packed, 0), swap(packed, 1)
    state = lax.all_to_all(payload, "mem", 0, 0, tiled=True)
    odd = (lax.axis_index("space") % 2).reshape(1, 1)

    used = jnp.arange(maxobs, dtype=jnp.int32)[None, :] < patch_count[0][:, None]
    idx = jnp.where(used, patch_index[0], -1).reshape(1, per * maxobs)
    cell_id = lax.axis_index("mem") * per + jnp.arange(per, dtype=jnp.int32)
    cell_id = jnp.broadcast_to(cell_id[:, None], (per, maxobs)).reshape(1, per * maxobs)
    pos = jnp.concatenate([cell_id // columns, cell_id % columns], axis=0).astype(F32)

    smem = pl.BlockSpec(memory_space=pltpu.SMEM)
    groups = per // 4
    hi, lo = call(
        weights_kernel,
        [jax.ShapeDtypeStruct((groups, 64, 256), BF16)] * 2,
        [
            pltpu.VMEM((2 * groups, 64, 128), F32),
            pltpu.VMEM((2 * groups, 64, 128), F32),
            pltpu.VMEM((2 * groups, 64, 128), F32),
            pltpu.VMEM((2 * groups, 16, 128), F32),
            pltpu.VMEM((2 * groups, 8, 128), F32),
        ],
        flops=10**10,
        specs=[smem] + [VMEM] * 5,
    )(odd, near_a, packed, near_b, idx, pos)
    back = call(
        transform_kernel,
        [jax.ShapeDtypeStruct((groups_mem, local, 40, 128), BF16)],
        [pltpu.VMEM((2, 64 * per, 128), F32)],
        flops=10**9,
    )(hi, lo, state)[0]
    returned = lax.all_to_all(back, "mem", 0, 0, tiled=True)
    parts = call(
        relayout_kernel,
        [jax.ShapeDtypeStruct((tile_rows, n, fields, columns), BF16) for n in sizes],
        flops=10**8,
    )(returned)
    halos = [(swap(x, 0), swap(x, 1)) for x in parts]

    done, start = None, 0
    for n, x, (side_a, side_b) in zip(sizes, parts, halos):
        operands = [odd, side_a, x, side_b, near_a, packed, near_b]
        operands += [dep_velocity.reshape(1, -1), surface_factor]
        in_specs = [smem] + [VMEM] * 8
        if done is not None:
            operands.append(done)
            in_specs.append(hbm)
        span = n * fields * tile_rows
        done = pl.pallas_call(
            functools.partial(advect_kernel, start),
            out_shape=jax.ShapeDtypeStruct(flat.shape, BF16),
            in_specs=in_specs,
            out_specs=hbm,
            scratch_shapes=[
                pltpu.VMEM((tile_rows, fields, columns), F32),
                pltpu.VMEM((span, columns), F32),
                pltpu.VMEM((span, columns), BF16),
                pltpu.SemaphoreType.DMA((n,)),
            ],
            input_output_aliases={} if start == 0 else {9: 0},
            compiler_params=params(),
            cost_estimate=cost(10**9),
        )(*operands)
        start += n
    return done.reshape(local, fields, tile_rows, columns)


def solution(mesh):
    in_specs = (
        P("mem", None, "space", None),
        P("space", None),
        P("space", None),
        P("space", None),
        P("space", None),
        P("space", "mem", None),
        P("space", "mem"),
        P(None, "space", None),
        P(None, "space", None),
        P(),
        P("space", None),
    )
    out_specs = P("mem", None, "space", None)
    return jax.shard_map(shards, mesh=mesh, in_specs=in_specs, out_specs=out_specs, check_vma=False)
```
